32 devices in a mesh: img: 8 (over z, y), seq: 4 (over x, core).
Axes of the slice: x: 2, y: 2, z: 4, core: 2. Of those that a mesh axis runs over, the one named last changes fastest.
Arguments:
- tokens: float32 [8, 4096, 384], P('img', 'seq'), may hold values from -6 to 6
- valid_mask: int32 [8, 4096], P('img', 'seq'), may hold values from 0 to 1, as said below
- timesteps: int32 [8], P('img'), may hold values from 0 to 999
- class_ids: int32 [8], P('img'), may hold values from 0 to 999
- time_first: float32 [256, 384], replicated, may hold values from -0.375 to 0.375
- time_second: float32 [384, 384], replicated, may hold values from -0.3125 to 0.3125
- class_table: float32 [1000, 384], replicated, may hold values from -6 to 6
- ada_weight: float32 [384, 2304], replicated, may hold values from -0.3125 to 0.3125
- ada_bias: float32 [2304], replicated, may hold values from -3 to 3
- conv_taps: float32 [9, 384], replicated, may hold values from -2 to 2
- query_proj: float32 [384, 384], replicated, may hold values from -0.3125 to 0.3125
- key_proj: float32 [384, 384], replicated, may hold values from -0.3125 to 0.3125
- value_proj: float32 [384, 384], replicated, may hold values from -0.3125 to 0.3125
- decay_down: float32 [384, 16], replicated, may hold values from -0.3125 to 0.3125
- decay_up: float32 [16, 384], replicated, may hold values from -1.5 to 1.5
- decay_bias: float32 [384], replicated, may hold values from 0.5 to 6
- gate_proj: float32 [384, 384], replicated, may hold values from -0.3125 to 0.3125
- out_proj: float32 [384, 384], replicated, may hold values from -0.625 to 0.625
- mlp_up: float32 [384, 1536], replicated, may hold values from -0.3125 to 0.3125
- mlp_down: float32 [1536, 384], replicated, may hold values from -0.3125 to 0.3125
- cotangent: float32 [8, 4096, 384], P('img', 'seq'), may hold values from -6 to 6
Outputs:
- block_out: float32 [8, 4096, 384], P('img', 'seq')
- tokens_grad: float32 [8, 4096, 384], P('img', 'seq')
- time_first_grad: float32 [256, 384], replicated
- time_second_grad: float32 [384, 384], replicated
- class_table_grad: float32 [1000, 384], replicated
- ada_weight_grad: float32 [384, 2304], replicated
- ada_bias_grad: float32 [2304], replicated
- conv_taps_grad: float32 [9, 384], replicated
- query_proj_grad: float32 [384, 384], replicated
- key_proj_grad: float32 [384, 384], replicated
- value_proj_grad: float32 [384, 384], replicated
- decay_down_grad: float32 [384, 16], replicated
- decay_up_grad: float32 [16, 384], replicated
- decay_bias_grad: float32 [384], replicated
- gate_proj_grad: float32 [384, 384], replicated
- out_proj_grad: float32 [384, 384], replicated
- mlp_up_grad: float32 [384, 1536], replicated
- mlp_down_grad: float32 [1536, 384], replicated
The draws below stay inside these ranges and needn't reach their ends.
Inputs may be any that keep to these rules, and one draw needn't show every extreme that they name: `valid_mask`: in each image the real patches are the first L of its 4096 patches, with 1024 <= L < 4096.
All inputs are finite; a program needn't handle non-finite values.
Results may differ from the reference program's by a relative error of at most 0.0003.
Values sent between devices are 32-bit elements; how exact they have to be, the bound alone decides.
No kernel may reach another device: no remote copies, remote signals or barrier semaphores. Data moves between devices by JAX's collectives and lax.ppermute only.
A program may use at most 320 MiB of HBM per device.

```python
import math
import jax
import jax.numpy as jnp
from jax import lax

D = 384
HEADS = 6
HEAD_DIM = 64
FF = 1536
CLASSES = 1000
RANK = 16
FREQ = 256
GRID = 64
STRETCH = 64
PATCHES = 4096
IMAGES = 8


def draw_valid_mask(key, part):
    lengths = jax.random.randint(key, (IMAGES,), PATCHES // 4, PATCHES)
    return (jnp.arange(PATCHES, dtype=jnp.int32)[None, :] < lengths[:, None]).astype(jnp.int32)


def touch_ends(drawn, key, low, top_value):
    shape = drawn.shape
    place = [jax.random.randint(jax.random.fold_in(key, axis), (), 0, shape[axis]) for axis in range(len(shape))]
    drawn = drawn.at[tuple(place)].set(low)
    longest = shape.index(max(shape))
    place[longest] = (place[longest] + 1) % shape[longest]
    return drawn.at[tuple(place)].set(top_value)


def level_of(stream_key, dims, cuts, least, top_value):
    def one(dim, parts):
        heights = jax.random.uniform(jax.random.fold_in(jax.random.fold_in(stream_key, 6), dim), (parts,), jnp.float32, least / len(cuts), top_value / len(cuts))
        return jnp.repeat(jnp.exp(heights), dims[dim] // parts).reshape((-1,) + (1,) * (len(dims) - dim - 1))

    factor_of = one(*cuts[0])
    for cut in cuts[1:]:
        factor_of = factor_of * one(*cut)
    return factor_of


def centred(own_key, dims, spread, limit, pieces=(), held_as=jnp.bfloat16):
    entries = jax.random.normal(own_key, dims, jnp.float32) * spread
    if len(pieces) > 0:
        entries = level_of(own_key, dims, pieces, -0.22, 0.18) * entries
    return jnp.clip(entries, min=-limit, max=limit).astype(held_as)


def setup_inputs(seed: int = 0) -> dict:
    streams_of = jax.random.split(jax.random.key(seed), 22)
    return {
        "tokens": centred(streams_of[0], (IMAGES, PATCHES, D), 1.0, 6.0, ((0, 8), (1, 4)), jnp.float32),
        "valid_mask": draw_valid_mask(jax.random.fold_in(streams_of[21], 71), 0),
        "timesteps": touch_ends(jax.random.randint(streams_of[2], (IMAGES,), 0, 1000), jax.random.fold_in(streams_of[2], 1), 0, 999).astype(jnp.int32),
        "class_ids": touch_ends(jax.random.randint(streams_of[3], (IMAGES,), 0, CLASSES), jax.random.fold_in(streams_of[3], 1), 0, CLASSES - 1).astype(jnp.int32),
        "time_first": centred(streams_of[4], (FREQ, D), FREQ ** -0.5, 0.375, (), jnp.float32),
        "time_second": centred(streams_of[5], (D, D), D ** -0.5, 0.3125, (), jnp.float32),
        "class_table": centred(streams_of[6], (CLASSES, D), 1.0, 6.0, (), jnp.float32),
        "ada_weight": centred(streams_of[7], (D, 6 * D), D ** -0.5, 0.3125, (), jnp.float32),
        "ada_bias": centred(streams_of[8], (6 * D,), 0.5, 3.0, (), jnp.float32),
        "conv_taps": centred(streams_of[9], (9, D), 9 ** -0.5, 2.0, (), jnp.float32),
        "query_proj": centred(streams_of[10], (D, D), D ** -0.5, 0.3125, (), jnp.float32),
        "key_proj": centred(streams_of[11], (D, D), D ** -0.5, 0.3125, (), jnp.float32),
        "value_proj": centred(streams_of[12], (D, D), D ** -0.5, 0.3125, (), jnp.float32),
        "decay_down": centred(streams_of[13], (D, RANK), D ** -0.5, 0.3125, (), jnp.float32),
        "decay_up": centred(streams_of[14], (RANK, D), RANK ** -0.5, 1.5, (), jnp.float32),
        "decay_bias": jnp.clip(jnp.exp(jax.random.uniform(streams_of[15], (D,), jnp.float32, math.log(0.5), math.log(6.0))), 0.5, 6.0),
        "gate_proj": centred(streams_of[16], (D, D), D ** -0.5, 0.3125, (), jnp.float32),
        "out_proj": centred(streams_of[17], (D, D), (D // 4) ** -0.5, 0.625, (), jnp.float32),
        "mlp_up": centred(streams_of[18], (D, FF), D ** -0.5, 0.3125, (), jnp.float32),
        "mlp_down": centred(streams_of[19], (FF, D), (FF // 4) ** -0.5, 0.3125, (), jnp.float32),
        "cotangent": centred(streams_of[20], (IMAGES, PATCHES, D), 1.0, 6.0, ((0, 8), (1, 4)), jnp.float32),
    }


HIGH = lax.Precision.HIGHEST

@jax.custom_vjp
def low(v):
    return lax.optimization_barrier(v.astype(jnp.bfloat16)).astype(jnp.float32)

@jax.custom_vjp
def low_back(v):
    return v

def low_keep(v):
    return (low(v), None)

def low_pass(kept, grad):
    return (grad,)

def back_keep(v):
    return (v, None)

def back_low(kept, grad):
    return (low(grad),)
low.defvjp(low_keep, low_pass)
low_back.defvjp(back_keep, back_low)

def product(left, right):
    return jnp.dot(left, right, precision=HIGH, preferred_element_type=jnp.float32)

def time_features(timesteps):
    half = FREQ // 2
    freqs = jnp.exp(-math.log(10000.0) * jnp.arange(half, dtype=jnp.float32) / half)
    angles = timesteps.astype(jnp.float32)[:, None] * freqs[None, :]
    return jnp.concatenate([jnp.cos(angles), jnp.sin(angles)], axis=1)

def condition(timesteps, class_ids, time_first, time_second, class_table, ada_weight, ada_bias):
    embed = product(jax.nn.silu(product(time_features(timesteps), time_first)), time_second)
    onehot = (class_ids[:, None] == jnp.arange(CLASSES, dtype=jnp.int32)[None, :]).astype(jnp.float32)
    embed = embed + product(onehot, class_table)
    return product(jax.nn.silu(embed), ada_weight) + ada_bias

def layer_norm(values):
    center = values - lax.optimization_barrier(jnp.mean(values, axis=-1, keepdims=True))
    return center * lax.rsqrt(lax.optimization_barrier(jnp.mean(center * center, axis=-1, keepdims=True)) + 1e-06)

def pair_mix(query, keys, values, cumul):
    diff = cumul[..., :, None, :, :] - cumul[..., None, :, :, :]
    size = cumul.shape[-3]
    causal = (jnp.arange(size)[:, None] >= jnp.arange(size)[None, :])[:, :, None, None]
    weight = jnp.where(causal, jnp.exp(jnp.where(causal, diff, 0.0)), 0.0)
    scores = lax.optimization_barrier(jnp.sum(query[..., :, None, :, :] * keys[..., None, :, :, :] * weight, axis=-1))
    return jnp.einsum('...tsh,...she->...the', scores, values, precision=HIGH)

def gla_image(query, keys, values, gates):

    def shaped(array):
        return array.reshape(PATCHES // STRETCH, STRETCH, HEADS, HEAD_DIM)

    def advance(state, items):
        query_part, keys_part, values_part, gates_part = items
        cumul = jnp.cumsum(gates_part, axis=0)
        inner = pair_mix(query_part, keys_part, values_part, cumul)
        outer = jnp.einsum('thd,hde->the', query_part * jnp.exp(cumul), state, precision=HIGH)
        final = cumul[-1]
        carried = jnp.einsum('shd,she->hde', keys_part * jnp.exp(final[None] - cumul), values_part, precision=HIGH)
        return (jnp.exp(final)[:, :, None] * state + carried, inner + outer)
    start = jnp.zeros((HEADS, HEAD_DIM, HEAD_DIM), jnp.float32)
    _, mixed = lax.scan(jax.checkpoint(advance), start, (shaped(query), shaped(keys), shaped(values), shaped(gates)))
    return mixed.reshape(PATCHES, HEADS, HEAD_DIM)

def forward(tokens, valid_mask, timesteps, class_ids, time_first, time_second, class_table, ada_weight, ada_bias, conv_taps, query_proj, key_proj, value_proj, decay_down, decay_up, decay_bias, gate_proj, out_proj, mlp_up, mlp_down):
    count = tokens.shape[0]
    modul = condition(timesteps, class_ids, time_first, time_second, class_table, ada_weight, ada_bias)
    shift_a, scale_a, gate_a, shift_b, scale_b, gate_b = jnp.split(modul, 6, axis=1)
    normed = layer_norm(tokens) * (1.0 + scale_a[:, None]) + shift_a[:, None]
    padded = jnp.pad(normed.reshape(count, GRID, GRID, D), ((0, 0), (1, 1), (1, 1), (0, 0)))
    mixed = jnp.zeros((count, GRID, GRID, D), jnp.float32)
    for row in range(3):
        for col in range(3):
            mixed = mixed + conv_taps[row * 3 + col] * padded[:, row:row + GRID, col:col + GRID]
    hidden = jax.nn.silu(mixed.reshape(count, PATCHES, D))
    keep = valid_mask.astype(jnp.float32)[..., None]
    query = product(hidden, query_proj) * HEAD_DIM ** (-0.5)
    keys = product(hidden, key_proj) * keep
    values = product(hidden, value_proj) * keep
    gates = jax.nn.log_sigmoid(product(product(hidden, decay_down), decay_up) + decay_bias) / 16.0 * keep

    def heads(array):
        return array.reshape(count, PATCHES, HEADS, HEAD_DIM)
    attended = jax.vmap(gla_image)(heads(query), heads(keys), heads(values), heads(gates))
    attended = attended * lax.rsqrt(lax.optimization_barrier(jnp.mean(attended * attended, axis=-1, keepdims=True)) + 1e-05)
    branch = product(attended.reshape(count, PATCHES, D) * jax.nn.silu(product(normed, gate_proj)), out_proj)
    middle = tokens + gate_a[:, None] * branch
    second = layer_norm(middle) * (1.0 + scale_b[:, None]) + shift_b[:, None]
    return middle + gate_b[:, None] * product(jax.nn.gelu(product(second, mlp_up)), mlp_down)

def reference(tokens, valid_mask, timesteps, class_ids, time_first, time_second, class_table, ada_weight, ada_bias, conv_taps, query_proj, key_proj, value_proj, decay_down, decay_up, decay_bias, gate_proj, out_proj, mlp_up, mlp_down, cotangent):
    group = math.gcd(IMAGES, max(1, 4096 // PATCHES))
    blocks = IMAGES // group
    weights = (time_first, time_second, class_table, ada_weight, ada_bias, conv_taps, query_proj, key_proj, value_proj, decay_down, decay_up, decay_bias, gate_proj, out_proj, mlp_up, mlp_down)

    def grouped(array):
        return array.reshape((blocks, group) + array.shape[1:])

    def one_group(totals, items):
        tok_part, mask_part, time_part, class_part, cot_part = items

        def run(tok_in, *params):
            return forward(tok_in, mask_part, time_part, class_part, *params)
        result, pull = jax.vjp(run, tok_part, *weights)
        grads = pull(cot_part)
        return (tuple((total + grad for total, grad in zip(totals, grads[1:]))), (result, grads[0]))
    start = tuple((jnp.zeros_like(weight) for weight in weights))
    totals, (results, tok_grads) = lax.scan(one_group, start, (grouped(tokens), grouped(valid_mask), grouped(timesteps), grouped(class_ids), grouped(cotangent)))
    return (results.reshape(IMAGES, PATCHES, D), tok_grads.reshape(IMAGES, PATCHES, D), totals[0], totals[1], totals[2], totals[3], totals[4], totals[5], totals[6], totals[7], totals[8], totals[9], totals[10], totals[11], totals[12], totals[13], totals[14], totals[15])
```

```python
import functools
import math

import jax
import jax.numpy as jnp
from jax import lax
from jax.experimental import pallas as pl
from jax.experimental.pallas import tpu as pltpu
from jax.sharding import PartitionSpec as P

HEADS = 6
HEAD_DIM = 64
CLASSES = 1000
FREQ = 256
GRID = 64
WIDTH = 384
PAIRS = 3
LANES = 128
CHUNK = 128
TILE = 256
HALF = 256
SPAN = 120.0
HIGH = lax.Precision.HIGHEST
F32 = jnp.float32
BF16 = jnp.bfloat16
GELU_C = math.sqrt(2.0 / math.pi)


def product(left, right):
    return jnp.dot(left, right, precision=HIGH, preferred_element_type=F32)


def dot(a, b, ca=1, cb=0):
    return lax.dot_general(a, b, (((ca,), (cb,)), ((), ())), preferred_element_type=F32)


def split(x):
    high = x.astype(BF16)
    return high, (x - high.astype(F32)).astype(BF16)


def mm3(a, b, ca=1, cb=0):
    return dot(a[0], b[0], ca, cb) + dot(a[1], b[0], ca, cb) + dot(a[0], b[1], ca, cb)


def split3(x):
    high = x.astype(BF16)
    rest = x - high.astype(F32)
    middle = rest.astype(BF16)
    return high, middle, (rest - middle.astype(F32)).astype(BF16)


def mm6(a, b, ca=1, cb=0):
    terms = ((0, 0), (0, 1), (1, 0), (1, 1), (0, 2), (2, 0))
    return sum(dot(a[i], b[j], ca, cb) for i, j in reversed(terms))


def wide6(x):
    h, m, l = split3(x)
    return jnp.concatenate([h, h, m, m, h, l], axis=1)


def tall6(w):
    h, m, l = split3(w)
    return jnp.concatenate([h, m, h, m, l, h], axis=0)


def wide(x):
    high, low = split(x)
    return jnp.concatenate([high, low, high], axis=1)


def tall(w):
    high, low = split(w)
    return jnp.concatenate([high, high, low], axis=0)


def across(w):
    high, low = split(w)
    return jnp.concatenate([high, high, low], axis=1)


def lanes(x, p):
    return x[..., p * LANES : (p + 1) * LANES]


def first_half(shape):
    return lax.broadcasted_iota(jnp.int32, shape, len(shape) - 1) < HEAD_DIM


def block_diagonal(square):
    rows = lax.broadcasted_iota(jnp.int32, square.shape, 0) < HEAD_DIM
    return jnp.where(rows == first_half(square.shape), square, 0.0)


def head_mean(x):
    rows = lax.broadcasted_iota(jnp.int32, (LANES, LANES), 0) < HEAD_DIM
    ones = jnp.where(rows == first_half((LANES, LANES)), 1.0 / HEAD_DIM, 0.0).astype(BF16)
    high, low = split(x)
    return dot(
        jnp.concatenate([high, low], axis=1), jnp.concatenate([ones, ones], axis=0)
    )


def head_means(x):
    return jnp.concatenate([head_mean(lanes(x, p)) for p in range(PAIRS)], axis=1)


def stacked_heads(x):
    keep = first_half(x.shape)
    zero = jnp.zeros_like(x)
    return jnp.concatenate([jnp.where(keep, x, zero), jnp.where(keep, zero, x)], axis=0)


def merged_heads(x):
    rows = x.shape[0] // 2
    return jnp.where(first_half((rows, LANES)), x[:rows], x[rows:])


def sigmoid(x):
    return 1.0 / (1.0 + jnp.exp(-x))


def shifted(x, step):
    rows = x.shape[0]
    column = lax.broadcasted_iota(jnp.int32, x.shape, 0) % GRID
    if step == 1:
        return jnp.where(column == 0, 0.0, pltpu.roll(x, 1, 0))
    return jnp.where(column == GRID - 1, 0.0, pltpu.roll(x, rows - 1, 0))


def normalized(x):
    center = x - jnp.mean(x, axis=-1, keepdims=True)
    rate = lax.rsqrt(jnp.mean(center * center, axis=-1, keepdims=True) + 1e-06)
    return center * rate, rate


def normal_back(dhat, hat, rate):
    return rate * (
        dhat
        - jnp.mean(dhat, axis=-1, keepdims=True)
        - hat * jnp.mean(dhat * hat, axis=-1, keepdims=True)
    )


def triangle(size, upper):
    rows = lax.broadcasted_iota(jnp.int32, (size, size), 0)
    cols = lax.broadcasted_iota(jnp.int32, (size, size), 1)
    return jnp.where(cols >= rows if upper else cols <= rows, 1.0, 0.0).astype(BF16)


def running_sum(x, upper):
    tri = triangle(x.shape[0], upper)
    high = x.astype(BF16)
    rest = x - high.astype(F32)
    middle = rest.astype(BF16)
    low = (rest - middle.astype(F32)).astype(BF16)
    return dot(tri, high) + dot(tri, middle) + dot(tri, low)


def front_kernel(
    edge_ref,
    real_ref,
    tok_ref,
    top_ref,
    bot_ref,
    mod_ref,
    taps_ref,
    w_ref,
    bias_ref,
    normed_ref,
    conv_ref,
    q_ref,
    k_ref,
    v_ref,
    cum_ref,
    slope_ref,
    far_ref,
    state_ref,
    fade_ref,
    out_ref,
    w3_ref,
    st_ref,
    dev_ref,
):
    image = pl.program_id(0)
    length = tok_ref.shape[0]

    @pl.when(image == 0)
    def _():
        w3_ref[...] = tall6(w_ref[...])

    shift = mod_ref[0:1, :]
    scale = 1.0 + mod_ref[1:2, :]

    def modulated(x):
        return normalized(x)[0] * scale + shift

    normed_ref[0:GRID, :] = jnp.where(edge_ref[0] > 0, 0.0, modulated(top_ref[...]))
    normed_ref[pl.ds(length + GRID, GRID), :] = jnp.where(
        edge_ref[1] > 0, 0.0, modulated(bot_ref[...])
    )

    def norm_step(i, carry):
        start = pl.multiple_of(i * TILE, TILE)
        normed_ref[pl.ds(start + GRID, TILE), :] = modulated(tok_ref[pl.ds(start, TILE), :])
        return carry

    lax.fori_loop(0, length // TILE, norm_step, 0)
    st_ref[...] = jnp.zeros_like(st_ref)
    dev_ref[...] = jnp.zeros_like(dev_ref)

    def tile_step(i, carry):
        start = pl.multiple_of(i * TILE, TILE)
        rows = [normed_ref[pl.ds(start + a * GRID, TILE), :] for a in range(3)]
        parts = [
            sum(taps_ref[3 * a + b : 3 * a + b + 1, :] * rows[a] for a in range(3))
            for b in range(3)
        ]
        conv = shifted(parts[0], 1) + parts[1] + shifted(parts[2], -1)
        conv_ref[pl.ds(start, TILE), :] = conv
        hidden = conv * sigmoid(conv)
        proj = dot(wide6(hidden), w3_ref[...])
        keep = (
            lax.broadcasted_iota(jnp.int32, (TILE, WIDTH), 0) + start < real_ref[image]
        )
        q = proj[:, :WIDTH]
        k = jnp.where(keep, proj[:, WIDTH : 2 * WIDTH], 0.0)
        v = jnp.where(keep, proj[:, 2 * WIDTH : 3 * WIDTH], 0.0)
        x = proj[:, 3 * WIDTH :] + bias_ref[...]
        small = jnp.exp(-jnp.abs(x))
        gates = jnp.where(keep, (jnp.minimum(x, 0.0) - jnp.log1p(small)) * (1.0 / 16.0), 0.0)
        slope = jnp.where(x >= 0, small, 1.0) / (1.0 + small)
        slope_ref[pl.ds(start, TILE), :] = jnp.where(keep, slope * (1.0 / 16.0), 0.0)
        q_ref[pl.ds(start, TILE), :] = q
        k_ref[pl.ds(start, TILE), :] = k
        v_ref[pl.ds(start, TILE), :] = v
        for c in range(TILE // CHUNK):
            at = slice(c * CHUNK, (c + 1) * CHUNK)
            chunk = i * (TILE // CHUNK) + c
            cum = running_sum(gates[at], False)
            cum_ref[pl.ds(start + c * CHUNK, CHUNK), :] = cum
            final = cum[CHUNK - 1 : CHUNK, :]
            dev = dev_ref[0:1, :]
            far_ref[pl.ds(start + c * CHUNK, CHUNK), :] = q[at] * jnp.exp(cum + dev)
            fade_ref[chunk] = jnp.broadcast_to(jnp.exp(dev), (8, WIDTH))
            kd = k[at] * jnp.exp(final - cum)
            factor = jnp.exp(final)
            for p in range(PAIRS):
                state_ref[chunk, p] = st_ref[p]
                update = mm3(split(lanes(v[at], p)), split(lanes(kd, p)), 0, 0)
                st_ref[p] = lanes(factor, p) * st_ref[p] + block_diagonal(update)
            dev_ref[...] = dev_ref[...] + final
        return carry

    lax.fori_loop(0, length // TILE, tile_step, 0)
    for p in range(PAIRS):
        out_ref[p, 0:HEAD_DIM, :] = st_ref[p, 0:HEAD_DIM, :] + st_ref[p, HEAD_DIM:, :]
        out_ref[p, HEAD_DIM:, :] = jnp.exp(lanes(dev_ref[...], p))


def exact_scores(q_ref, k_ref, cum_ref, base, s_ref):
    q = q_ref[pl.ds(base, CHUNK), :]
    cum = cum_ref[pl.ds(base, CHUNK), :]
    s_ref[...] = jnp.zeros_like(s_ref)

    def step(j, carry):
        key = k_ref[pl.ds(base + j, 1), :]
        weight = jnp.exp(jnp.minimum(cum - cum_ref[pl.ds(base + j, 1), :], 0.0))
        terms = q * key * weight
        for p in range(PAIRS):
            column = jnp.sum(stacked_heads(lanes(terms, p)), axis=1, keepdims=True)
            at = lax.broadcasted_iota(jnp.int32, (2 * CHUNK, CHUNK), 1) == j
            s_ref[p] = jnp.where(at, column, s_ref[p])
        return carry

    lax.fori_loop(0, CHUNK, step, 0)


def causal_two():
    rows = lax.broadcasted_iota(jnp.int32, (2 * CHUNK, CHUNK), 0) % CHUNK
    return rows >= lax.broadcasted_iota(jnp.int32, (2 * CHUNK, CHUNK), 1)


def inner_kernel(
    q_ref, k_ref, v_ref, cum_ref, state_ref, normed_ref, gate_ref, o_ref, s_ref, gp_ref, w3_ref, tmp_ref
):
    @pl.when((pl.program_id(0) == 0) & (pl.program_id(1) == 0))
    def _():
        w3_ref[...] = tall(gate_ref[...])

    start = pl.multiple_of(pl.program_id(1) * TILE + GRID, GRID)
    gp_ref[...] = dot(wide(normed_ref[pl.ds(start, TILE), :]), w3_ref[...])
    mask = causal_two()
    for c in range(TILE // CHUNK):
        base = c * CHUNK
        at = slice(base, base + CHUNK)
        q = q_ref[at, :]
        k = k_ref[at, :]
        cum = cum_ref[at, :]
        final = cum[CHUNK - 1 : CHUNK, :]
        wild = jnp.max(-final) > SPAN
        middle = 0.5 * final
        qf = split3(q * jnp.exp(cum - middle))
        kf = split3(k * jnp.exp(middle - cum))
        for p in range(PAIRS):
            qp = tuple(stacked_heads(lanes(part, p)) for part in qf)
            kp = tuple(lanes(part, p) for part in kf)
            tmp_ref[p] = mm6(qp, kp, 1, 1)

        @pl.when(wild)
        def _():
            exact_scores(q_ref, k_ref, cum_ref, base, tmp_ref)

        qd = q * jnp.exp(cum)
        for p in range(PAIRS):
            s = jnp.where(mask, tmp_ref[p], 0.0)
            s_ref[c, p] = s
            inner = merged_heads(mm3(split(s), split(lanes(v_ref[at, :], p))))
            outer = mm3(split(lanes(qd, p)), split(state_ref[c, p]), 1, 1)
            o_ref[at, p * LANES : (p + 1) * LANES] = inner + outer


def tail_kernel(
    o_ref,
    far_ref,
    tok_ref,
    normed_ref,
    gp_ref,
    cot_ref,
    st_ref,
    mod_ref,
    out_w_ref,
    gate_w_ref,
    up_ref,
    down_ref,
    block_ref,
    dmid_ref,
    datt_ref,
    dnorm_ref,
    g_out_ref,
    g_gate_ref,
    g_up_ref,
    g_down_ref,
    dmod_ref,
    dst_ref,
    o3_ref,
    ot3_ref,
    gt3_ref,
    u3_ref,
    ut_ref,
    d_ref,
    dt3_ref,
    gd_ref,
    mlp_ref,
    dsec_ref,
):
    image, tile = pl.program_id(0), pl.program_id(1)
    blocks = u3_ref.shape[0]

    @pl.when((image == 0) & (tile == 0))
    def _():
        o3_ref[...] = tall(out_w_ref[...])
        ot3_ref[...] = across(out_w_ref[...])
        gt3_ref[...] = across(gate_w_ref[...])
        g_out_ref[...] = jnp.zeros_like(g_out_ref)
        g_gate_ref[...] = jnp.zeros_like(g_gate_ref)
        g_up_ref[...] = jnp.zeros_like(g_up_ref)
        gd_ref[...] = jnp.zeros_like(gd_ref)
        for j in range(blocks):
            up = up_ref[:, j * HALF : (j + 1) * HALF]
            u3_ref[j] = tall(up)
            ut_ref[j] = jnp.concatenate(split(up), axis=0)
            down = down_ref[j * HALF : (j + 1) * HALF, :]
            d_ref[j] = jnp.concatenate(split(down), axis=0)
            dt3_ref[j] = across(down)

    @pl.when(tile == 0)
    def _():
        dmod_ref[...] = jnp.zeros_like(dmod_ref)
        dst_ref[...] = jnp.zeros_like(dst_ref)

    gate_a = mod_ref[2:3, :]
    shift_b = mod_ref[3:4, :]
    scale_b = 1.0 + mod_ref[4:5, :]
    gate_b = mod_ref[5:6, :]
    far = split(far_ref[...])
    att = o_ref[...] + jnp.concatenate(
        [
            mm3(tuple(lanes(part, p) for part in far), split(st_ref[p]), 1, 1)
            for p in range(PAIRS)
        ],
        axis=1,
    )
    rate = lax.rsqrt(head_means(att * att) + 1e-05)
    unit = att * rate
    gp = gp_ref[...]
    sig = sigmoid(gp)
    gate = gp * sig
    y = unit * gate
    y_pair = split(y)
    branch = dot(jnp.concatenate([y_pair[0], y_pair[1], y_pair[0]], axis=1), o3_ref[...])
    middle = tok_ref[...] + gate_a * branch
    hat, rate_b = normalized(middle)
    second = hat * scale_b + shift_b
    second3 = wide(second)
    cot = cot_ref[...]
    dmlp = cot * gate_b
    dmlp3 = wide(dmlp)
    second_t = split(second.T)
    dmlp_t = split(dmlp.T)
    mlp_ref[...] = jnp.zeros_like(mlp_ref)
    dsec_ref[...] = jnp.zeros_like(dsec_ref)

    def step(j, carry):
        u = dot(second3, u3_ref[j])
        square = u * u
        th = jnp.tanh(GELU_C * (u + 0.044715 * u * square))
        act = 0.5 * u * (1.0 + th)
        slope = 0.5 * (1.0 + th) + 0.5 * u * (1.0 - th * th) * (
            GELU_C * (1.0 + 3.0 * 0.044715 * square)
        )
        act_pair = split(act)
        down = (d_ref[j, 0:HALF, :], d_ref[j, HALF:, :])
        mlp_ref[...] += mm3(act_pair, down)
        du = split(dot(dmlp3, dt3_ref[j], 1, 1) * slope)
        up = (ut_ref[j, 0:WIDTH, :], ut_ref[j, WIDTH:, :])
        dsec_ref[...] += mm3(du, up, 1, 1)
        at = pl.ds(pl.multiple_of(j * HALF, HALF), HALF)
        g_up_ref[:, at] += mm3(second_t, du)
        gd_ref[j] += mm3(dmlp_t, act_pair)
        return carry

    lax.fori_loop(0, blocks, step, 0)

    mlp = mlp_ref[...]
    block_ref[...] = middle + gate_b * mlp
    dsec = dsec_ref[...]
    dmid = cot + normal_back(dsec * scale_b, hat, rate_b)
    dmid_ref[...] = dmid

    def total(x):
        return jnp.sum(x, axis=0, keepdims=True)

    dmod_ref[2:3, :] += total(dmid * branch)
    dmod_ref[3:4, :] += total(dsec)
    dmod_ref[4:5, :] += total(dsec * hat)
    dmod_ref[5:6, :] += total(cot * mlp)
    dbranch = dmid * gate_a
    dbr = split(dbranch)
    dy = dot(jnp.concatenate([dbr[0], dbr[1], dbr[0]], axis=1), ot3_ref[...], 1, 1)
    g_out_ref[...] += mm3(y_pair, dbr, 0, 0)
    dunit = dy * gate
    dgp = (dy * unit) * (sig * (1.0 + gp * (1.0 - sig)))
    datt = rate * (dunit - unit * head_means(dunit * unit))
    datt_ref[...] = datt
    dg = split(dgp)
    dnorm_ref[...] = dot(jnp.concatenate([dg[0], dg[1], dg[0]], axis=1), gt3_ref[...], 1, 1)
    start = pl.multiple_of(tile * TILE + GRID, GRID)
    g_gate_ref[...] += mm3(split(normed_ref[pl.ds(start, TILE), :]), dg, 0, 0)
    da = split(datt)
    for p in range(PAIRS):
        grad = mm3(
            tuple(lanes(part, p) for part in da), tuple(lanes(part, p) for part in far), 0, 0
        )
        dst_ref[p] += block_diagonal(grad)

    @pl.when((image == pl.num_programs(0) - 1) & (tile == pl.num_programs(1) - 1))
    def _():
        for j in range(blocks):
            g_down_ref[j * HALF : (j + 1) * HALF, :] = gd_ref[j].T


def exact_back(q_ref, k_ref, cum_ref, ds_ref, base, dq_ref, dk_ref):
    q = q_ref[pl.ds(base, CHUNK), :]
    cum = cum_ref[pl.ds(base, CHUNK), :]
    dq_ref[...] = jnp.zeros_like(dq_ref)

    def step(j, carry):
        key = k_ref[pl.ds(base + j, 1), :]
        weight = jnp.exp(jnp.minimum(cum - cum_ref[pl.ds(base + j, 1), :], 0.0))
        at = lax.broadcasted_iota(jnp.int32, (2 * CHUNK, CHUNK), 1) == j
        columns = []
        for p in range(PAIRS):
            column = jnp.sum(jnp.where(at, ds_ref[p], 0.0), axis=1, keepdims=True)
            columns.append(merged_heads(jnp.broadcast_to(column, (2 * CHUNK, LANES))))
        ds = jnp.concatenate(columns, axis=1) * weight
        dq_ref[...] += ds * key
        dk_ref[pl.ds(j, 1), :] = jnp.sum(ds * q, axis=0, keepdims=True)
        return carry

    lax.fori_loop(0, CHUNK, step, 0)


def inner_back_kernel(
    q_ref,
    k_ref,
    v_ref,
    cum_ref,
    datt_ref,
    s_ref,
    state_ref,
    fade_ref,
    st_ref,
    dq_ref,
    dk_ref,
    dv_ref,
    full_ref,
    ds_ref,
    dqi_ref,
    dki_ref,
):
    mask = causal_two()
    for c in range(TILE // CHUNK):
        base = c * CHUNK
        at = slice(base, base + CHUNK)
        q = q_ref[at, :]
        k = k_ref[at, :]
        cum = cum_ref[at, :]
        final = cum[CHUNK - 1 : CHUNK, :]
        wild = jnp.max(-final) > SPAN
        middle = 0.5 * final
        eq = jnp.exp(cum - middle)
        ek = jnp.exp(middle - cum)
        qf = split(q * eq)
        kf = split(k * ek)
        da = split3(datt_ref[at, :])
        vs = split3(v_ref[at, :])
        for p in range(PAIRS):
            da2 = tuple(stacked_heads(lanes(part, p)) for part in da)
            vp = tuple(lanes(part, p) for part in vs)
            ds = jnp.where(mask, mm6(da2, vp, 1, 1), 0.0)
            ds_ref[p] = ds
            ds2 = split(ds)
            kp = tuple(lanes(part, p) for part in kf)
            qp = tuple(lanes(part, p) for part in qf)
            dqi_ref[:, p * LANES : (p + 1) * LANES] = merged_heads(mm3(ds2, kp)) * lanes(eq, p)
            q2 = tuple(stacked_heads(part) for part in qp)
            dki_ref[:, p * LANES : (p + 1) * LANES] = mm3(ds2, q2, 0, 0) * lanes(ek, p)
            s2 = split(s_ref[c, p])
            dv_ref[at, p * LANES : (p + 1) * LANES] = mm3(s2, da2, 0, 0)

        @pl.when(wild)
        def _():
            exact_back(q_ref, k_ref, cum_ref, ds_ref, base, dqi_ref, dki_ref)

        grow = jnp.exp(cum)
        for p in range(PAIRS):
            full = state_ref[c, p] + lanes(fade_ref[c, 0:1, :], p) * st_ref[p]
            full_ref[c, p] = full
            outer = mm3(tuple(lanes(part, p) for part in da), split(full))
            dq_ref[at, p * LANES : (p + 1) * LANES] = (
                dqi_ref[:, p * LANES : (p + 1) * LANES] + outer * lanes(grow, p)
            )
        dk_ref[at, :] = dki_ref[...]


def state_back_kernel(
    real_ref,
    q_ref,
    k_ref,
    v_ref,
    cum_ref,
    slope_ref,
    conv_ref,
    datt_ref,
    dq_ref,
    dk_ref,
    dv_ref,
    full_ref,
    dout_ref,
    w_ref,
    proj_ref,
    dconv_ref,
    dbias_ref,
    wt3_ref,
    dst_ref,
):
    image, turn = pl.program_id(0), pl.program_id(1)
    tile = pl.num_programs(1) - 1 - turn

    @pl.when((image == 0) & (turn == 0))
    def _():
        wt3_ref[...] = across(w_ref[...])
        dbias_ref[...] = jnp.zeros_like(dbias_ref)

    @pl.when(turn == 0)
    def _():
        dst_ref[...] = dout_ref[...]

    keep = (
        lax.broadcasted_iota(jnp.int32, (CHUNK, WIDTH), 0) + tile * TILE
    )
    for c in reversed(range(TILE // CHUNK)):
        at = slice(c * CHUNK, (c + 1) * CHUNK)
        q = q_ref[at, :]
        k = k_ref[at, :]
        cum = cum_ref[at, :]
        final = cum[CHUNK - 1 : CHUNK, :]
        late = jnp.exp(final - cum)
        kd = k * late
        v = v_ref[at, :]
        qd = split(q * jnp.exp(cum))
        da = split(datt_ref[at, :])
        factor = jnp.exp(final)
        dk_parts, dv_parts, cross = [], [], []
        for p in range(PAIRS):
            old = dst_ref[p]
            pair = split(old)
            dk_parts.append(mm3(split(lanes(v, p)), pair))
            dv_parts.append(mm3(split(lanes(kd, p)), pair, 1, 1))
            leaving = lanes(factor, p) * full_ref[c, p] + block_diagonal(
                mm3(split(lanes(v, p)), split(lanes(kd, p)), 0, 0)
            )
            cross.append(jnp.sum(leaving * old, axis=0, keepdims=True))
            update = mm3(
                tuple(lanes(part, p) for part in da), tuple(lanes(part, p) for part in qd), 0, 0
            )
            dst_ref[p] = lanes(factor, p) * old + block_diagonal(update)
        dq = dq_ref[at, :]
        dk = dk_ref[at, :] + jnp.concatenate(dk_parts, axis=1) * late
        dv = dv_ref[at, :] + jnp.concatenate(dv_parts, axis=1)
        dgates = running_sum(q * dq - k * dk, True) + jnp.concatenate(cross, axis=1)
        dx = dgates * slope_ref[at, :]
        real = keep + c * CHUNK < real_ref[image]
        dk = jnp.where(real, dk, 0.0)
        dv = jnp.where(real, dv, 0.0)
        dbias_ref[...] += jnp.sum(dx.reshape(CHUNK // 8, 8, WIDTH), axis=0)
        proj_ref[at, 0:WIDTH] = dq
        proj_ref[at, WIDTH : 2 * WIDTH] = dk
        proj_ref[at, 2 * WIDTH : 3 * WIDTH] = dv
        proj_ref[at, 3 * WIDTH :] = dx
    dhidden = dot(wide(proj_ref[...]), wt3_ref[...], 1, 1)
    conv = conv_ref[...]
    sig = sigmoid(conv)
    dconv_ref[...] = dhidden * (sig * (1.0 + conv * (1.0 - sig)))


def weight_kernel(conv_ref, proj_ref, g_ref):
    @pl.when((pl.program_id(0) == 0) & (pl.program_id(1) == 0))
    def _():
        g_ref[...] = jnp.zeros_like(g_ref)

    conv = conv_ref[...]
    hidden = split((conv * sigmoid(conv)).T)
    for j in range(4):
        at = slice(j * WIDTH, (j + 1) * WIDTH)
        g_ref[:, at] += mm3(hidden, split(proj_ref[:, at]))


def front_back_kernel(
    tok_ref,
    normed_ref,
    dconv_ref,
    top_ref,
    bot_ref,
    dnorm_ref,
    dmid_ref,
    mod_ref,
    taps_ref,
    grad_ref,
    dmod_ref,
    dtaps_ref,
    pad_ref,
):
    length = tok_ref.shape[0]

    @pl.when(pl.program_id(0) == 0)
    def _():
        dtaps_ref[...] = jnp.zeros_like(dtaps_ref)

    dmod_ref[...] = jnp.zeros_like(dmod_ref)
    pad_ref[0:GRID, :] = top_ref[...]
    pad_ref[pl.ds(length + GRID, GRID), :] = bot_ref[...]
    pad_ref[pl.ds(GRID, length), :] = dconv_ref[...]
    scale = 1.0 + mod_ref[1:2, :]

    def eights(x):
        return jnp.sum(x.reshape(x.shape[0] // 8, 8, WIDTH), axis=0)

    def step(i, carry):
        start = pl.multiple_of(i * TILE, TILE)
        rows = [pad_ref[pl.ds(start + (2 - a) * GRID, TILE), :] for a in range(3)]
        parts = [
            sum(taps_ref[3 * a + b : 3 * a + b + 1, :] * rows[a] for a in range(3))
            for b in range(3)
        ]
        dn = (
            shifted(parts[0], -1)
            + parts[1]
            + shifted(parts[2], 1)
            + dnorm_ref[pl.ds(start, TILE), :]
        )
        hat, rate = normalized(tok_ref[pl.ds(start, TILE), :])
        grad_ref[pl.ds(start, TILE), :] = dmid_ref[pl.ds(start, TILE), :] + normal_back(
            dn * scale, hat, rate
        )
        dmod_ref[0:1, :] += jnp.sum(dn, axis=0, keepdims=True)
        dmod_ref[1:2, :] += jnp.sum(dn * hat, axis=0, keepdims=True)
        own = rows[1]
        moved = [shifted(own, -1), own, shifted(own, 1)]
        for a in range(3):
            near = normed_ref[pl.ds(start + a * GRID, TILE), :]
            for b in range(3):
                dtaps_ref[3 * a + b] += eights(moved[b] * near)
        return carry

    lax.fori_loop(0, length // TILE, step, 0)


def call(kernel, grid, ins, outs, scratch, flops=0, moved=0, prefetch=0, limit=60):
    return pl.pallas_call(
        kernel,
        grid_spec=pltpu.PrefetchScalarGridSpec(
            num_scalar_prefetch=prefetch,
            grid=grid,
            in_specs=ins,
            out_specs=[spec for spec, _ in outs],
            scratch_shapes=scratch,
        ),
        out_shape=[jax.ShapeDtypeStruct(shape, F32) for _, shape in outs],
        compiler_params=pltpu.CompilerParams(vmem_limit_bytes=limit * 1024 * 1024),
        cost_estimate=pl.CostEstimate(flops=flops, bytes_accessed=moved, transcendentals=0),
    )


def whole(shape):
    zeros = (0,) * len(shape)
    return pl.BlockSpec(shape, lambda *_: zeros, pipeline_mode=pl.Buffered(1))


def per_image(shape):
    zeros = (0,) * len(shape)
    return pl.BlockSpec((None,) + shape, lambda n, *_: (n,) + zeros)


def time_features(timesteps):
    half = FREQ // 2
    freqs = jnp.exp(-math.log(10000.0) * jnp.arange(half, dtype=F32) / half)
    angles = timesteps.astype(F32)[:, None] * freqs[None, :]
    return jnp.concatenate([jnp.cos(angles), jnp.sin(angles)], axis=1)


def expanded(compact):
    keep = jnp.arange(LANES) < HEAD_DIM
    zero = jnp.zeros_like(compact)
    return jnp.concatenate(
        [jnp.where(keep, compact, zero), jnp.where(keep, zero, compact)], axis=-2
    )


def chained(message, axis, backward):
    size = lax.axis_size(axis)
    total = jnp.zeros_like(message[..., :HEAD_DIM, :])
    got = []
    for far in range(1, size):
        pairs = [(i, i + far) for i in range(size - far)]
        if backward:
            pairs = [(j, i) for i, j in pairs]
        got.append(lax.ppermute(message, axis, pairs))
    for part in reversed(got):
        total = part[..., :HEAD_DIM, :] + part[..., HEAD_DIM : HEAD_DIM + 1, :] * total
    return expanded(total)


def body(
    tokens,
    valid_mask,
    timesteps,
    class_ids,
    time_first,
    time_second,
    class_table,
    ada_weight,
    ada_bias,
    conv_taps,
    query_proj,
    key_proj,
    value_proj,
    decay_down,
    decay_up,
    decay_bias,
    gate_proj,
    out_proj,
    mlp_up,
    mlp_down,
    cotangent,
):
    count, length, width = tokens.shape
    size, mine = lax.axis_size("seq"), lax.axis_index("seq")
    hidden_units = mlp_up.shape[1]
    tiles, chunks = length // TILE, length // CHUNK
    per_tile = TILE // CHUNK
    blocks = hidden_units // HALF
    up_pairs = [(i, i + 1) for i in range(size - 1)]
    down_pairs = [(j, i) for i, j in up_pairs]

    def borders(x, before_of, after_of):
        return (
            lax.ppermute(before_of(x), "seq", up_pairs),
            lax.ppermute(after_of(x), "seq", down_pairs),
        )

    above, below = borders(tokens, lambda x: x[:, length - GRID :], lambda x: x[:, :GRID])

    features = time_features(timesteps)
    first = product(features, time_first)
    embed = product(jax.nn.silu(first), time_second)
    onehot = (class_ids[:, None] == jnp.arange(CLASSES, dtype=jnp.int32)[None, :]).astype(F32)
    embed = embed + product(onehot, class_table)
    modul = (product(jax.nn.silu(embed), ada_weight) + ada_bias).reshape(count, 6, width)

    real = jnp.sum(valid_mask, axis=1, dtype=jnp.int32)
    edge = jnp.stack([mine == 0, mine == size - 1]).astype(jnp.int32)
    weights = jnp.concatenate(
        [query_proj * HEAD_DIM ** (-0.5), key_proj, value_proj, product(decay_down, decay_up)],
        axis=1,
    )
    row = (length, width)
    image_row = (per_image(row), (count,) + row)
    dense = 2 * 3 * count * length * width
    (
        normed,
        conv,
        query,
        keys,
        values,
        cumul,
        slope,
        far,
        states,
        fades,
        message,
    ) = call(
        front_kernel,
        (count,),
        [
            per_image(row),
            per_image((GRID, width)),
            per_image((GRID, width)),
            per_image((6, width)),
            whole((9, width)),
            whole((width, 4 * width)),
            whole((1, width)),
        ],
        [(per_image((length + 2 * GRID, width)), (count, length + 2 * GRID, width))]
        + [image_row] * 7
        + [
            (
                per_image((chunks, PAIRS, LANES, LANES)),
                (count, chunks, PAIRS, LANES, LANES),
            ),
            (per_image((chunks, 8, width)), (count, chunks, 8, width)),
            (per_image((PAIRS, HEAD_DIM + 8, LANES)), (count, PAIRS, HEAD_DIM + 8, LANES)),
        ],
        [
            pltpu.VMEM((6 * width, 4 * width), BF16),
            pltpu.VMEM((PAIRS, LANES, LANES), F32),
            pltpu.VMEM((8, width), F32),
        ],
        flops=dense * 4 * width,
        moved=4 * count * length * width * 10,
        prefetch=2,
    )(edge, real, tokens, above, below, modul, conv_taps, weights, decay_bias[None])

    def tiled(shape=(TILE, width)):
        return pl.BlockSpec((None,) + shape, lambda n, i: (n, i, 0))

    tile_row = (tiled(), (count,) + row)
    pair_spec = pl.BlockSpec(
        (None, per_tile, PAIRS, LANES, LANES), lambda n, i: (n, i, 0, 0, 0)
    )
    state_spec = pl.BlockSpec((None, PAIRS, LANES, LANES), lambda n, i: (n, 0, 0, 0))
    score_shape = (count, chunks, PAIRS, 2 * CHUNK, CHUNK)
    score_spec = pl.BlockSpec(
        (None, per_tile, PAIRS, 2 * CHUNK, CHUNK), lambda n, i: (n, i, 0, 0, 0)
    )
    normed_spec = per_image((length + 2 * GRID, width))
    state_in = chained(message, "seq", False)
    inner, scores, gate_in = call(
        inner_kernel,
        (count, tiles),
        [tiled()] * 4 + [pair_spec, normed_spec, whole((width, width))],
        [tile_row, (score_spec, score_shape), tile_row],
        [pltpu.VMEM((3 * width, width), BF16), pltpu.VMEM((PAIRS, 2 * CHUNK, CHUNK), F32)],
        flops=dense * 2 * width,
        moved=4 * count * length * width * 9,
    )(query, keys, values, cumul, states, normed, gate_proj)

    square, up_shape, down_shape = (width, width), (width, hidden_units), (hidden_units, width)
    mod_spec = per_image((6, width))
    dmod_spec = per_image((8, width))
    (
        block_out,
        dmid,
        datt,
        dnorm,
        g_out,
        g_gate,
        g_up,
        g_down,
        dmod_tail,
        dstate,
    ) = call(
        tail_kernel,
        (count, tiles),
        [tiled(), tiled(), tiled(), normed_spec, tiled(), tiled(), state_spec, mod_spec]
        + [whole(square), whole(square), whole(up_shape), whole(down_shape)],
        [tile_row] * 4
        + [(whole(shape), shape) for shape in (square, square, up_shape, down_shape)]
        + [
            (dmod_spec, (count, 8, width)),
            (state_spec, (count, PAIRS, LANES, LANES)),
        ],
        [
            pltpu.VMEM((3 * width, width), BF16),
            pltpu.VMEM((width, 3 * width), BF16),
            pltpu.VMEM((width, 3 * width), BF16),
            pltpu.VMEM((blocks, 3 * width, HALF), BF16),
            pltpu.VMEM((blocks, 2 * width, HALF), BF16),
            pltpu.VMEM((blocks, 2 * HALF, width), BF16),
            pltpu.VMEM((blocks, HALF, 3 * width), BF16),
            pltpu.VMEM((blocks, width, HALF), F32),
            pltpu.VMEM((TILE, width), F32),
            pltpu.VMEM((TILE, width), F32),
        ],
        flops=dense * 3 * (2 * hidden_units + 2 * width),
        moved=4 * count * length * width * 12,
    )(
        inner,
        far,
        tokens,
        normed,
        gate_in,
        cotangent,
        state_in,
        modul,
        out_proj,
        gate_proj,
        mlp_up,
        mlp_down,
    )

    dcompact = dstate[:, :, :HEAD_DIM] + dstate[:, :, HEAD_DIM:]
    d_message = jnp.concatenate([dcompact, message[:, :, HEAD_DIM:]], axis=2)
    d_outgoing = chained(d_message, "seq", True)
    fade_spec = pl.BlockSpec((None, per_tile, 8, width), lambda n, i: (n, i, 0, 0))
    dquery, dkeys, dvalues, full = call(
        inner_back_kernel,
        (count, tiles),
        [tiled()] * 5 + [score_spec, pair_spec, fade_spec, state_spec],
        [tile_row] * 3 + [(pair_spec, (count, chunks, PAIRS, LANES, LANES))],
        [
            pltpu.VMEM((PAIRS, 2 * CHUNK, CHUNK), F32),
            pltpu.VMEM((CHUNK, width), F32),
            pltpu.VMEM((CHUNK, width), F32),
        ],
        flops=dense * 2 * width,
        moved=4 * count * length * width * 12,
    )(query, keys, values, cumul, datt, scores, states, fades, state_in)

    def turned(shape=(TILE, width)):
        return pl.BlockSpec((None,) + shape, lambda n, i, *_: (n, tiles - 1 - i, 0))

    dproj, dconv, dbias = call(
        state_back_kernel,
        (count, tiles),
        [turned()] * 10
        + [
            pl.BlockSpec(
                (None, per_tile, PAIRS, LANES, LANES),
                lambda n, i, *_: (n, tiles - 1 - i, 0, 0, 0),
            ),
            pl.BlockSpec((None, PAIRS, LANES, LANES), lambda n, i, *_: (n, 0, 0, 0)),
            whole((width, 4 * width)),
        ],
        [
            (turned((TILE, 4 * width)), (count, length, 4 * width)),
            (turned(), (count,) + row),
            (whole((8, width)), (8, width)),
        ],
        [
            pltpu.VMEM((width, 3 * 4 * width), BF16),
            pltpu.VMEM((PAIRS, LANES, LANES), F32),
        ],
        flops=dense * 5 * width,
        moved=4 * count * length * width * 16,
        prefetch=1,
    )(
        real,
        query,
        keys,
        values,
        cumul,
        slope,
        conv,
        datt,
        dquery,
        dkeys,
        dvalues,
        full,
        d_outgoing,
        weights,
    )

    d_above, d_below = borders(dconv, lambda x: x[:, length - GRID :], lambda x: x[:, :GRID])
    (g_weights,) = call(
        weight_kernel,
        (count, tiles),
        [tiled(), tiled((TILE, 4 * width))],
        [(whole((width, 4 * width)), (width, 4 * width))],
        [],
        flops=dense * 4 * width,
        moved=4 * count * length * width * 7,
    )(conv, dproj)

    tokens_grad, dmod_front, dtaps = call(
        front_back_kernel,
        (count,),
        [
            per_image(row),
            per_image((length + 2 * GRID, width)),
            per_image(row),
            per_image((GRID, width)),
            per_image((GRID, width)),
            per_image(row),
            per_image(row),
            per_image((6, width)),
            whole((9, width)),
        ],
        [
            image_row,
            (per_image((8, width)), (count, 8, width)),
            (whole((9, 8, width)), (9, 8, width)),
        ],
        [pltpu.VMEM((length + 2 * GRID, width), F32)],
        flops=count * length * width * 100,
        moved=4 * count * length * width * 6,
    )(tokens, normed, dconv, d_above, d_below, dnorm, dmid, modul, conv_taps)

    g_query, g_key, g_value, g_decay = jnp.split(g_weights, 4, axis=1)
    g_query = g_query * HEAD_DIM ** (-0.5)
    g_decay_down = product(g_decay, decay_up.T)
    g_decay_up = product(decay_down.T, g_decay)
    both = ("img", "seq")
    g_gate, g_out, g_up, g_down = lax.psum((g_gate, g_out, g_up, g_down), both)
    late = lax.psum(
        (
            jnp.sum(dtaps, axis=1),
            g_query,
            g_key,
            g_value,
            g_decay_down,
            g_decay_up,
            jnp.sum(dbias, axis=0),
        ),
        both,
    )

    dmod = dmod_front[:, :6].reshape(count, 6 * width) + dmod_tail[:, :6].reshape(count, 6 * width)
    images = lax.all_gather(
        jnp.concatenate([lax.psum(dmod, "seq"), features, first, embed], axis=1), "img", tiled=True
    )
    ids = lax.all_gather(class_ids, "img", tiled=True)
    dmod = images[:, : 6 * width]
    features = images[:, 6 * width : 6 * width + FREQ]
    first = images[:, 6 * width + FREQ : 7 * width + FREQ]
    embed = images[:, 7 * width + FREQ :]
    g_ada_weight = product(jax.nn.silu(embed).T, dmod)
    g_ada_bias = jnp.sum(dmod, axis=0)

    def silu_back(x, grad):
        sig = jax.nn.sigmoid(x)
        return grad * (sig * (1.0 + x * (1.0 - sig)))

    dembed = silu_back(embed, product(dmod, ada_weight.T))
    hot = (ids[None, :] == jnp.arange(CLASSES, dtype=jnp.int32)[:, None]).astype(F32)
    g_class_table = product(hot, dembed)
    g_time_second = product(jax.nn.silu(first).T, dembed)
    dfirst = silu_back(first, product(dembed, time_second.T))
    g_time_first = product(features.T, dfirst)
    return (
        block_out,
        tokens_grad,
        g_time_first,
        g_time_second,
        g_class_table,
        g_ada_weight,
        g_ada_bias,
        late[0],
        late[1],
        late[2],
        late[3],
        late[4],
        late[5],
        late[6],
        g_gate,
        g_out,
        g_up,
        g_down,
    )


def solution(mesh):
    image, shared = P("img", "seq", None), P()
    return jax.shard_map(
        body,
        mesh=mesh,
        in_specs=(image, P("img", "seq"), P("img"), P("img")) + (shared,) * 16 + (image,),
        out_specs=(image, image) + (shared,) * 16,
        check_vma=False,
    )
```

```python
import functools
import math

import jax
import jax.numpy as jnp
from jax import lax
from jax.experimental import pallas as pl
from jax.experimental.pallas import tpu as pltpu
from jax.sharding import PartitionSpec as P

HEADS = 6
HEAD_DIM = 64
CLASSES = 1000
FREQ = 256
GRID = 64
WIDTH = 384
PAIRS = 3
LANES = 128
CHUNK = 128
TILE = 256
BLOCK = 768
ROWS = 1280
SMALL = 48
SPAN = 120.0
HIGH = lax.Precision.HIGHEST
F32 = jnp.float32
BF16 = jnp.bfloat16
GELU_C = math.sqrt(2.0 / math.pi)


def product(left, right):
    return jnp.dot(left, right, precision=HIGH, preferred_element_type=F32)


def dot(a, b, ca=1, cb=0):
    return lax.dot_general(a, b, (((ca,), (cb,)), ((), ())), preferred_element_type=F32)


def split(x):
    high = x.astype(BF16)
    return high, (x - high.astype(F32)).astype(BF16)


def mm3(a, b, ca=1, cb=0):
    return dot(a[0], b[0], ca, cb) + dot(a[1], b[0], ca, cb) + dot(a[0], b[1], ca, cb)


def split3(x):
    high = x.astype(BF16)
    rest = x - high.astype(F32)
    middle = rest.astype(BF16)
    return high, middle, (rest - middle.astype(F32)).astype(BF16)


def mm6(a, b, ca=1, cb=0):
    terms = ((0, 0), (0, 1), (1, 0), (1, 1), (0, 2), (2, 0))
    return sum(dot(a[i], b[j], ca, cb) for i, j in reversed(terms))


def wide6(x):
    h, m, l = split3(x)
    return jnp.concatenate([h, h, m, m, h, l], axis=1)


def tall6(w):
    h, m, l = split3(w)
    return jnp.concatenate([h, m, h, m, l, h], axis=0)


def wide3(x):
    high, low = split(x)
    return jnp.concatenate([high, high, low], axis=1)


def wide(x):
    high, low = split(x)
    return jnp.concatenate([high, low, high], axis=1)


def tall(w):
    high, low = split(w)
    return jnp.concatenate([high, high, low], axis=0)


def across(w):
    high, low = split(w)
    return jnp.concatenate([high, high, low], axis=1)


def lanes(x, p):
    return x[..., p * LANES : (p + 1) * LANES]


def first_half(shape):
    return lax.broadcasted_iota(jnp.int32, shape, len(shape) - 1) < HEAD_DIM


def block_diagonal(square):
    rows = lax.broadcasted_iota(jnp.int32, square.shape, 0) < HEAD_DIM
    return jnp.where(rows == first_half(square.shape), square, 0.0)


def head_mean(x):
    rows = lax.broadcasted_iota(jnp.int32, (LANES, LANES), 0) < HEAD_DIM
    ones = jnp.where(rows == first_half((LANES, LANES)), 1.0 / HEAD_DIM, 0.0).astype(BF16)
    high, low = split(x)
    return dot(
        jnp.concatenate([high, low], axis=1), jnp.concatenate([ones, ones], axis=0)
    )


def head_means(x):
    return jnp.concatenate([head_mean(lanes(x, p)) for p in range(PAIRS)], axis=1)


def stacked_heads(x):
    keep = first_half(x.shape)
    zero = jnp.zeros_like(x)
    return jnp.concatenate([jnp.where(keep, x, zero), jnp.where(keep, zero, x)], axis=0)


def merged_heads(x):
    rows = x.shape[0] // 2
    return jnp.where(first_half((rows, LANES)), x[:rows], x[rows:])


def sigmoid(x):
    return 1.0 / (1.0 + jnp.exp(-x))


def shifted(x, step):
    rows = x.shape[0]
    column = lax.broadcasted_iota(jnp.int32, x.shape, 0) % GRID
    if step == 1:
        return jnp.where(column == 0, 0.0, pltpu.roll(x, 1, 0))
    return jnp.where(column == GRID - 1, 0.0, pltpu.roll(x, rows - 1, 0))


def normalized(x):
    center = x - jnp.mean(x, axis=-1, keepdims=True)
    rate = lax.rsqrt(jnp.mean(center * center, axis=-1, keepdims=True) + 1e-06)
    return center * rate, rate


def normal_back(dhat, hat, rate):
    return rate * (
        dhat
        - jnp.mean(dhat, axis=-1, keepdims=True)
        - hat * jnp.mean(dhat * hat, axis=-1, keepdims=True)
    )


def triangle(size, upper):
    rows = lax.broadcasted_iota(jnp.int32, (size, size), 0)
    cols = lax.broadcasted_iota(jnp.int32, (size, size), 1)
    return jnp.where(cols >= rows if upper else cols <= rows, 1.0, 0.0).astype(BF16)


def running_sum(x, upper):
    tri = triangle(x.shape[0], upper)
    high = x.astype(BF16)
    rest = x - high.astype(F32)
    middle = rest.astype(BF16)
    low = (rest - middle.astype(F32)).astype(BF16)
    return dot(tri, high) + dot(tri, middle) + dot(tri, low)


def opening(tile):
    return (lax.axis_index("seq") == 0) & (tile == 0)


def spread(compact):
    keep = first_half(compact.shape)
    return jnp.concatenate(
        [jnp.where(keep, compact, 0.0), jnp.where(keep, 0.0, compact)], axis=0
    )


def linked(parts, p):
    total = jnp.zeros((HEAD_DIM, LANES), F32)
    for part in reversed(parts):
        total = part[p, 0:HEAD_DIM, :] + part[p, HEAD_DIM : HEAD_DIM + 1, :] * total
    return spread(total)


def as_column(row):
    return jnp.broadcast_to(row, (8, row.shape[1])).T[:, 0:1]


def applied(row, w_ref):
    return jnp.sum(as_column(row) * w_ref[...], axis=0, keepdims=True)


def condition_kernel(ids_ref, feat_ref, first_w_ref, second_w_ref, row_ref, ada_ref, bias_ref, mod_ref, info_ref):
    features = feat_ref[...]
    first = applied(features, first_w_ref)
    embed = applied(first * sigmoid(first), second_w_ref)
    at = lax.broadcasted_iota(jnp.int32, row_ref.shape, 0) == ids_ref[pl.program_id(0)] % 8
    embed = embed + jnp.sum(jnp.where(at, row_ref[...], 0.0), axis=0, keepdims=True)
    modul = applied(embed * sigmoid(embed), ada_ref)
    for j in range(6):
        at = slice(j * WIDTH, (j + 1) * WIDTH)
        mod_ref[j : j + 1, :] = modul[:, at] + bias_ref[at][None, :]
    info_ref[...] = jnp.zeros_like(info_ref)
    info_ref[0:1, 0:FREQ] = features
    info_ref[1:2, :] = first
    info_ref[2:3, :] = embed


def embed_kernel(ids_ref, rows_ref, ada_ref, second_ref, gf_ref, gs_ref, gc_ref, ga_ref, gb_ref):
    images = rows_ref.shape[1]
    features, first, embed = rows_ref[6][:, 0:FREQ], rows_ref[7], rows_ref[8]

    def silu_back(x, grad):
        sig = sigmoid(x)
        return grad * (sig * (1.0 + x * (1.0 - sig)))

    act = split((embed * sigmoid(embed)).T)
    dembed = jnp.zeros((images, WIDTH), F32)
    for j in range(6):
        at = slice(j * WIDTH, (j + 1) * WIDTH)
        dmod = split(rows_ref[j])
        ga_ref[:, at] = mm3(act, dmod)
        gb_ref[:, at] = jnp.sum(rows_ref[j], axis=0, keepdims=True)
        dembed = dembed + mm3(dmod, split(ada_ref[:, at]), 1, 1)
    dembed = silu_back(embed, dembed)
    gc_ref[...] = jnp.zeros_like(gc_ref)

    def put(n, carry):
        mine = lax.broadcasted_iota(jnp.int32, (images, WIDTH), 0) == n
        row = jnp.sum(jnp.where(mine, dembed, 0.0), axis=0, keepdims=True)
        gc_ref[pl.ds(ids_ref[n], 1), :] += row
        return carry

    lax.fori_loop(0, images, put, 0)
    de = split(dembed)
    gs_ref[...] = mm3(split((first * sigmoid(first)).T), de)
    dfirst = silu_back(first, mm3(de, split(second_ref[...]), 1, 1))
    gf_ref[...] = mm3(split(features.T), split(dfirst))


def front_kernel(
    tok_ref,
    top_ref,
    bot_ref,
    valid_ref,
    mod_ref,
    taps_ref,
    wq_ref,
    wk_ref,
    wv_ref,
    down_ref,
    up_ref,
    bias_ref,
    w_ref,
    normed_ref,
    conv_ref,
    q_ref,
    k_ref,
    v_ref,
    cum_ref,
    slope_ref,
    far_ref,
    state_ref,
    fade_ref,
    out_ref,
    w3_ref,
    proj_ref,
    st_ref,
    dev_ref,
):
    image, i = pl.program_id(0), pl.program_id(1)
    length = tok_ref.shape[0]

    @pl.when((image == 0) & (i == 0))
    def _():
        w_ref[:, 0:WIDTH] = wq_ref[...] * HEAD_DIM ** (-0.5)
        w_ref[:, WIDTH : 2 * WIDTH] = wk_ref[...]
        w_ref[:, 2 * WIDTH : 3 * WIDTH] = wv_ref[...]
        w_ref[:, 3 * WIDTH :] = mm6(split3(down_ref[...]), split3(up_ref[...]), 0, 0)
        w3_ref[...] = tall6(w_ref[...])

    real = jnp.sum(valid_ref[...], axis=1, keepdims=True)
    shift = mod_ref[0:1, :]
    scale = 1.0 + mod_ref[1:2, :]

    def modulated(x):
        return normalized(x)[0] * scale + shift

    @pl.when(i == 0)
    def _():
        normed_ref[0:GRID, :] = jnp.where(
            lax.axis_index("seq") == 0, 0.0, modulated(top_ref[...])
        )
        normed_ref[pl.ds(length + GRID, GRID), :] = jnp.where(
            lax.axis_index("seq") == lax.axis_size("seq") - 1, 0.0, modulated(bot_ref[...])
        )
        for at in range(0, length, TILE):
            normed_ref[GRID + at : GRID + at + TILE, :] = modulated(tok_ref[at : at + TILE, :])
        st_ref[...] = jnp.zeros_like(st_ref)
        dev_ref[...] = jnp.zeros_like(dev_ref)

    start = pl.multiple_of(i * TILE, TILE)
    rows = [normed_ref[pl.ds(start + a * GRID, TILE), :] for a in range(3)]
    parts = [
        sum(taps_ref[3 * a + b : 3 * a + b + 1, :] * rows[a] for a in range(3))
        for b in range(3)
    ]
    conv = shifted(parts[0], 1) + parts[1] + shifted(parts[2], -1)
    conv_ref[...] = conv
    hidden = conv * sigmoid(conv)
    first = opening(i)

    @pl.when(first)
    def _():
        proj_ref[...] = dot(wide6(hidden), w3_ref[...])

    @pl.when(jnp.logical_not(first))
    def _():
        proj_ref[...] = dot(wide3(hidden), w3_ref[0 : 3 * WIDTH, :])

    proj = proj_ref[...]
    keep = (
        lax.broadcasted_iota(jnp.int32, (TILE, WIDTH), 0) + start < real
    )
    q = proj[:, :WIDTH]
    k = jnp.where(keep, proj[:, WIDTH : 2 * WIDTH], 0.0)
    v = jnp.where(keep, proj[:, 2 * WIDTH : 3 * WIDTH], 0.0)
    x = proj[:, 3 * WIDTH :] + bias_ref[...][None, :]
    small = jnp.exp(-jnp.abs(x))
    gates = jnp.where(keep, (jnp.minimum(x, 0.0) - jnp.log1p(small)) * (1.0 / 16.0), 0.0)
    slope = jnp.where(x >= 0, small, 1.0) / (1.0 + small)
    slope_ref[...] = jnp.where(keep, slope * (1.0 / 16.0), 0.0)
    q_ref[...] = q
    k_ref[...] = k
    v_ref[...] = v
    for c in range(TILE // CHUNK):
        at = slice(c * CHUNK, (c + 1) * CHUNK)
        cum = running_sum(gates[at], False)
        cum_ref[at, :] = cum
        final = cum[CHUNK - 1 : CHUNK, :]
        dev = dev_ref[0:1, :]
        far_ref[at, :] = q[at] * jnp.exp(cum + dev)
        fade_ref[c] = jnp.broadcast_to(jnp.exp(dev), (8, WIDTH))
        kd = k[at] * jnp.exp(final - cum)
        factor = jnp.exp(final)
        for p in range(PAIRS):
            state_ref[c, p] = st_ref[p]
            update = mm3(split(lanes(v[at], p)), split(lanes(kd, p)), 0, 0)
            st_ref[p] = lanes(factor, p) * st_ref[p] + block_diagonal(update)
        dev_ref[...] = dev_ref[...] + final

    @pl.when(i == pl.num_programs(1) - 1)
    def _():
        for p in range(PAIRS):
            out_ref[p, 0:HEAD_DIM, :] = st_ref[p, 0:HEAD_DIM, :] + st_ref[p, HEAD_DIM:, :]
            out_ref[p, HEAD_DIM:, :] = jnp.exp(lanes(dev_ref[...], p))


def exact_scores(q_ref, k_ref, cum_ref, base, s_ref):
    q = q_ref[pl.ds(base, CHUNK), :]
    cum = cum_ref[pl.ds(base, CHUNK), :]
    s_ref[...] = jnp.zeros_like(s_ref)

    def step(j, carry):
        key = k_ref[pl.ds(base + j, 1), :]
        weight = jnp.exp(jnp.minimum(cum - cum_ref[pl.ds(base + j, 1), :], 0.0))
        terms = q * key * weight
        for p in range(PAIRS):
            column = jnp.sum(stacked_heads(lanes(terms, p)), axis=1, keepdims=True)
            at = lax.broadcasted_iota(jnp.int32, (2 * CHUNK, CHUNK), 1) == j
            s_ref[p] = jnp.where(at, column, s_ref[p])
        return carry

    lax.fori_loop(0, CHUNK, step, 0)


def causal_two():
    rows = lax.broadcasted_iota(jnp.int32, (2 * CHUNK, CHUNK), 0) % CHUNK
    return rows >= lax.broadcasted_iota(jnp.int32, (2 * CHUNK, CHUNK), 1)


def inner_kernel(
    q_ref, k_ref, v_ref, cum_ref, state_ref, normed_ref, gate_ref, o_ref, s_ref, gp_ref, w3_ref, tmp_ref
):
    @pl.when((pl.program_id(0) == 0) & (pl.program_id(1) == 0))
    def _():
        w3_ref[...] = tall(gate_ref[...])

    start = pl.multiple_of(pl.program_id(1) * TILE + GRID, GRID)
    gp_ref[...] = dot(wide(normed_ref[pl.ds(start, TILE), :]), w3_ref[...])
    mask = causal_two()
    for c in range(TILE // CHUNK):
        base = c * CHUNK
        at = slice(base, base + CHUNK)
        q = q_ref[at, :]
        k = k_ref[at, :]
        cum = cum_ref[at, :]
        final = cum[CHUNK - 1 : CHUNK, :]
        wild = jnp.max(-final) > SPAN
        middle = 0.5 * final
        qf = split3(q * jnp.exp(cum - middle))
        kf = split3(k * jnp.exp(middle - cum))
        for p in range(PAIRS):
            qp = tuple(stacked_heads(lanes(part, p)) for part in qf[:2])
            kp = tuple(lanes(part, p) for part in kf[:2])
            tmp_ref[p] = mm3(qp, kp, 1, 1)

        @pl.when(opening(pl.program_id(1)) & (c == 0))
        def _():
            for p in range(PAIRS):
                qp = tuple(stacked_heads(lanes(part, p)) for part in qf)
                kp = tuple(lanes(part, p) for part in kf)
                tmp_ref[p] = mm6(qp, kp, 1, 1)

        @pl.when(wild)
        def _():
            exact_scores(q_ref, k_ref, cum_ref, base, tmp_ref)

        qd = q * jnp.exp(cum)
        for p in range(PAIRS):
            s = jnp.where(mask, tmp_ref[p], 0.0)
            s_ref[c, p] = s
            inner = merged_heads(mm3(split(s), split(lanes(v_ref[at, :], p))))
            outer = mm3(split(lanes(qd, p)), split(state_ref[c, p]), 1, 1)
            o_ref[at, p * LANES : (p + 1) * LANES] = inner + outer


def mix_kernel(o_ref, far_ref, tok_ref, gp_ref, mod_ref, out_w_ref, *rest):
    parts, (mid_ref, branch_ref, att_ref, st_ref, o3_ref) = rest[:-5], rest[-5:]
    image, tile = pl.program_id(0), pl.program_id(1)

    @pl.when((image == 0) & (tile == 0))
    def _():
        o3_ref[...] = tall(out_w_ref[...])

    @pl.when(tile == 0)
    def _():
        for p in range(PAIRS):
            st_ref[p] = linked(parts, p)

    far = split(far_ref[...])
    att = o_ref[...] + jnp.concatenate(
        [
            mm3(tuple(lanes(part, p) for part in far), split(st_ref[p]), 1, 1)
            for p in range(PAIRS)
        ],
        axis=1,
    )
    att_ref[...] = att
    rate = lax.rsqrt(head_means(att * att) + 1e-05)
    gp = gp_ref[...]
    branch = dot(wide(att * rate * (gp * sigmoid(gp))), o3_ref[...])
    branch_ref[...] = branch
    mid_ref[...] = tok_ref[...] + mod_ref[2:3, :] * branch


def mlp_kernel(last, mid_ref, cot_ref, mod_ref, up_ref, down_ref, *rest):
    if last:
        mlp_in_ref, dsec_in_ref, block_ref, dmid_ref, dmod_ref = rest[:5]
    else:
        block_ref, dmid_ref = rest[:2]
    g_ref, u3_ref, ut_ref, d_ref, dt3_ref, gu_ref, gd_ref = rest[-7:]
    image, tile = pl.program_id(0), pl.program_id(1)

    @pl.when((image == 0) & (tile == 0))
    def _():
        u3_ref[...] = tall(up_ref[...])
        ut_ref[...] = jnp.concatenate(split(up_ref[...]), axis=0)
        d_ref[...] = jnp.concatenate(split(down_ref[...]), axis=0)
        dt3_ref[...] = across(down_ref[...])
        gu_ref[...] = jnp.zeros_like(gu_ref)
        gd_ref[...] = jnp.zeros_like(gd_ref)

    shift_b = mod_ref[3:4, :]
    scale_b = 1.0 + mod_ref[4:5, :]
    gate_b = mod_ref[5:6, :]
    middle = mid_ref[...]
    hat, rate_b = normalized(middle)
    second = hat * scale_b + shift_b
    cot = cot_ref[...]
    dmlp = cot * gate_b
    u = dot(wide(second), u3_ref[...])
    square = u * u
    th = jnp.tanh(GELU_C * (u + 0.044715 * u * square))
    slope = 0.5 * (1.0 + th) + 0.5 * u * (1.0 - th * th) * (
        GELU_C * (1.0 + 3.0 * 0.044715 * square)
    )
    act = split(0.5 * u * (1.0 + th))
    mlp = mm3(act, (d_ref[0:BLOCK, :], d_ref[BLOCK:, :]))
    du = split(dot(wide(dmlp), dt3_ref[...], 1, 1) * slope)
    dsec = mm3(du, (ut_ref[0:WIDTH, :], ut_ref[WIDTH:, :]), 1, 1)
    gu_ref[...] += mm3(split(second.T), du)
    gd_ref[...] += mm3(split(dmlp.T), act)
    if not last:
        block_ref[...] = mlp
        dmid_ref[...] = dsec
    else:
        mlp = mlp + mlp_in_ref[...]
        dsec = dsec + dsec_in_ref[...]
        block_ref[...] = middle + gate_b * mlp
        dmid_ref[...] = cot + normal_back(dsec * scale_b, hat, rate_b)

        @pl.when(tile == 0)
        def _():
            dmod_ref[...] = jnp.zeros_like(dmod_ref)

        dmod_ref[3:4, :] += jnp.sum(dsec, axis=0, keepdims=True)
        dmod_ref[4:5, :] += jnp.sum(dsec * hat, axis=0, keepdims=True)
        dmod_ref[5:6, :] += jnp.sum(cot * mlp, axis=0, keepdims=True)

    @pl.when((image == pl.num_programs(0) - 1) & (tile == pl.num_programs(1) - 1))
    def _():
        for j in range(BLOCK // WIDTH):
            at = slice(j * WIDTH, (j + 1) * WIDTH)
            g_ref[at, :] = gu_ref[:, at]
        g_ref[BLOCK:, :] = gd_ref[...].T


def mix_back_kernel(
    dmid_ref,
    branch_ref,
    att_ref,
    gp_ref,
    far_ref,
    normed_ref,
    mod_ref,
    message_ref,
    out_w_ref,
    gate_w_ref,
    datt_ref,
    dnorm_ref,
    g_ref,
    dmod_ref,
    dmessage_ref,
    ot3_ref,
    gt3_ref,
    dst_ref,
):
    image, tile = pl.program_id(0), pl.program_id(1)

    @pl.when((image == 0) & (tile == 0))
    def _():
        ot3_ref[...] = across(out_w_ref[...])
        gt3_ref[...] = across(gate_w_ref[...])
        g_ref[...] = jnp.zeros_like(g_ref)

    @pl.when(tile == 0)
    def _():
        dmod_ref[...] = jnp.zeros_like(dmod_ref)
        dst_ref[...] = jnp.zeros_like(dst_ref)

    dmid = dmid_ref[...]
    dmod_ref[2:3, :] += jnp.sum(dmid * branch_ref[...], axis=0, keepdims=True)
    dbr = split(dmid * mod_ref[2:3, :])
    dy = dot(jnp.concatenate([dbr[0], dbr[1], dbr[0]], axis=1), ot3_ref[...], 1, 1)
    att = att_ref[...]
    rate = lax.rsqrt(head_means(att * att) + 1e-05)
    unit = att * rate
    gp = gp_ref[...]
    sig = sigmoid(gp)
    gate = gp * sig
    g_ref[0:WIDTH, :] += mm3(split(unit * gate), dbr, 0, 0)
    dunit = dy * gate
    datt = rate * (dunit - unit * head_means(dunit * unit))
    datt_ref[...] = datt
    dg = split((dy * unit) * (sig * (1.0 + gp * (1.0 - sig))))
    dnorm_ref[...] = dot(jnp.concatenate([dg[0], dg[1], dg[0]], axis=1), gt3_ref[...], 1, 1)
    start = pl.multiple_of(tile * TILE + GRID, GRID)
    g_ref[WIDTH:, :] += mm3(split(normed_ref[pl.ds(start, TILE), :]), dg, 0, 0)
    da = split(datt)
    far = split(far_ref[...])
    for p in range(PAIRS):
        dst_ref[p] += block_diagonal(
            mm3(tuple(lanes(part, p) for part in da), tuple(lanes(part, p) for part in far), 0, 0)
        )

    @pl.when(tile == pl.num_programs(1) - 1)
    def _():
        for p in range(PAIRS):
            dmessage_ref[p, 0:HEAD_DIM, :] = dst_ref[p, 0:HEAD_DIM, :] + dst_ref[p, HEAD_DIM:, :]
            dmessage_ref[p, HEAD_DIM:, :] = message_ref[p, HEAD_DIM:, :]


def exact_back(q_ref, k_ref, cum_ref, ds_ref, base, dq_ref, dk_ref):
    q = q_ref[pl.ds(base, CHUNK), :]
    cum = cum_ref[pl.ds(base, CHUNK), :]
    dq_ref[...] = jnp.zeros_like(dq_ref)

    def step(j, carry):
        key = k_ref[pl.ds(base + j, 1), :]
        weight = jnp.exp(jnp.minimum(cum - cum_ref[pl.ds(base + j, 1), :], 0.0))
        at = lax.broadcasted_iota(jnp.int32, (2 * CHUNK, CHUNK), 1) == j
        columns = []
        for p in range(PAIRS):
            column = jnp.sum(jnp.where(at, ds_ref[p], 0.0), axis=1, keepdims=True)
            columns.append(merged_heads(jnp.broadcast_to(column, (2 * CHUNK, LANES))))
        ds = jnp.concatenate(columns, axis=1) * weight
        dq_ref[...] += ds * key
        dk_ref[pl.ds(j, 1), :] = jnp.sum(ds * q, axis=0, keepdims=True)
        return carry

    lax.fori_loop(0, CHUNK, step, 0)


def inner_back_kernel(
    q_ref,
    k_ref,
    v_ref,
    cum_ref,
    datt_ref,
    s_ref,
    state_ref,
    fade_ref,
    st_ref,
    dq_ref,
    dk_ref,
    dv_ref,
    full_ref,
    ds_ref,
    dqi_ref,
    dki_ref,
):
    mask = causal_two()
    for c in range(TILE // CHUNK):
        base = c * CHUNK
        at = slice(base, base + CHUNK)
        q = q_ref[at, :]
        k = k_ref[at, :]
        cum = cum_ref[at, :]
        final = cum[CHUNK - 1 : CHUNK, :]
        wild = jnp.max(-final) > SPAN
        middle = 0.5 * final
        eq = jnp.exp(cum - middle)
        ek = jnp.exp(middle - cum)
        qf = split(q * eq)
        kf = split(k * ek)
        da = split3(datt_ref[at, :])
        vs = split3(v_ref[at, :])
        for p in range(PAIRS):
            da2 = tuple(stacked_heads(lanes(part, p)) for part in da[:2])
            vp = tuple(lanes(part, p) for part in vs[:2])
            ds_ref[p] = jnp.where(mask, mm3(da2, vp, 1, 1), 0.0)

        @pl.when(opening(pl.program_id(1)) & (c == 0))
        def _():
            for p in range(PAIRS):
                da2 = tuple(stacked_heads(lanes(part, p)) for part in da)
                vp = tuple(lanes(part, p) for part in vs)
                ds_ref[p] = jnp.where(mask, mm6(da2, vp, 1, 1), 0.0)

        for p in range(PAIRS):
            da2 = tuple(stacked_heads(lanes(part, p)) for part in da[:2])
            ds2 = split(ds_ref[p])
            kp = tuple(lanes(part, p) for part in kf)
            qp = tuple(lanes(part, p) for part in qf)
            dqi_ref[:, p * LANES : (p + 1) * LANES] = merged_heads(mm3(ds2, kp)) * lanes(eq, p)
            q2 = tuple(stacked_heads(part) for part in qp)
            dki_ref[:, p * LANES : (p + 1) * LANES] = mm3(ds2, q2, 0, 0) * lanes(ek, p)
            s2 = split(s_ref[c, p])
            dv_ref[at, p * LANES : (p + 1) * LANES] = mm3(s2, da2, 0, 0)

        @pl.when(wild)
        def _():
            exact_back(q_ref, k_ref, cum_ref, ds_ref, base, dqi_ref, dki_ref)

        grow = jnp.exp(cum)
        for p in range(PAIRS):
            full = state_ref[c, p] + lanes(fade_ref[c, 0:1, :], p) * st_ref[p]
            full_ref[c, p] = full
            outer = mm3(tuple(lanes(part, p) for part in da[:2]), split(full))
            dq_ref[at, p * LANES : (p + 1) * LANES] = (
                dqi_ref[:, p * LANES : (p + 1) * LANES] + outer * lanes(grow, p)
            )
        dk_ref[at, :] = dki_ref[...]


def state_back_kernel(
    valid_ref,
    q_ref,
    k_ref,
    v_ref,
    cum_ref,
    slope_ref,
    conv_ref,
    datt_ref,
    dq_ref,
    dk_ref,
    dv_ref,
    full_ref,
    w_ref,
    *rest,
):
    parts, (proj_ref, dconv_ref, dbias_ref, wt3_ref, dst_ref) = rest[:-5], rest[-5:]
    image, turn = pl.program_id(0), pl.program_id(1)
    tile = pl.num_programs(1) - 1 - turn

    @pl.when((image == 0) & (turn == 0))
    def _():
        wt3_ref[...] = across(w_ref[...])
        dbias_ref[...] = jnp.zeros_like(dbias_ref)

    @pl.when(turn == 0)
    def _():
        for p in range(PAIRS):
            dst_ref[p] = linked(parts, p)

    count = jnp.sum(valid_ref[...], axis=1, keepdims=True)
    keep = (
        lax.broadcasted_iota(jnp.int32, (CHUNK, WIDTH), 0) + tile * TILE
    )
    for c in reversed(range(TILE // CHUNK)):
        at = slice(c * CHUNK, (c + 1) * CHUNK)
        q = q_ref[at, :]
        k = k_ref[at, :]
        cum = cum_ref[at, :]
        final = cum[CHUNK - 1 : CHUNK, :]
        late = jnp.exp(final - cum)
        kd = k * late
        v = v_ref[at, :]
        qd = split(q * jnp.exp(cum))
        da = split(datt_ref[at, :])
        factor = jnp.exp(final)
        dk_parts, dv_parts, cross = [], [], []
        for p in range(PAIRS):
            old = dst_ref[p]
            pair = split(old)
            dk_parts.append(mm3(split(lanes(v, p)), pair))
            dv_parts.append(mm3(split(lanes(kd, p)), pair, 1, 1))
            leaving = lanes(factor, p) * full_ref[c, p] + block_diagonal(
                mm3(split(lanes(v, p)), split(lanes(kd, p)), 0, 0)
            )
            cross.append(jnp.sum(leaving * old, axis=0, keepdims=True))
            update = mm3(
                tuple(lanes(part, p) for part in da), tuple(lanes(part, p) for part in qd), 0, 0
            )
            dst_ref[p] = lanes(factor, p) * old + block_diagonal(update)
        dq = dq_ref[at, :]
        dk = dk_ref[at, :] + jnp.concatenate(dk_parts, axis=1) * late
        dv = dv_ref[at, :] + jnp.concatenate(dv_parts, axis=1)
        dgates = running_sum(q * dq - k * dk, True) + jnp.concatenate(cross, axis=1)
        dx = dgates * slope_ref[at, :]
        real = keep + c * CHUNK < count
        dk = jnp.where(real, dk, 0.0)
        dv = jnp.where(real, dv, 0.0)
        dbias_ref[...] += jnp.sum(dx.reshape(CHUNK // 8, 8, WIDTH), axis=0)
        proj_ref[at, 0:WIDTH] = dq
        proj_ref[at, WIDTH : 2 * WIDTH] = dk
        proj_ref[at, 2 * WIDTH : 3 * WIDTH] = dv
        proj_ref[at, 3 * WIDTH :] = dx
    dhidden = dot(wide(proj_ref[...]), wt3_ref[...], 1, 1)
    conv = conv_ref[...]
    sig = sigmoid(conv)
    dconv_ref[...] = dhidden * (sig * (1.0 + conv * (1.0 - sig)))


def weight_kernel(conv_ref, proj_ref, dbias_ref, down_ref, up_ref, g_ref, acc_ref):
    image, tile = pl.program_id(0), pl.program_id(1)

    @pl.when((image == 0) & (tile == 0))
    def _():
        acc_ref[...] = jnp.zeros_like(acc_ref)

    conv = conv_ref[...]
    hidden = split((conv * sigmoid(conv)).T)
    for j in range(4):
        at = slice(j * WIDTH, (j + 1) * WIDTH)
        acc_ref[:, at] += mm3(hidden, split(proj_ref[:, at]))

    @pl.when((image == pl.num_programs(0) - 1) & (tile == pl.num_programs(1) - 1))
    def _():
        for j in range(3):
            grad = acc_ref[:, j * WIDTH : (j + 1) * WIDTH]
            g_ref[j * WIDTH : (j + 1) * WIDTH, :] = (
                grad * HEAD_DIM ** (-0.5) if j == 0 else grad
            )
        grad = acc_ref[:, 3 * WIDTH :]
        base = 3 * WIDTH
        rank = up_ref.shape[0]
        g_ref[base:, :] = jnp.zeros_like(g_ref[base:, :])
        g_ref[base : base + rank, :] = mm6(split3(up_ref[...]), split3(grad), 1, 1)
        g_ref[base + rank : base + 2 * rank, :] = mm6(split3(down_ref[...]), split3(grad))
        g_ref[base + 2 * rank : base + 2 * rank + 1, :] = jnp.sum(
            dbias_ref[...], axis=0, keepdims=True
        )


def front_back_kernel(
    tok_ref,
    normed_ref,
    dconv_ref,
    top_ref,
    bot_ref,
    dnorm_ref,
    dmid_ref,
    mod_ref,
    taps_ref,
    grad_ref,
    dmod_ref,
    dtaps_ref,
    pad_ref,
    taps_acc_ref,
):
    length = dconv_ref.shape[0]
    image, i = pl.program_id(0), pl.program_id(1)

    @pl.when((image == 0) & (i == 0))
    def _():
        taps_acc_ref[...] = jnp.zeros_like(taps_acc_ref)

    @pl.when(i == 0)
    def _():
        dmod_ref[...] = jnp.zeros_like(dmod_ref)
        pad_ref[0:GRID, :] = top_ref[...]
        pad_ref[pl.ds(length + GRID, GRID), :] = bot_ref[...]
        pad_ref[pl.ds(GRID, length), :] = dconv_ref[...]

    scale = 1.0 + mod_ref[1:2, :]

    def eights(x):
        return jnp.sum(x.reshape(x.shape[0] // 8, 8, WIDTH), axis=0)

    start = pl.multiple_of(i * TILE, TILE)
    rows = [pad_ref[pl.ds(start + (2 - a) * GRID, TILE), :] for a in range(3)]
    parts = [
        sum(taps_ref[3 * a + b : 3 * a + b + 1, :] * rows[a] for a in range(3))
        for b in range(3)
    ]
    dn = (
        shifted(parts[0], -1)
        + parts[1]
        + shifted(parts[2], 1)
        + dnorm_ref[...]
    )
    hat, rate = normalized(tok_ref[...])
    grad_ref[...] = dmid_ref[...] + normal_back(
        dn * scale, hat, rate
    )
    dmod_ref[0:1, :] += jnp.sum(dn, axis=0, keepdims=True)
    dmod_ref[1:2, :] += jnp.sum(dn * hat, axis=0, keepdims=True)
    own = rows[1]
    moved = [shifted(own, -1), own, shifted(own, 1)]
    for a in range(3):
        near = normed_ref[pl.ds(start + a * GRID, TILE), :]
        for b in range(3):
            taps_acc_ref[3 * a + b] += eights(moved[b] * near)

    @pl.when((image == pl.num_programs(0) - 1) & (i == pl.num_programs(1) - 1))
    def _():
        dtaps_ref[...] = jnp.zeros_like(dtaps_ref)
        for t in range(9):
            dtaps_ref[t : t + 1, :] = jnp.sum(taps_acc_ref[t], axis=0, keepdims=True)


def call(kernel, grid, ins, outs, scratch, flops=0, moved=0, prefetch=0, limit=60):
    return pl.pallas_call(
        kernel,
        grid_spec=pltpu.PrefetchScalarGridSpec(
            num_scalar_prefetch=prefetch,
            grid=grid,
            in_specs=ins,
            out_specs=[spec for spec, _ in outs],
            scratch_shapes=scratch,
        ),
        out_shape=[jax.ShapeDtypeStruct(shape, F32) for _, shape in outs],
        compiler_params=pltpu.CompilerParams(vmem_limit_bytes=limit * 1024 * 1024),
        cost_estimate=pl.CostEstimate(flops=1, bytes_accessed=1, transcendentals=0),
    )


def whole(shape):
    zeros = (0,) * len(shape)
    return pl.BlockSpec(shape, lambda *_: zeros, pipeline_mode=pl.Buffered(1))


def per_image(shape):
    zeros = (0,) * len(shape)
    return pl.BlockSpec((None,) + shape, lambda n, *_: (n,) + zeros)


def time_features(timesteps):
    half = FREQ // 2
    freqs = jnp.exp(-math.log(10000.0) * jnp.arange(half, dtype=F32) / half)
    angles = timesteps.astype(F32)[:, None] * freqs[None, :]
    return jnp.concatenate([jnp.cos(angles), jnp.sin(angles)], axis=1)


def halves(axis):
    return [1 << b for b in range(lax.axis_size(axis).bit_length() - 1)]


def swapped(x, axis, bit):
    return lax.ppermute(x, axis, [(i, i ^ bit) for i in range(lax.axis_size(axis))])


def is_high(axis, bit):
    return (lax.axis_index(axis) // bit) % 2


def fold_kernel(links, *refs):
    ins, outs = refs[: 2 * len(links)], list(refs[2 * len(links) :])
    for n, link in enumerate(links):
        keep, got = ins[2 * n], ins[2 * n + 1]
        if link is None:
            outs.pop(0)[...] = keep[...] + got[...]
            continue
        half = keep.shape[0] // 2
        high = is_high(*link)
        for side in (1 - high, high):
            start = side * half
            at = pl.ds(pl.multiple_of(start, 8) if half % 8 == 0 else start, half)
            outs.pop(0)[...] = keep[at, :] + got[at, :]


def fold(flows):
    links = [flow.order[0] if flow.order else None for flow in flows]
    if any(flow.keep.shape[0] % 16 and flow.order for flow in flows):
        for flow, link in zip(flows, links):
            total = flow.keep + flow.got
            if link is None:
                flow.keep = total
            else:
                flow.halve(total)
        return
    shapes = []
    for flow, link in zip(flows, links):
        rows = flow.keep.shape[0]
        shapes += [(rows, WIDTH)] if link is None else [(rows // 2, WIDTH)] * 2
    outs = call(
        functools.partial(fold_kernel, links),
        (1,),
        [whole(x.shape) for flow in flows for x in (flow.keep, flow.got)],
        [(whole(shape), shape) for shape in shapes],
        [],
        limit=32,
    )(*(x for flow in flows for x in (flow.keep, flow.got)))
    outs = list(outs)
    for flow, link in zip(flows, links):
        if link is None:
            flow.keep = outs.pop(0)
        else:
            flow.sent, flow.keep = outs.pop(0), outs.pop(0)


class Flow:
    def __init__(self, x, order):
        self.order, self.used = list(order), []
        self.halve(x)

    def halve(self, x):
        half = x.shape[0] // 2
        high = is_high(*self.order[0])
        self.sent = lax.dynamic_slice_in_dim(x, (1 - high) * half, half)
        self.keep = lax.dynamic_slice_in_dim(x, high * half, half)

    def busy(self):
        return bool(self.order)

    def send(self):
        return self.sent

    def link(self):
        return self.order[0]

    def take(self, got):
        self.got = got
        self.used.append(self.order.pop(0))


class Spread:
    def __init__(self, x, used):
        self.x, self.used = x[None], list(used)

    def busy(self):
        return bool(self.used)

    def send(self):
        return self.x

    def link(self):
        return self.used[-1]

    def take(self, got):
        high = is_high(*self.used.pop())
        pair = jnp.concatenate([got, self.x]), jnp.concatenate([self.x, got])
        self.x = jnp.where(high == 1, *pair)


class Whole:
    def __init__(self, arrays, link):
        self.arrays, self.at = arrays, link
        self.total = None

    def halves(self, high):
        return [
            lax.dynamic_slice_in_dim(x, high * (x.shape[0] // 2), x.shape[0] // 2)
            for x in self.arrays
        ]

    def busy(self):
        return self.total is None

    def send(self):
        return jnp.concatenate(self.halves(1 - is_high(*self.at)))

    def link(self):
        return self.at

    def take(self, got):
        self.total = jnp.concatenate(self.halves(is_high(*self.at))) + got


class Rows:
    def __init__(self, x, sums, joins):
        self.x, self.sums, self.joins = x, list(sums), list(joins)

    def busy(self):
        return bool(self.sums or self.joins)

    def send(self):
        return self.x

    def link(self):
        return self.sums[0] if self.sums else self.joins[0]

    def take(self, got):
        axis, bit = self.link()
        if self.sums:
            self.sums.pop(0)
            self.x = self.x + got
            return
        self.joins.pop(0)
        high = (lax.axis_index(axis) // bit) % 2
        pair = [jnp.concatenate(p, axis=1) for p in ((got, self.x), (self.x, got))]
        self.x = jnp.where(high == 1, *pair)


def beside(flows, first, kernel):
    flows = [flow for flow in flows if flow.busy()]
    first, *sends = lax.optimization_barrier((first, *(flow.send() for flow in flows)))
    got = [swapped(x, *flow.link()) for flow, x in zip(flows, sends)]
    outs = kernel(first)
    head, *got = lax.optimization_barrier((outs[0], *got))
    for flow, x in zip(flows, got):
        flow.take(x)
    folding = [flow for flow in flows if isinstance(flow, Flow)]
    if folding:
        fold(folding)
    return [head] + list(outs[1:])


def swap_two(outs):
    return [outs[1], outs[0]] + list(outs[2:])


def move_first(outs):
    return list(outs[1:]) + [outs[0]]


def messages(message, backward):
    size = lax.axis_size("seq")
    got = []
    for far in range(1, size):
        pairs = [(i, i + far) for i in range(size - far)]
        if backward:
            pairs = [(j, i) for i, j in pairs]
        got.append(lax.ppermute(message, "seq", pairs))
    return got


def body(
    tokens,
    valid_mask,
    timesteps,
    class_ids,
    time_first,
    time_second,
    class_table,
    ada_weight,
    ada_bias,
    conv_taps,
    query_proj,
    key_proj,
    value_proj,
    decay_down,
    decay_up,
    decay_bias,
    gate_proj,
    out_proj,
    mlp_up,
    mlp_down,
    cotangent,
):
    count, length, width = tokens.shape
    size, mine = lax.axis_size("seq"), lax.axis_index("seq")
    tiles, chunks = length // TILE, length // CHUNK
    per_tile = TILE // CHUNK
    up_pairs = [(i, i + 1) for i in range(size - 1)]
    down_pairs = [(j, i) for i, j in up_pairs]
    seq_bits = [("seq", bit) for bit in halves("seq")]
    img_bits = [("img", bit) for bit in halves("img")]
    core, order_a = seq_bits[0], seq_bits[1:] + img_bits
    order_b = img_bits[:2] + seq_bits[1:] + img_bits[2:]

    def borders(x):
        return (
            lax.ppermute(x[:, length - GRID :], "seq", up_pairs),
            lax.ppermute(x[:, :GRID], "seq", down_pairs),
        )

    above, below = borders(tokens)

    square = (width, width)
    row = (length, width)
    dense = 2 * 3 * count * length * width
    each = 4 * count * length * width
    features = time_features(timesteps)
    mod_spec = per_image((6, width))
    modul, info = call(
        condition_kernel,
        (count,),
        [
            per_image((1, FREQ)),
            whole(time_first.shape),
            whole(time_second.shape),
            pl.BlockSpec((8, width), lambda n, ids: (ids[n] // 8, 0)),
            whole(ada_weight.shape),
            whole((6 * width,)),
        ],
        [
            (mod_spec, (count, 6, width)),
            (per_image((8, width)), (count, 8, width)),
        ],
        [],
        flops=1000000,
        moved=4 * 6 * width * width,
        prefetch=1,
    )(class_ids, features[:, None], time_first, time_second, class_table, ada_weight, ada_bias)

    valid = valid_mask[:, None]
    valid_spec = per_image((1, length))
    message_shape = (PAIRS, HEAD_DIM + 8, LANES)
    def tiled(shape=(TILE, width)):
        return pl.BlockSpec((None,) + shape, lambda n, i: (n, i, 0))

    tile_row = (tiled(), (count,) + row)
    pair_spec = pl.BlockSpec(
        (None, per_tile, PAIRS, LANES, LANES), lambda n, i: (n, i, 0, 0, 0)
    )
    state_spec = pl.BlockSpec((None, PAIRS, LANES, LANES), lambda n, i: (n, 0, 0, 0))
    state_shape = (count, PAIRS, LANES, LANES)
    score_shape = (count, chunks, PAIRS, 2 * CHUNK, CHUNK)
    score_spec = pl.BlockSpec(
        (None, per_tile, PAIRS, 2 * CHUNK, CHUNK), lambda n, i: (n, i, 0, 0, 0)
    )
    normed_spec = per_image((length + 2 * GRID, width))
    message_spec = per_image(message_shape)
    fade_spec = pl.BlockSpec((None, per_tile, 8, width), lambda n, i: (n, i, 0, 0))
    (
        weights,
        normed,
        conv,
        query,
        keys,
        values,
        cumul,
        slope,
        far,
        states,
        fades,
        message,
    ) = call(
        front_kernel,
        (count, tiles),
        [
            per_image(row),
            per_image((GRID, width)),
            per_image((GRID, width)),
            valid_spec,
            mod_spec,
            whole((9, width)),
            whole(square),
            whole(square),
            whole(square),
            whole(decay_up.shape),
            whole(decay_up.shape),
            whole((width,)),
        ],
        [
            (whole((width, 4 * width)), (width, 4 * width)),
            (per_image((length + 2 * GRID, width)), (count, length + 2 * GRID, width)),
        ]
        + [tile_row] * 7
        + [
            (pair_spec, (count, chunks, PAIRS, LANES, LANES)),
            (fade_spec, (count, chunks, 8, width)),
            (message_spec, (count,) + message_shape),
        ],
        [
            pltpu.VMEM((6 * width, 4 * width), BF16),
            pltpu.VMEM((TILE, 4 * width), F32),
            pltpu.VMEM((PAIRS, LANES, LANES), F32),
            pltpu.VMEM((8, width), F32),
        ],
        flops=dense * 4 * width,
        moved=each * 10,
    )(
        tokens,
        above,
        below,
        valid,
        modul,
        conv_taps,
        query_proj,
        key_proj,
        value_proj,
        decay_down.T,
        decay_up,
        decay_bias,
    )

    forward_parts = messages(message, False)
    inner, scores, gate_in = call(
        inner_kernel,
        (count, tiles),
        [tiled()] * 4 + [pair_spec, normed_spec, whole(square)],
        [tile_row, (score_spec, score_shape), tile_row],
        [pltpu.VMEM((3 * width, width), BF16), pltpu.VMEM((PAIRS, 2 * CHUNK, CHUNK), F32)],
        flops=dense * 2 * width,
        moved=each * 9,
    )(query, keys, values, cumul, states, normed, gate_proj)

    middle, branch, attended, state_in = call(
        mix_kernel,
        (count, tiles),
        [tiled()] * 4 + [mod_spec, whole(square)] + [message_spec] * (size - 1),
        [tile_row] * 3 + [(state_spec, state_shape)],
        [pltpu.VMEM((3 * width, width), BF16)],
        flops=dense * 2 * width,
        moved=each * 7,
    )(inner, far, tokens, gate_in, modul, out_proj, *forward_parts)

    dmod_spec = per_image((8, width))
    dmod_out = (dmod_spec, (count, 8, width))

    def feed_forward(part, last, *partial):
        return call(
            functools.partial(mlp_kernel, last),
            (count, tiles),
            [
                tiled(),
                tiled(),
                mod_spec,
                pl.BlockSpec((width, BLOCK), lambda n, i: (0, part), pipeline_mode=pl.Buffered(1)),
                pl.BlockSpec((BLOCK, width), lambda n, i: (part, 0), pipeline_mode=pl.Buffered(1)),
            ]
            + [tiled()] * len(partial),
            [tile_row] * 2
            + ([dmod_out] if last else [])
            + [(whole((2 * BLOCK, width)), (2 * BLOCK, width))],
            [
                pltpu.VMEM((3 * width, BLOCK), BF16),
                pltpu.VMEM((2 * width, BLOCK), BF16),
                pltpu.VMEM((2 * BLOCK, width), BF16),
                pltpu.VMEM((BLOCK, 3 * width), BF16),
                pltpu.VMEM((width, BLOCK), F32),
                pltpu.VMEM((width, BLOCK), F32),
            ],
            flops=dense * 6 * BLOCK,
            moved=each * 6,
        )(middle, cotangent, modul, mlp_up, mlp_down, *partial)

    mlp_part, dsec_part, g_mlp_a = feed_forward(0, False)
    block_out, dmid, dmod_mlp, g_mlp_b = feed_forward(1, True, mlp_part, dsec_part)

    datt, dnorm, g_mix, dmod_mix, d_message = call(
        mix_back_kernel,
        (count, tiles),
        [tiled()] * 5
        + [normed_spec, mod_spec, message_spec, whole(square), whole(square)],
        [tile_row] * 2
        + [(whole((2 * width, width)), (2 * width, width)), dmod_out]
        + [(message_spec, (count,) + message_shape)],
        [
            pltpu.VMEM((width, 3 * width), BF16),
            pltpu.VMEM((width, 3 * width), BF16),
            pltpu.VMEM((PAIRS, LANES, LANES), F32),
        ],
        flops=dense * 5 * width,
        moved=each * 8,
    )(dmid, branch, attended, gate_in, far, normed, modul, message, out_proj, gate_proj)
    first = Whole([g_mlp_a, g_mlp_b, g_mix], core)
    (datt,) = beside([first], datt, lambda x: [x])
    cut = 1024
    early = [Flow(first.total[:cut], order_a), Flow(first.total[cut:], order_b)]
    d_message, datt = lax.optimization_barrier((d_message, datt))
    backward_parts = messages(d_message, True)

    dquery, dkeys, dvalues, full = beside(early, datt, lambda x: call(
        inner_back_kernel,
        (count, tiles),
        [tiled()] * 5 + [score_spec, pair_spec, fade_spec, state_spec],
        [tile_row] * 3 + [(pair_spec, (count, chunks, PAIRS, LANES, LANES))],
        [
            pltpu.VMEM((PAIRS, 2 * CHUNK, CHUNK), F32),
            pltpu.VMEM((CHUNK, width), F32),
            pltpu.VMEM((CHUNK, width), F32),
        ],
        flops=dense * 2 * width,
        moved=each * 12,
    )(query, keys, values, cumul, x, scores, states, fades, state_in))

    def turned(shape=(TILE, width)):
        return pl.BlockSpec((None,) + shape, lambda n, i: (n, tiles - 1 - i, 0))

    dconv, dproj, dbias = beside(early, dquery, lambda x: swap_two(call(
        state_back_kernel,
        (count, tiles),
        [valid_spec]
        + [turned()] * 10
        + [
            pl.BlockSpec(
                (None, per_tile, PAIRS, LANES, LANES),
                lambda n, i: (n, tiles - 1 - i, 0, 0, 0),
            ),
            whole((width, 4 * width)),
        ]
        + [message_spec] * (size - 1),
        [
            (turned((TILE, 4 * width)), (count, length, 4 * width)),
            (turned(), (count,) + row),
            (whole((8, width)), (8, width)),
        ],
        [
            pltpu.VMEM((width, 3 * 4 * width), BF16),
            pltpu.VMEM((PAIRS, LANES, LANES), F32),
        ],
        flops=dense * 5 * width,
        moved=each * 16,
    )(
        valid,
        query,
        keys,
        values,
        cumul,
        slope,
        conv,
        datt,
        x,
        dkeys,
        dvalues,
        full,
        weights,
        *backward_parts,
    )))

    d_above, d_below = borders(dconv)
    (g_proj,) = beside(early, dproj, lambda x: call(
        weight_kernel,
        (count, tiles),
        [
            tiled(),
            tiled((TILE, 4 * width)),
            whole((8, width)),
            whole(decay_up.shape),
            whole(decay_up.shape),
        ],
        [(whole((ROWS, width)), (ROWS, width))],
        [pltpu.VMEM((width, 4 * width), F32)],
        flops=dense * 4 * width,
        moved=each * 7,
    )(conv, x, dbias, decay_down.T, decay_up))
    second = Whole([g_proj], core)
    (dconv,) = beside([second], dconv, lambda x: [x])
    late_cut = 384
    late = [Flow(second.total[:late_cut], order_a), Flow(second.total[late_cut:], order_b)]

    dmod_front, dtaps, tokens_grad = beside(early + late, dconv, lambda x: move_first(call(
        front_back_kernel,
        (count, tiles),
        [
            tiled(),
            per_image((length + 2 * GRID, width)),
            per_image(row),
            per_image((GRID, width)),
            per_image((GRID, width)),
            tiled(),
            tiled(),
            mod_spec,
            whole((9, width)),
        ],
        [
            tile_row,
            dmod_out,
            (whole((16, width)), (16, width)),
        ],
        [
            pltpu.VMEM((length + 2 * GRID, width), F32),
            pltpu.VMEM((9, 8, width), F32),
        ],
        flops=count * length * width * 100,
        moved=each * 6,
    )(tokens, normed, x, d_above, d_below, dnorm, dmid, modul, conv_taps)))

    dmod = (dmod_front + dmod_mlp + dmod_mix)[:, :6]
    own = jnp.where(mine == 0, info[:, :3], 0.0)
    ids = jnp.where(mine == 0, class_ids, 0).astype(F32)[:, None, None]
    ids = jnp.broadcast_to(ids, (count, 1, width))
    rows = jnp.moveaxis(jnp.concatenate([dmod, own, ids], axis=1), 1, 0)
    taps = jnp.concatenate([dtaps[:9, None], jnp.zeros((9, count - 1, width), F32)], axis=1)
    flow_r = Rows(jnp.concatenate([rows, taps]), seq_bits, img_bits)
    none = jnp.zeros((), F32)
    while any(flow.busy() for flow in early + late):
        beside([flow_r] + early + late, none, lambda x: [x])
    spread_a, spread_b = (
        Spread(jnp.concatenate([one.keep, two.keep]), one.used) for one, two in zip(early, late)
    )
    while flow_r.busy():
        beside([flow_r, spread_a, spread_b], none, lambda x: [x])
    rows, taps = flow_r.x[:10], jnp.sum(flow_r.x[10:], axis=1)
    images = rows.shape[1]
    ids = rows[9, :, 0].astype(jnp.int32)
    g_first, g_second, g_class, g_ada, g_ada_bias = beside([spread_a, spread_b], rows, lambda x: call(
        embed_kernel,
        (1,),
        [
            whole(rows.shape),
            whole(ada_weight.shape),
            whole(time_second.shape),
        ],
        [
            (whole(shape), shape)
            for shape in (
                time_first.shape,
                time_second.shape,
                class_table.shape,
                ada_weight.shape,
                (1, 6 * width),
            )
        ],
        [],
        flops=images * 2 * 3 * width * width * 14,
        moved=4 * width * width * 20,
        prefetch=1,
    )(ids, x, ada_weight, time_second))
    while spread_a.busy() or spread_b.busy():
        beside([spread_a, spread_b], none, lambda x: [x])
    mine_a, mine_b = spread_a.x, spread_b.x
    other_a, other_b = (swapped(x, *core) for x in (mine_a, mine_b))
    high = is_high(*core)

    def unpacked(x, y):
        rows_a, rows_b = early[0].keep.shape[0], early[1].keep.shape[0]
        flat = [
            part.reshape(-1, width)
            for part in (x[:, :rows_a], y[:, :rows_b], x[:, rows_a:], y[:, rows_b:])
        ]
        return jnp.concatenate(flat[:2]), jnp.concatenate(flat[2:])

    lower = unpacked(jnp.where(high == 0, mine_a, other_a), jnp.where(high == 0, mine_b, other_b))
    upper = unpacked(jnp.where(high == 0, other_a, mine_a), jnp.where(high == 0, other_b, mine_b))

    def pieces(index, start, rows):
        half = rows // 2
        at = slice(start // 2, start // 2 + half)
        return jnp.concatenate([lower[index][at], upper[index][at]])

    mlp_rows = 2 * BLOCK
    g_mlp_a = pieces(0, 0, mlp_rows)
    g_mlp_b = pieces(0, mlp_rows, mlp_rows)
    g_mix = pieces(0, 2 * mlp_rows, 2 * width)
    g_proj = pieces(1, 0, ROWS)

    rank = decay_up.shape[0]
    base = 3 * width
    hidden_rows = 2 * BLOCK

    def joined(first, second):
        return jnp.concatenate(
            [part[j * width : (j + 1) * width] for part in (first, second) for j in range(BLOCK // width)],
            axis=1,
        )

    return (
        block_out,
        tokens_grad,
        g_first,
        g_second,
        g_class,
        g_ada,
        g_ada_bias[0],
        taps,
        g_proj[:width],
        g_proj[width : 2 * width],
        g_proj[2 * width : base],
        g_proj[base : base + rank].T,
        g_proj[base + rank : base + 2 * rank],
        g_proj[base + 2 * rank],
        g_mix[width:],
        g_mix[:width],
        joined(g_mlp_a, g_mlp_b),
        jnp.concatenate([g_mlp_a[BLOCK:], g_mlp_b[BLOCK:hidden_rows]]),
    )


def solution(mesh):
    image, shared = P("img", "seq", None), P()
    return jax.shard_map(
        body,
        mesh=mesh,
        in_specs=(image, P("img", "seq"), P("img"), P("img")) + (shared,) * 16 + (image,),
        out_specs=(image, image) + (shared,) * 16,
        check_vma=False,
    )
```

```python
import functools
import math

import jax
import jax.numpy as jnp
from jax import lax
from jax.experimental import pallas as pl
from jax.experimental.pallas import tpu as pltpu
from jax.sharding import PartitionSpec as P

HEADS = 6
HEAD_DIM = 64
CLASSES = 1000
FREQ = 256
GRID = 64
WIDTH = 384
PAIRS = 3
LANES = 128
CHUNK = 128
TILE = 256
ROWS = 1280
SMALL = 48
SPAN = 120.0
HIGH = lax.Precision.HIGHEST
F32 = jnp.float32
BF16 = jnp.bfloat16
GELU_C = math.sqrt(2.0 / math.pi)


def product(left, right):
    return jnp.dot(left, right, precision=HIGH, preferred_element_type=F32)


def dot(a, b, ca=1, cb=0):
    return lax.dot_general(a, b, (((ca,), (cb,)), ((), ())), preferred_element_type=F32)


def split(x):
    high = x.astype(BF16)
    return high, (x - high.astype(F32)).astype(BF16)


def mm3(a, b, ca=1, cb=0):
    return dot(a[0], b[0], ca, cb) + dot(a[1], b[0], ca, cb) + dot(a[0], b[1], ca, cb)


def split3(x):
    high = x.astype(BF16)
    rest = x - high.astype(F32)
    middle = rest.astype(BF16)
    return high, middle, (rest - middle.astype(F32)).astype(BF16)


def mm6(a, b, ca=1, cb=0):
    terms = ((0, 0), (0, 1), (1, 0), (1, 1), (0, 2), (2, 0))
    return sum(dot(a[i], b[j], ca, cb) for i, j in reversed(terms))


def wide6(x):
    h, m, l = split3(x)
    return jnp.concatenate([h, h, m, m, h, l], axis=1)


def tall6(w):
    h, m, l = split3(w)
    return jnp.concatenate([h, m, h, m, l, h], axis=0)


def wide3(x):
    high, low = split(x)
    return jnp.concatenate([high, high, low], axis=1)


def wide(x):
    high, low = split(x)
    return jnp.concatenate([high, low, high], axis=1)


def tall(w):
    high, low = split(w)
    return jnp.concatenate([high, high, low], axis=0)


def across(w):
    high, low = split(w)
    return jnp.concatenate([high, high, low], axis=1)


def lanes(x, p):
    return x[..., p * LANES : (p + 1) * LANES]


def first_half(shape):
    return lax.broadcasted_iota(jnp.int32, shape, len(shape) - 1) < HEAD_DIM


def block_diagonal(square):
    rows = lax.broadcasted_iota(jnp.int32, square.shape, 0) < HEAD_DIM
    return jnp.where(rows == first_half(square.shape), square, 0.0)


def head_mean(x):
    rows = lax.broadcasted_iota(jnp.int32, (LANES, LANES), 0) < HEAD_DIM
    ones = jnp.where(rows == first_half((LANES, LANES)), 1.0 / HEAD_DIM, 0.0).astype(BF16)
    high, low = split(x)
    return dot(
        jnp.concatenate([high, low], axis=1), jnp.concatenate([ones, ones], axis=0)
    )


def head_means(x):
    return jnp.concatenate([head_mean(lanes(x, p)) for p in range(PAIRS)], axis=1)


def stacked_heads(x):
    keep = first_half(x.shape)
    zero = jnp.zeros_like(x)
    return jnp.concatenate([jnp.where(keep, x, zero), jnp.where(keep, zero, x)], axis=0)


def merged_heads(x):
    rows = x.shape[0] // 2
    return jnp.where(first_half((rows, LANES)), x[:rows], x[rows:])


def sigmoid(x):
    return 1.0 / (1.0 + jnp.exp(-x))


def shifted(x, step):
    rows = x.shape[0]
    column = lax.broadcasted_iota(jnp.int32, x.shape, 0) % GRID
    if step == 1:
        return jnp.where(column == 0, 0.0, pltpu.roll(x, 1, 0))
    return jnp.where(column == GRID - 1, 0.0, pltpu.roll(x, rows - 1, 0))


def normalized(x):
    center = x - jnp.mean(x, axis=-1, keepdims=True)
    rate = lax.rsqrt(jnp.mean(center * center, axis=-1, keepdims=True) + 1e-06)
    return center * rate, rate


def normal_back(dhat, hat, rate):
    return rate * (
        dhat
        - jnp.mean(dhat, axis=-1, keepdims=True)
        - hat * jnp.mean(dhat * hat, axis=-1, keepdims=True)
    )


def triangle(size, upper):
    rows = lax.broadcasted_iota(jnp.int32, (size, size), 0)
    cols = lax.broadcasted_iota(jnp.int32, (size, size), 1)
    return jnp.where(cols >= rows if upper else cols <= rows, 1.0, 0.0).astype(BF16)


def running_sum(x, upper):
    tri = triangle(x.shape[0], upper)
    high = x.astype(BF16)
    rest = x - high.astype(F32)
    middle = rest.astype(BF16)
    low = (rest - middle.astype(F32)).astype(BF16)
    return dot(tri, high) + dot(tri, middle) + dot(tri, low)


def opening(tile):
    return (lax.axis_index("seq") == 0) & (tile == 0)


def spread(compact):
    keep = first_half(compact.shape)
    return jnp.concatenate(
        [jnp.where(keep, compact, 0.0), jnp.where(keep, 0.0, compact)], axis=0
    )


def linked(parts, p):
    total = jnp.zeros((HEAD_DIM, LANES), F32)
    for part in reversed(parts):
        total = part[p, 0:HEAD_DIM, :] + part[p, HEAD_DIM : HEAD_DIM + 1, :] * total
    return spread(total)


def as_column(row):
    return jnp.broadcast_to(row, (8, row.shape[1])).T[:, 0:1]


def applied(row, w_ref):
    return jnp.sum(as_column(row) * w_ref[...], axis=0, keepdims=True)


def condition_kernel(ids_ref, feat_ref, first_w_ref, second_w_ref, row_ref, ada_ref, bias_ref, mod_ref, info_ref):
    features = feat_ref[...]
    first = applied(features, first_w_ref)
    embed = applied(first * sigmoid(first), second_w_ref)
    at = lax.broadcasted_iota(jnp.int32, row_ref.shape, 0) == ids_ref[pl.program_id(0)] % 8
    embed = embed + jnp.sum(jnp.where(at, row_ref[...], 0.0), axis=0, keepdims=True)
    modul = applied(embed * sigmoid(embed), ada_ref)
    for j in range(6):
        at = slice(j * WIDTH, (j + 1) * WIDTH)
        mod_ref[j : j + 1, :] = modul[:, at] + bias_ref[at][None, :]
    info_ref[...] = jnp.zeros_like(info_ref)
    info_ref[0:1, 0:FREQ] = features
    info_ref[1:2, :] = first
    info_ref[2:3, :] = embed


def embed_kernel(
    ids_ref, rows_ref, ada_ref, second_ref, gf_ref, gs_ref, gc_ref, ga_ref, gb_ref, gt_ref
):
    images = rows_ref.shape[0]
    features, first, embed = rows_ref[:, 6, 0:FREQ], rows_ref[:, 7, :], rows_ref[:, 8, :]
    gt_ref[...] = jnp.sum(rows_ref[:, 10:19, :], axis=0)

    def silu_back(x, grad):
        sig = sigmoid(x)
        return grad * (sig * (1.0 + x * (1.0 - sig)))

    act = split((embed * sigmoid(embed)).T)
    dembed = jnp.zeros((images, WIDTH), F32)
    for j in range(6):
        at = slice(j * WIDTH, (j + 1) * WIDTH)
        grad = rows_ref[:, j, :]
        dmod = split(grad)
        ga_ref[:, at] = mm3(act, dmod)
        gb_ref[:, at] = jnp.sum(grad, axis=0, keepdims=True)
        dembed = dembed + mm3(dmod, split(ada_ref[:, at]), 1, 1)
    dembed = silu_back(embed, dembed)
    gc_ref[...] = jnp.zeros_like(gc_ref)

    def put(n, carry):
        mine = lax.broadcasted_iota(jnp.int32, (images, WIDTH), 0) == n
        row = jnp.sum(jnp.where(mine, dembed, 0.0), axis=0, keepdims=True)
        gc_ref[pl.ds(ids_ref[n], 1), :] += row
        return carry

    lax.fori_loop(0, images, put, 0)
    de = split(dembed)
    gs_ref[...] = mm3(split((first * sigmoid(first)).T), de)
    dfirst = silu_back(first, mm3(de, split(second_ref[...]), 1, 1))
    gf_ref[...] = mm3(split(features.T), split(dfirst))


def front_kernel(
    tok_ref,
    top_ref,
    bot_ref,
    valid_ref,
    mod_ref,
    taps_ref,
    wq_ref,
    wk_ref,
    wv_ref,
    down_ref,
    up_ref,
    bias_ref,
    w_ref,
    normed_ref,
    conv_ref,
    q_ref,
    k_ref,
    v_ref,
    cum_ref,
    slope_ref,
    far_ref,
    state_ref,
    fade_ref,
    out_ref,
    w3_ref,
    proj_ref,
    st_ref,
    dev_ref,
):
    image, i = pl.program_id(0), pl.program_id(1)
    length = tok_ref.shape[0]

    @pl.when((image == 0) & (i == 0))
    def _():
        w_ref[:, 0:WIDTH] = wq_ref[...] * HEAD_DIM ** (-0.5)
        w_ref[:, WIDTH : 2 * WIDTH] = wk_ref[...]
        w_ref[:, 2 * WIDTH : 3 * WIDTH] = wv_ref[...]
        w_ref[:, 3 * WIDTH :] = mm6(split3(down_ref[...]), split3(up_ref[...]), 0, 0)
        w3_ref[...] = tall6(w_ref[...])

    real = jnp.sum(valid_ref[...], axis=1, keepdims=True)
    shift = mod_ref[0:1, :]
    scale = 1.0 + mod_ref[1:2, :]

    def modulated(x):
        return normalized(x)[0] * scale + shift

    @pl.when(i == 0)
    def _():
        normed_ref[0:GRID, :] = jnp.where(
            lax.axis_index("seq") == 0, 0.0, modulated(top_ref[...])
        )
        normed_ref[pl.ds(length + GRID, GRID), :] = jnp.where(
            lax.axis_index("seq") == lax.axis_size("seq") - 1, 0.0, modulated(bot_ref[...])
        )
        for at in range(0, length, TILE):
            normed_ref[GRID + at : GRID + at + TILE, :] = modulated(tok_ref[at : at + TILE, :])
        st_ref[...] = jnp.zeros_like(st_ref)
        dev_ref[...] = jnp.zeros_like(dev_ref)

    start = pl.multiple_of(i * TILE, TILE)
    rows = [normed_ref[pl.ds(start + a * GRID, TILE), :] for a in range(3)]
    parts = [
        sum(taps_ref[3 * a + b : 3 * a + b + 1, :] * rows[a] for a in range(3))
        for b in range(3)
    ]
    conv = shifted(parts[0], 1) + parts[1] + shifted(parts[2], -1)
    conv_ref[...] = conv
    hidden = conv * sigmoid(conv)
    first = opening(i)

    @pl.when(first)
    def _():
        proj_ref[...] = dot(wide6(hidden), w3_ref[...])

    @pl.when(jnp.logical_not(first))
    def _():
        proj_ref[...] = dot(wide3(hidden), w3_ref[0 : 3 * WIDTH, :])

    proj = proj_ref[...]
    keep = (
        lax.broadcasted_iota(jnp.int32, (TILE, WIDTH), 0) + start < real
    )
    q = proj[:, :WIDTH]
    k = jnp.where(keep, proj[:, WIDTH : 2 * WIDTH], 0.0)
    v = jnp.where(keep, proj[:, 2 * WIDTH : 3 * WIDTH], 0.0)
    x = proj[:, 3 * WIDTH :] + bias_ref[...][None, :]
    small = jnp.exp(-jnp.abs(x))
    gates = jnp.where(keep, (jnp.minimum(x, 0.0) - jnp.log1p(small)) * (1.0 / 16.0), 0.0)
    slope = jnp.where(x >= 0, small, 1.0) / (1.0 + small)
    slope_ref[...] = jnp.where(keep, slope * (1.0 / 16.0), 0.0)
    q_ref[...] = q
    k_ref[...] = k
    v_ref[...] = v
    for c in range(TILE // CHUNK):
        at = slice(c * CHUNK, (c + 1) * CHUNK)
        cum = running_sum(gates[at], False)
        cum_ref[at, :] = cum
        final = cum[CHUNK - 1 : CHUNK, :]
        dev = dev_ref[0:1, :]
        far_ref[at, :] = q[at] * jnp.exp(cum + dev)
        fade_ref[c] = jnp.broadcast_to(jnp.exp(dev), (8, WIDTH))
        kd = k[at] * jnp.exp(final - cum)
        factor = jnp.exp(final)
        for p in range(PAIRS):
            state_ref[c, p] = st_ref[p]
            update = mm3(split(lanes(v[at], p)), split(lanes(kd, p)), 0, 0)
            st_ref[p] = lanes(factor, p) * st_ref[p] + block_diagonal(update)
        dev_ref[...] = dev_ref[...] + final

    @pl.when(i == pl.num_programs(1) - 1)
    def _():
        for p in range(PAIRS):
            out_ref[p, 0:HEAD_DIM, :] = st_ref[p, 0:HEAD_DIM, :] + st_ref[p, HEAD_DIM:, :]
            out_ref[p, HEAD_DIM:, :] = jnp.exp(lanes(dev_ref[...], p))


def exact_scores(q_ref, k_ref, cum_ref, base, s_ref):
    q = q_ref[pl.ds(base, CHUNK), :]
    cum = cum_ref[pl.ds(base, CHUNK), :]
    s_ref[...] = jnp.zeros_like(s_ref)

    def step(j, carry):
        key = k_ref[pl.ds(base + j, 1), :]
        weight = jnp.exp(jnp.minimum(cum - cum_ref[pl.ds(base + j, 1), :], 0.0))
        terms = q * key * weight
        for p in range(PAIRS):
            column = jnp.sum(stacked_heads(lanes(terms, p)), axis=1, keepdims=True)
            at = lax.broadcasted_iota(jnp.int32, (2 * CHUNK, CHUNK), 1) == j
            s_ref[p] = jnp.where(at, column, s_ref[p])
        return carry

    lax.fori_loop(0, CHUNK, step, 0)


def causal_two():
    rows = lax.broadcasted_iota(jnp.int32, (2 * CHUNK, CHUNK), 0) % CHUNK
    return rows >= lax.broadcasted_iota(jnp.int32, (2 * CHUNK, CHUNK), 1)


def inner_kernel(
    q_ref, k_ref, v_ref, cum_ref, state_ref, normed_ref, gate_ref, o_ref, s_ref, gp_ref, w3_ref, tmp_ref
):
    @pl.when((pl.program_id(0) == 0) & (pl.program_id(1) == 0))
    def _():
        w3_ref[...] = tall(gate_ref[...])

    start = pl.multiple_of(pl.program_id(1) * TILE + GRID, GRID)
    gp_ref[...] = dot(wide(normed_ref[pl.ds(start, TILE), :]), w3_ref[...])
    mask = causal_two()
    for c in range(TILE // CHUNK):
        base = c * CHUNK
        at = slice(base, base + CHUNK)
        q = q_ref[at, :]
        k = k_ref[at, :]
        cum = cum_ref[at, :]
        final = cum[CHUNK - 1 : CHUNK, :]
        wild = jnp.max(-final) > SPAN
        middle = 0.5 * final
        qf = split3(q * jnp.exp(cum - middle))
        kf = split3(k * jnp.exp(middle - cum))
        for p in range(PAIRS):
            qp = tuple(stacked_heads(lanes(part, p)) for part in qf[:2])
            kp = tuple(lanes(part, p) for part in kf[:2])
            tmp_ref[p] = mm3(qp, kp, 1, 1)

        @pl.when(opening(pl.program_id(1)) & (c == 0))
        def _():
            for p in range(PAIRS):
                qp = tuple(stacked_heads(lanes(part, p)) for part in qf)
                kp = tuple(lanes(part, p) for part in kf)
                tmp_ref[p] = mm6(qp, kp, 1, 1)

        @pl.when(wild)
        def _():
            exact_scores(q_ref, k_ref, cum_ref, base, tmp_ref)

        qd = q * jnp.exp(cum)
        for p in range(PAIRS):
            s = jnp.where(mask, tmp_ref[p], 0.0)
            s_ref[c, p] = s
            inner = merged_heads(mm3(split(s), split(lanes(v_ref[at, :], p))))
            outer = mm3(split(lanes(qd, p)), split(state_ref[c, p]), 1, 1)
            o_ref[at, p * LANES : (p + 1) * LANES] = inner + outer


def mix_kernel(o_ref, far_ref, tok_ref, gp_ref, mod_ref, out_w_ref, *rest):
    parts, (mid_ref, branch_ref, att_ref, st_ref, o3_ref) = rest[:-5], rest[-5:]
    image, tile = pl.program_id(0), pl.program_id(1)

    @pl.when((image == 0) & (tile == 0))
    def _():
        o3_ref[...] = tall(out_w_ref[...])

    @pl.when(tile == 0)
    def _():
        for p in range(PAIRS):
            st_ref[p] = linked(parts, p)

    far = split(far_ref[...])
    att = o_ref[...] + jnp.concatenate(
        [
            mm3(tuple(lanes(part, p) for part in far), split(st_ref[p]), 1, 1)
            for p in range(PAIRS)
        ],
        axis=1,
    )
    att_ref[...] = att
    rate = lax.rsqrt(head_means(att * att) + 1e-05)
    gp = gp_ref[...]
    branch = dot(wide(att * rate * (gp * sigmoid(gp))), o3_ref[...])
    branch_ref[...] = branch
    mid_ref[...] = tok_ref[...] + mod_ref[2:3, :] * branch


def mlp_kernel(
    mid_ref, cot_ref, mod_ref, up_ref, down_ref, block_ref, dmid_ref, dmod_ref, send_ref, keep_ref, u3_ref, ut_ref, d_ref, dt3_ref, gu_ref, gd_ref
):
    image, tile = pl.program_id(0), pl.program_id(1)
    units = up_ref.shape[1]

    @pl.when((image == 0) & (tile == 0))
    def _():
        u3_ref[...] = tall(up_ref[...])
        ut_ref[...] = across(up_ref[...])
        d_ref[...] = tall(down_ref[...])
        dt3_ref[...] = across(down_ref[...])
        gu_ref[...] = jnp.zeros_like(gu_ref)
        gd_ref[...] = jnp.zeros_like(gd_ref)

    @pl.when(tile == 0)
    def _():
        dmod_ref[...] = jnp.zeros_like(dmod_ref)

    shift_b = mod_ref[3:4, :]
    scale_b = 1.0 + mod_ref[4:5, :]
    gate_b = mod_ref[5:6, :]
    middle = mid_ref[...]
    hat, rate_b = normalized(middle)
    second = hat * scale_b + shift_b
    cot = cot_ref[...]
    dmlp = cot * gate_b
    u = dot(wide(second), u3_ref[...])
    square = u * u
    th = jnp.tanh(GELU_C * (u + 0.044715 * u * square))
    slope = 0.5 * (1.0 + th) + 0.5 * u * (1.0 - th * th) * (
        GELU_C * (1.0 + 3.0 * 0.044715 * square)
    )
    act = split(0.5 * u * (1.0 + th))
    mlp = dot(jnp.concatenate([act[0], act[1], act[0]], axis=1), d_ref[...])
    du = split(dot(wide(dmlp), dt3_ref[...], 1, 1) * slope)
    dsec = dot(jnp.concatenate([du[0], du[1], du[0]], axis=1), ut_ref[...], 1, 1)
    gu_ref[...] += dot(wide(second.T), jnp.concatenate([du[0], du[0], du[1]], axis=0))
    gd_ref[...] += dot(wide(dmlp.T), jnp.concatenate([act[0], act[0], act[1]], axis=0))
    block_ref[...] = middle + gate_b * mlp
    dmid_ref[...] = cot + normal_back(dsec * scale_b, hat, rate_b)
    dmod_ref[3:4, :] += jnp.sum(dsec, axis=0, keepdims=True)
    dmod_ref[4:5, :] += jnp.sum(dsec * hat, axis=0, keepdims=True)
    dmod_ref[5:6, :] += jnp.sum(cot * mlp, axis=0, keepdims=True)

    @pl.when((image == pl.num_programs(0) - 1) & (tile == pl.num_programs(1) - 1))
    def _():
        def lower(ref):
            for j in range(units // WIDTH):
                at = slice(j * WIDTH, (j + 1) * WIDTH)
                ref[at, :] = gu_ref[:, at]

        def upper(ref):
            ref[...] = gd_ref[...].T

        halves_out(lower, upper, send_ref, keep_ref)


def mix_back_kernel(
    dmid_ref,
    branch_ref,
    att_ref,
    gp_ref,
    far_ref,
    normed_ref,
    mod_ref,
    message_ref,
    out_w_ref,
    gate_w_ref,
    datt_ref,
    dnorm_ref,
    send_ref,
    keep_ref,
    dmod_ref,
    dmessage_ref,
    g_ref,
    ot3_ref,
    gt3_ref,
    dst_ref,
):
    image, tile = pl.program_id(0), pl.program_id(1)

    @pl.when((image == 0) & (tile == 0))
    def _():
        ot3_ref[...] = across(out_w_ref[...])
        gt3_ref[...] = across(gate_w_ref[...])
        g_ref[...] = jnp.zeros_like(g_ref)

    @pl.when(tile == 0)
    def _():
        dmod_ref[...] = jnp.zeros_like(dmod_ref)
        dst_ref[...] = jnp.zeros_like(dst_ref)

    dmid = dmid_ref[...]
    dmod_ref[2:3, :] += jnp.sum(dmid * branch_ref[...], axis=0, keepdims=True)
    dbr = split(dmid * mod_ref[2:3, :])
    dy = dot(jnp.concatenate([dbr[0], dbr[1], dbr[0]], axis=1), ot3_ref[...], 1, 1)
    att = att_ref[...]
    rate = lax.rsqrt(head_means(att * att) + 1e-05)
    unit = att * rate
    gp = gp_ref[...]
    sig = sigmoid(gp)
    gate = gp * sig
    g_ref[0:WIDTH, :] += dot(
        wide((unit * gate).T), jnp.concatenate([dbr[0], dbr[0], dbr[1]], axis=0)
    )
    dunit = dy * gate
    datt = rate * (dunit - unit * head_means(dunit * unit))
    datt_ref[...] = datt
    dg = split((dy * unit) * (sig * (1.0 + gp * (1.0 - sig))))
    dnorm_ref[...] = dot(jnp.concatenate([dg[0], dg[1], dg[0]], axis=1), gt3_ref[...], 1, 1)
    start = pl.multiple_of(tile * TILE + GRID, GRID)
    g_ref[WIDTH:, :] += dot(
        wide(normed_ref[pl.ds(start, TILE), :].T), jnp.concatenate([dg[0], dg[0], dg[1]], axis=0)
    )
    da = split(datt)
    far = split(far_ref[...])
    for p in range(PAIRS):
        dst_ref[p] += block_diagonal(
            mm3(tuple(lanes(part, p) for part in da), tuple(lanes(part, p) for part in far), 0, 0)
        )

    @pl.when(tile == pl.num_programs(1) - 1)
    def _():
        for p in range(PAIRS):
            dmessage_ref[p, 0:HEAD_DIM, :] = dst_ref[p, 0:HEAD_DIM, :] + dst_ref[p, HEAD_DIM:, :]
            dmessage_ref[p, HEAD_DIM:, :] = message_ref[p, HEAD_DIM:, :]

    @pl.when((image == pl.num_programs(0) - 1) & (tile == pl.num_programs(1) - 1))
    def _():
        def lower(ref):
            ref[...] = g_ref[0:WIDTH, :]

        def upper(ref):
            ref[...] = g_ref[WIDTH:, :]

        halves_out(lower, upper, send_ref, keep_ref)


def exact_back(q_ref, k_ref, cum_ref, ds_ref, base, dq_ref, dk_ref):
    q = q_ref[pl.ds(base, CHUNK), :]
    cum = cum_ref[pl.ds(base, CHUNK), :]
    dq_ref[...] = jnp.zeros_like(dq_ref)

    def step(j, carry):
        key = k_ref[pl.ds(base + j, 1), :]
        weight = jnp.exp(jnp.minimum(cum - cum_ref[pl.ds(base + j, 1), :], 0.0))
        at = lax.broadcasted_iota(jnp.int32, (2 * CHUNK, CHUNK), 1) == j
        columns = []
        for p in range(PAIRS):
            column = jnp.sum(jnp.where(at, ds_ref[p], 0.0), axis=1, keepdims=True)
            columns.append(merged_heads(jnp.broadcast_to(column, (2 * CHUNK, LANES))))
        ds = jnp.concatenate(columns, axis=1) * weight
        dq_ref[...] += ds * key
        dk_ref[pl.ds(j, 1), :] = jnp.sum(ds * q, axis=0, keepdims=True)
        return carry

    lax.fori_loop(0, CHUNK, step, 0)


def inner_back_kernel(
    q_ref,
    k_ref,
    v_ref,
    cum_ref,
    datt_ref,
    s_ref,
    state_ref,
    fade_ref,
    st_ref,
    dq_ref,
    dk_ref,
    dv_ref,
    full_ref,
    ds_ref,
    dqi_ref,
    dki_ref,
):
    mask = causal_two()
    for c in range(TILE // CHUNK):
        base = c * CHUNK
        at = slice(base, base + CHUNK)
        q = q_ref[at, :]
        k = k_ref[at, :]
        cum = cum_ref[at, :]
        final = cum[CHUNK - 1 : CHUNK, :]
        wild = jnp.max(-final) > SPAN
        middle = 0.5 * final
        eq = jnp.exp(cum - middle)
        ek = jnp.exp(middle - cum)
        qf = split(q * eq)
        kf = split(k * ek)
        da = split3(datt_ref[at, :])
        vs = split3(v_ref[at, :])
        for p in range(PAIRS):
            da2 = tuple(stacked_heads(lanes(part, p)) for part in da[:2])
            vp = tuple(lanes(part, p) for part in vs[:2])
            ds_ref[p] = jnp.where(mask, mm3(da2, vp, 1, 1), 0.0)

        @pl.when(opening(pl.program_id(1)) & (c == 0))
        def _():
            for p in range(PAIRS):
                da2 = tuple(stacked_heads(lanes(part, p)) for part in da)
                vp = tuple(lanes(part, p) for part in vs)
                ds_ref[p] = jnp.where(mask, mm6(da2, vp, 1, 1), 0.0)

        for p in range(PAIRS):
            da2 = tuple(stacked_heads(lanes(part, p)) for part in da[:2])
            ds2 = split(ds_ref[p])
            kp = tuple(lanes(part, p) for part in kf)
            qp = tuple(lanes(part, p) for part in qf)
            dqi_ref[:, p * LANES : (p + 1) * LANES] = merged_heads(mm3(ds2, kp)) * lanes(eq, p)
            q2 = tuple(stacked_heads(part) for part in qp)
            dki_ref[:, p * LANES : (p + 1) * LANES] = mm3(ds2, q2, 0, 0) * lanes(ek, p)
            s2 = split(s_ref[c, p])
            dv_ref[at, p * LANES : (p + 1) * LANES] = mm3(s2, da2, 0, 0)

        @pl.when(wild)
        def _():
            exact_back(q_ref, k_ref, cum_ref, ds_ref, base, dqi_ref, dki_ref)

        grow = jnp.exp(cum)
        for p in range(PAIRS):
            full = state_ref[c, p] + lanes(fade_ref[c, 0:1, :], p) * st_ref[p]
            full_ref[c, p] = full
            outer = mm3(tuple(lanes(part, p) for part in da[:2]), split(full))
            dq_ref[at, p * LANES : (p + 1) * LANES] = (
                dqi_ref[:, p * LANES : (p + 1) * LANES] + outer * lanes(grow, p)
            )
        dk_ref[at, :] = dki_ref[...]


def state_back_kernel(
    valid_ref,
    q_ref,
    k_ref,
    v_ref,
    cum_ref,
    slope_ref,
    datt_ref,
    dq_ref,
    dk_ref,
    dv_ref,
    full_ref,
    *rest,
):
    parts, (proj_ref, dbias_ref, dst_ref) = rest[:-3], rest[-3:]
    image, turn = pl.program_id(0), pl.program_id(1)
    tile = pl.num_programs(1) - 1 - turn

    @pl.when((image == 0) & (turn == 0))
    def _():
        dbias_ref[...] = jnp.zeros_like(dbias_ref)

    @pl.when(turn == 0)
    def _():
        for p in range(PAIRS):
            dst_ref[p] = linked(parts, p)

    count = jnp.sum(valid_ref[...], axis=1, keepdims=True)
    keep = (
        lax.broadcasted_iota(jnp.int32, (CHUNK, WIDTH), 0) + tile * TILE
    )
    for c in reversed(range(TILE // CHUNK)):
        at = slice(c * CHUNK, (c + 1) * CHUNK)
        q = q_ref[at, :]
        k = k_ref[at, :]
        cum = cum_ref[at, :]
        final = cum[CHUNK - 1 : CHUNK, :]
        late = jnp.exp(final - cum)
        kd = k * late
        v = v_ref[at, :]
        qd = split(q * jnp.exp(cum))
        da = split(datt_ref[at, :])
        factor = jnp.exp(final)
        dk_parts, dv_parts, cross = [], [], []
        for p in range(PAIRS):
            old = dst_ref[p]
            pair = split(old)
            dk_parts.append(mm3(split(lanes(v, p)), pair))
            dv_parts.append(mm3(split(lanes(kd, p)), pair, 1, 1))
            leaving = lanes(factor, p) * full_ref[c, p] + block_diagonal(
                mm3(split(lanes(v, p)), split(lanes(kd, p)), 0, 0)
            )
            cross.append(jnp.sum(leaving * old, axis=0, keepdims=True))
            update = mm3(
                tuple(lanes(part, p) for part in da), tuple(lanes(part, p) for part in qd), 0, 0
            )
            dst_ref[p] = lanes(factor, p) * old + block_diagonal(update)
        dq = dq_ref[at, :]
        dk = dk_ref[at, :] + jnp.concatenate(dk_parts, axis=1) * late
        dv = dv_ref[at, :] + jnp.concatenate(dv_parts, axis=1)
        dgates = running_sum(q * dq - k * dk, True) + jnp.concatenate(cross, axis=1)
        dx = dgates * slope_ref[at, :]
        real = keep + c * CHUNK < count
        dk = jnp.where(real, dk, 0.0)
        dv = jnp.where(real, dv, 0.0)
        dbias_ref[...] += jnp.sum(dx.reshape(CHUNK // 8, 8, WIDTH), axis=0)
        proj_ref[at, 0:WIDTH] = dq
        proj_ref[at, WIDTH : 2 * WIDTH] = dk
        proj_ref[at, 2 * WIDTH : 3 * WIDTH] = dv
        proj_ref[at, 3 * WIDTH :] = dx


def hidden_kernel(proj_ref, conv_ref, w_ref, dconv_ref, wt3_ref):
    @pl.when((pl.program_id(0) == 0) & (pl.program_id(1) == 0))
    def _():
        wt3_ref[...] = across(w_ref[...])

    dhidden = dot(wide(proj_ref[...]), wt3_ref[...], 1, 1)
    conv = conv_ref[...]
    sig = sigmoid(conv)
    dconv_ref[...] = dhidden * (sig * (1.0 + conv * (1.0 - sig)))


def weight_kernel(
    conv_ref, proj_ref, dbias_ref, down_ref, up_ref, send_ref, keep_ref, acc_ref, g_ref
):
    image, tile = pl.program_id(0), pl.program_id(1)

    @pl.when((image == 0) & (tile == 0))
    def _():
        acc_ref[...] = jnp.zeros_like(acc_ref)

    conv = conv_ref[...]
    proj = split(proj_ref[...])
    acc_ref[...] += dot(
        wide((conv * sigmoid(conv)).T), jnp.concatenate([proj[0], proj[0], proj[1]], axis=0)
    )

    @pl.when((image == pl.num_programs(0) - 1) & (tile == pl.num_programs(1) - 1))
    def _():
        for j in range(3):
            grad = acc_ref[:, j * WIDTH : (j + 1) * WIDTH]
            g_ref[j * WIDTH : (j + 1) * WIDTH, :] = (
                grad * HEAD_DIM ** (-0.5) if j == 0 else grad
            )
        grad = acc_ref[:, 3 * WIDTH :]
        base = 3 * WIDTH
        rank = up_ref.shape[0]
        g_ref[base:, :] = jnp.zeros_like(g_ref[base:, :])
        g_ref[base : base + rank, :] = mm6(split3(up_ref[...]), split3(grad), 1, 1)
        g_ref[base + rank : base + 2 * rank, :] = mm6(split3(down_ref[...]), split3(grad))
        g_ref[base + 2 * rank : base + 2 * rank + 1, :] = jnp.sum(
            dbias_ref[...], axis=0, keepdims=True
        )

        def lower(ref):
            ref[...] = g_ref[0 : ROWS // 2, :]

        def upper(ref):
            ref[...] = g_ref[ROWS // 2 :, :]

        halves_out(lower, upper, send_ref, keep_ref)


def front_back_kernel(
    tok_ref,
    normed_ref,
    dconv_ref,
    top_ref,
    bot_ref,
    dnorm_ref,
    dmid_ref,
    mod_ref,
    taps_ref,
    grad_ref,
    dmod_ref,
    dtaps_ref,
    pad_ref,
    taps_acc_ref,
):
    length = dconv_ref.shape[0]
    image, i = pl.program_id(0), pl.program_id(1)

    @pl.when((image == 0) & (i == 0))
    def _():
        taps_acc_ref[...] = jnp.zeros_like(taps_acc_ref)

    @pl.when(i == 0)
    def _():
        dmod_ref[...] = jnp.zeros_like(dmod_ref)
        pad_ref[0:GRID, :] = top_ref[...]
        pad_ref[pl.ds(length + GRID, GRID), :] = bot_ref[...]
        pad_ref[pl.ds(GRID, length), :] = dconv_ref[...]

    scale = 1.0 + mod_ref[1:2, :]

    def eights(x):
        return jnp.sum(x.reshape(x.shape[0] // 8, 8, WIDTH), axis=0)

    start = pl.multiple_of(i * TILE, TILE)
    rows = [pad_ref[pl.ds(start + (2 - a) * GRID, TILE), :] for a in range(3)]
    parts = [
        sum(taps_ref[3 * a + b : 3 * a + b + 1, :] * rows[a] for a in range(3))
        for b in range(3)
    ]
    dn = (
        shifted(parts[0], -1)
        + parts[1]
        + shifted(parts[2], 1)
        + dnorm_ref[...]
    )
    hat, rate = normalized(tok_ref[...])
    grad_ref[...] = dmid_ref[...] + normal_back(
        dn * scale, hat, rate
    )
    dmod_ref[0:1, :] += jnp.sum(dn, axis=0, keepdims=True)
    dmod_ref[1:2, :] += jnp.sum(dn * hat, axis=0, keepdims=True)
    own = rows[1]
    moved = [shifted(own, -1), own, shifted(own, 1)]
    for a in range(3):
        near = normed_ref[pl.ds(start + a * GRID, TILE), :]
        for b in range(3):
            taps_acc_ref[3 * a + b] += eights(moved[b] * near)

    @pl.when((image == pl.num_programs(0) - 1) & (i == pl.num_programs(1) - 1))
    def _():
        dtaps_ref[...] = jnp.zeros_like(dtaps_ref)
        for t in range(9):
            dtaps_ref[t : t + 1, :] = jnp.sum(taps_acc_ref[t], axis=0, keepdims=True)


def call(kernel, grid, ins, outs, scratch, flops=0, moved=0, prefetch=0, limit=24):
    return pl.pallas_call(
        kernel,
        grid_spec=pltpu.PrefetchScalarGridSpec(
            num_scalar_prefetch=prefetch,
            grid=grid,
            in_specs=ins,
            out_specs=[spec for spec, _ in outs],
            scratch_shapes=scratch,
        ),
        out_shape=[jax.ShapeDtypeStruct(shape, F32) for _, shape in outs],
        compiler_params=pltpu.CompilerParams(vmem_limit_bytes=limit * 1024 * 1024),
        cost_estimate=pl.CostEstimate(flops=4 * flops, bytes_accessed=4 * moved, transcendentals=0),
    )


def whole(shape):
    zeros = (0,) * len(shape)
    return pl.BlockSpec(shape, lambda *_: zeros, pipeline_mode=pl.Buffered(1))


def per_image(shape):
    zeros = (0,) * len(shape)
    return pl.BlockSpec((None,) + shape, lambda n, *_: (n,) + zeros)


def time_features(timesteps):
    half = FREQ // 2
    freqs = jnp.exp(-math.log(10000.0) * jnp.arange(half, dtype=F32) / half)
    angles = timesteps.astype(F32)[:, None] * freqs[None, :]
    return jnp.concatenate([jnp.cos(angles), jnp.sin(angles)], axis=1)


def halves(axis):
    return [1 << b for b in range(lax.axis_size(axis).bit_length() - 1)]


def swapped(x, axis, bit):
    return lax.ppermute(x, axis, [(i, i ^ bit) for i in range(lax.axis_size(axis))])


def is_high(axis, bit):
    return (lax.axis_index(axis) // bit) % 2


def step_kernel(items, *refs):
    ins, outs = refs[: 2 * len(items)], list(refs[2 * len(items) :])
    for n, (kind, link) in enumerate(items):
        own, got = ins[2 * n], ins[2 * n + 1]
        if kind == "sum":
            outs.pop(0)[...] = own[...] + got[...]
        elif kind == "join":
            out, size, high = outs.pop(0), own.shape[0], is_high(*link) == 1
            out[0:size] = jnp.where(high, got[...], own[...])
            out[size:] = jnp.where(high, own[...], got[...])
        else:
            half = own.shape[0] // 2
            high = is_high(*link)
            for side in (1 - high, high):
                start = side * half
                at = pl.ds(pl.multiple_of(start, 8) if half % 8 == 0 else start, half)
                outs.pop(0)[...] = own[at, :] + got[at, :]


def stepped(flows, got):
    items, arrays, shapes = [], [], []
    for flow, x in zip(flows, got):
        kind, link, own = flow.item()
        if kind == "split" and own.shape[0] % 16:
            flow.took_whole(own + x)
            continue
        items.append((flow, kind, link))
        arrays += [own, x]
        if kind == "split":
            shapes += [(own.shape[0] // 2, WIDTH)] * 2
        else:
            shapes.append((own.shape[0] * (2 if kind == "join" else 1),) + own.shape[1:])
    if not items:
        return
    outs = call(
        functools.partial(step_kernel, [item[1:] for item in items]),
        (1,),
        [whole(x.shape) for x in arrays],
        [(whole(shape), shape) for shape in shapes],
        [],
        flops=sum(x.size for x in arrays),
        moved=8 * sum(x.size for x in arrays),
        limit=24,
    )(*arrays)
    outs = list(outs)
    for flow, kind, _ in items:
        flow.took(*(outs.pop(0) for _ in range(2 if kind == "split" else 1)))


class Flow:
    def __init__(self, sent, keep, order):
        self.sent, self.keep = sent, keep
        self.order, self.used = list(order), []

    def busy(self):
        return bool(self.order)

    def send(self):
        return self.sent

    def link(self):
        return self.order[0]

    def item(self):
        self.used.append(self.order.pop(0))
        if self.order:
            return "split", self.order[0], self.keep
        return "sum", None, self.keep

    def took(self, *new):
        if len(new) == 2:
            self.sent, self.keep = new
        else:
            (self.keep,) = new

    def took_whole(self, total):
        half = total.shape[0] // 2
        high = is_high(*self.order[0])
        self.sent = lax.dynamic_slice_in_dim(total, (1 - high) * half, half)
        self.keep = lax.dynamic_slice_in_dim(total, high * half, half)


class Spread:
    def __init__(self, x, used):
        self.x, self.used = x[None], list(used)

    def busy(self):
        return bool(self.used)

    def send(self):
        return self.x

    def link(self):
        return self.used[-1]

    def item(self):
        return "join", self.used.pop(), self.x

    def took(self, new):
        self.x = new


class Rows:
    def __init__(self, x, sums, joins):
        self.x, self.sums, self.joins = x, list(sums), list(joins)

    def busy(self):
        return bool(self.sums or self.joins)

    def send(self):
        return self.x

    def link(self):
        return self.sums[0] if self.sums else self.joins[0]

    def item(self):
        if self.sums:
            self.sums.pop(0)
            return "sum", None, self.x
        return "join", self.joins.pop(0), self.x

    def took(self, new):
        self.x = new


class Paired:
    def __init__(self, sent, keep, link):
        self.sent, self.keep, self.at, self.got = sent, keep, link, None

    def busy(self):
        return self.got is None

    def send(self):
        return self.sent

    def link(self):
        return self.at


def fork_kernel(parts, *refs):
    count = (len(refs) - 1 - 2 * len(parts)) // 2
    ins, outs, total = refs[: 2 * count], list(refs[2 * count : -1]), refs[-1]
    at = 0
    for n in range(count):
        rows = ins[2 * n].shape[0]
        total[at : at + rows, :] = ins[2 * n][...] + ins[2 * n + 1][...]
        at += rows
    for first, rows, link in parts:
        high = is_high(*link)
        for side in (1 - high, high):
            start = side * (rows // 2) + first
            outs.pop(0)[...] = total[pl.ds(pl.multiple_of(start, 8), rows // 2), :]


def forked(pairs, cut, orders):
    rows = sum(pair.keep.shape[0] for pair in pairs)
    parts = [(0, cut, orders[0][0]), (cut, rows - cut, orders[1][0])]
    arrays = [x for pair in pairs for x in (pair.keep, pair.got)]
    shapes = [(part[1] // 2, WIDTH) for part in parts for _ in range(2)]
    outs = call(
        functools.partial(fork_kernel, parts),
        (1,),
        [whole(x.shape) for x in arrays],
        [(whole(shape), shape) for shape in shapes],
        [pltpu.VMEM((rows, WIDTH), F32)],
        flops=rows * WIDTH,
        moved=12 * rows * WIDTH,
        limit=24,
    )(*arrays)
    return [Flow(outs[0], outs[1], orders[0]), Flow(outs[2], outs[3], orders[1])]


def beside(flows, first, kernel):
    flows = [flow for flow in flows if flow.busy()]
    first, *sends = lax.optimization_barrier((first, *(flow.send() for flow in flows)))
    got = [swapped(x, *flow.link()) for flow, x in zip(flows, sends)]
    outs = kernel(first)
    head, *got = lax.optimization_barrier((outs[0], *got))
    for flow, x in zip(flows, got):
        if isinstance(flow, Paired):
            flow.got = x
    rest = [(flow, x) for flow, x in zip(flows, got) if not isinstance(flow, Paired)]
    stepped([flow for flow, _ in rest], [x for _, x in rest])
    return [head] + list(outs[1:])


def halves_out(lower, upper, send_ref, keep_ref):
    core = lax.axis_index("seq") % 2

    @pl.when(core == 0)
    def _():
        lower(keep_ref)
        upper(send_ref)

    @pl.when(core == 1)
    def _():
        lower(send_ref)
        upper(keep_ref)


def move_first(outs):
    return list(outs[1:]) + [outs[0]]


def messages(message, backward):
    size = lax.axis_size("seq")
    got = []
    for far in range(1, size):
        pairs = [(i, i + far) for i in range(size - far)]
        if backward:
            pairs = [(j, i) for i, j in pairs]
        got.append(lax.ppermute(message, "seq", pairs))
    return got


def plan(early_rows, pieces, units):
    late_rows = tuple(total // pieces for total in (384, ROWS // 2 - 384))
    moves = []

    def place(kind, half, at):
        if kind == 0:
            if at >= units:
                return 2, half * WIDTH + at - units, 0, units + WIDTH - at
            if half == 0:
                return 0, at % WIDTH, at // WIDTH, WIDTH - at % WIDTH
            return 1, at, 0, units - at
        return 3, half * (ROWS // 2) + at, 0, ROWS // 2 - at

    for half in range(2):
        for kind in range(2):
            at = 0
            for flow in range(2):
                rows = early_rows[flow] if kind == 0 else late_rows[flow]
                base = 0 if kind == 0 else early_rows[flow]
                for piece in range(pieces):
                    done = 0
                    while done < rows:
                        out, row, block, room = place(kind, half, at)
                        span = min(rows - done, room)
                        moves.append((half, flow, piece, base + done, out, row, block, span))
                        done, at = done + span, at + span
    return moves


def assemble_kernel(moves, pieces, lasts, core, *refs):
    near, other, near_core, other_core = refs[0:2], refs[2:4], refs[4:6], refs[6:8]
    outs = refs[8:]
    mine = is_high(*core)
    for half, flow, piece, row, out, start, block, span in moves:
        side, index = piece // (pieces // 2), piece % (pieces // 2)
        at = (index, slice(row, row + span), slice(None))
        own = is_high(*lasts[flow]) == side
        here = jnp.where(own, near[flow][at], other[flow][at])
        there = jnp.where(own, near_core[flow][at], other_core[flow][at])
        outs[out][start : start + span, block * WIDTH : (block + 1) * WIDTH] = jnp.where(
            mine == half, here, there
        )


def assembled(near, other, near_core, other_core, lasts, core, early, units):
    early_rows = tuple(flow.keep.shape[0] for flow in early)
    pieces = 2 * near[0].shape[0]
    moves = plan(early_rows, pieces, units)
    shapes = [(WIDTH, units), (units, WIDTH), (2 * WIDTH, WIDTH), (ROWS, WIDTH)]
    arrays = near + other + near_core + other_core
    return call(
        functools.partial(assemble_kernel, moves, pieces, lasts, core),
        (1,),
        [whole(x.shape) for x in arrays],
        [(whole(shape), shape) for shape in shapes],
        [],
        moved=4 * 4 * sum(x.size for x in near),
        limit=40,
    )(*arrays)


def body(
    tokens,
    valid_mask,
    timesteps,
    class_ids,
    time_first,
    time_second,
    class_table,
    ada_weight,
    ada_bias,
    conv_taps,
    query_proj,
    key_proj,
    value_proj,
    decay_down,
    decay_up,
    decay_bias,
    gate_proj,
    out_proj,
    mlp_up,
    mlp_down,
    cotangent,
):
    count, length, width = tokens.shape
    size, mine = lax.axis_size("seq"), lax.axis_index("seq")
    tiles, chunks = length // TILE, length // CHUNK
    per_tile = TILE // CHUNK
    up_pairs = [(i, i + 1) for i in range(size - 1)]
    down_pairs = [(j, i) for i, j in up_pairs]
    seq_bits = [("seq", bit) for bit in halves("seq")]
    img_bits = [("img", bit) for bit in halves("img")]
    core, order_a = seq_bits[0], seq_bits[1:] + img_bits
    order_b = img_bits[:2] + seq_bits[1:] + img_bits[2:]

    def borders(x):
        return (
            lax.ppermute(x[:, length - GRID :], "seq", up_pairs),
            lax.ppermute(x[:, :GRID], "seq", down_pairs),
        )

    above, below = borders(tokens)

    square = (width, width)
    row = (length, width)
    dense = 2 * 3 * count * length * width
    each = 4 * count * length * width
    features = time_features(timesteps)
    mod_spec = per_image((6, width))
    modul, info = call(
        condition_kernel,
        (count,),
        [
            per_image((1, FREQ)),
            whole(time_first.shape),
            whole(time_second.shape),
            pl.BlockSpec((8, width), lambda n, ids: (ids[n] // 8, 0)),
            whole(ada_weight.shape),
            whole((6 * width,)),
        ],
        [
            (mod_spec, (count, 6, width)),
            (per_image((8, width)), (count, 8, width)),
        ],
        [],
        flops=1000000,
        moved=4 * 6 * width * width,
        prefetch=1,
        limit=60,
    )(class_ids, features[:, None], time_first, time_second, class_table, ada_weight, ada_bias)

    valid = valid_mask[:, None]
    valid_spec = per_image((1, length))
    message_shape = (PAIRS, HEAD_DIM + 8, LANES)
    def tiled(shape=(TILE, width)):
        return pl.BlockSpec((None,) + shape, lambda n, i: (n, i, 0))

    tile_row = (tiled(), (count,) + row)
    pair_spec = pl.BlockSpec(
        (None, per_tile, PAIRS, LANES, LANES), lambda n, i: (n, i, 0, 0, 0)
    )
    state_spec = pl.BlockSpec((None, PAIRS, LANES, LANES), lambda n, i: (n, 0, 0, 0))
    state_shape = (count, PAIRS, LANES, LANES)
    score_shape = (count, chunks, PAIRS, 2 * CHUNK, CHUNK)
    score_spec = pl.BlockSpec(
        (None, per_tile, PAIRS, 2 * CHUNK, CHUNK), lambda n, i: (n, i, 0, 0, 0)
    )
    normed_spec = per_image((length + 2 * GRID, width))
    message_spec = per_image(message_shape)
    fade_spec = pl.BlockSpec((None, per_tile, 8, width), lambda n, i: (n, i, 0, 0))
    (
        weights,
        normed,
        conv,
        query,
        keys,
        values,
        cumul,
        slope,
        far,
        states,
        fades,
        message,
    ) = call(
        front_kernel,
        (count, tiles),
        [
            per_image(row),
            per_image((GRID, width)),
            per_image((GRID, width)),
            valid_spec,
            mod_spec,
            whole((9, width)),
            whole(square),
            whole(square),
            whole(square),
            whole(decay_up.shape),
            whole(decay_up.shape),
            whole((width,)),
        ],
        [
            (whole((width, 4 * width)), (width, 4 * width)),
            (per_image((length + 2 * GRID, width)), (count, length + 2 * GRID, width)),
        ]
        + [tile_row] * 7
        + [
            (pair_spec, (count, chunks, PAIRS, LANES, LANES)),
            (fade_spec, (count, chunks, 8, width)),
            (message_spec, (count,) + message_shape),
        ],
        [
            pltpu.VMEM((6 * width, 4 * width), BF16),
            pltpu.VMEM((TILE, 4 * width), F32),
            pltpu.VMEM((PAIRS, LANES, LANES), F32),
            pltpu.VMEM((8, width), F32),
        ],
        flops=dense * 4 * width,
        moved=each * 10,
    )(
        tokens,
        above,
        below,
        valid,
        modul,
        conv_taps,
        query_proj,
        key_proj,
        value_proj,
        decay_down.T,
        decay_up,
        decay_bias,
    )

    forward_parts = messages(message, False)
    inner, scores, gate_in = call(
        inner_kernel,
        (count, tiles),
        [tiled()] * 4 + [pair_spec, normed_spec, whole(square)],
        [tile_row, (score_spec, score_shape), tile_row],
        [pltpu.VMEM((3 * width, width), BF16), pltpu.VMEM((PAIRS, 2 * CHUNK, CHUNK), F32)],
        flops=dense * 2 * width,
        moved=each * 9,
    )(query, keys, values, cumul, states, normed, gate_proj)

    middle, branch, attended, state_in = call(
        mix_kernel,
        (count, tiles),
        [tiled()] * 4 + [mod_spec, whole(square)] + [message_spec] * (size - 1),
        [tile_row] * 3 + [(state_spec, state_shape)],
        [pltpu.VMEM((3 * width, width), BF16)],
        flops=dense * 2 * width,
        moved=each * 7,
    )(inner, far, tokens, gate_in, modul, out_proj, *forward_parts)

    dmod_spec = per_image((8, width))
    dmod_out = (dmod_spec, (count, 8, width))

    units = mlp_up.shape[1]
    block_out, dmid, dmod_mlp, mlp_sent, mlp_kept = call(
        mlp_kernel,
        (count, tiles),
        [tiled(), tiled(), mod_spec, whole(mlp_up.shape), whole(mlp_down.shape)],
        [tile_row] * 2 + [dmod_out] + [(whole((units, width)), (units, width))] * 2,
        [
            pltpu.VMEM((3 * width, units), BF16),
            pltpu.VMEM((width, 3 * units), BF16),
            pltpu.VMEM((3 * units, width), BF16),
            pltpu.VMEM((units, 3 * width), BF16),
            pltpu.VMEM((width, units), F32),
            pltpu.VMEM((width, units), F32),
        ],        flops=dense * 6 * units,
        moved=each * 8,
        limit=40,
    )(middle, cotangent, modul, mlp_up, mlp_down)

    mlp_pair = Paired(mlp_sent, mlp_kept, core)
    datt, dnorm, mix_sent, mix_kept, dmod_mix, d_message = beside([mlp_pair], dmid, lambda x: call(
        mix_back_kernel,
        (count, tiles),
        [tiled()] * 5
        + [normed_spec, mod_spec, message_spec, whole(square), whole(square)],
        [tile_row] * 2
        + [(whole(square), square)] * 2
        + [dmod_out]
        + [(message_spec, (count,) + message_shape)],
        [
            pltpu.VMEM((2 * width, width), F32),
            pltpu.VMEM((width, 3 * width), BF16),
            pltpu.VMEM((width, 3 * width), BF16),
            pltpu.VMEM((PAIRS, LANES, LANES), F32),
        ],
        flops=dense * 5 * width,
        moved=each * 8,
    )(x, branch, attended, gate_in, far, normed, modul, message, out_proj, gate_proj))
    mix_pair = Paired(mix_sent, mix_kept, core)
    d_message, datt = lax.optimization_barrier((d_message, datt))
    backward_parts = messages(d_message, True)

    dquery, dkeys, dvalues, full = beside([mix_pair], datt, lambda x: call(
        inner_back_kernel,
        (count, tiles),
        [tiled()] * 5 + [score_spec, pair_spec, fade_spec, state_spec],
        [tile_row] * 3 + [(pair_spec, (count, chunks, PAIRS, LANES, LANES))],
        [
            pltpu.VMEM((PAIRS, 2 * CHUNK, CHUNK), F32),
            pltpu.VMEM((CHUNK, width), F32),
            pltpu.VMEM((CHUNK, width), F32),
        ],
        flops=dense * 2 * width,
        moved=each * 12,
        limit=60,
    )(query, keys, values, cumul, x, scores, states, fades, state_in))

    early = forked([mlp_pair, mix_pair], 1024, (order_a, order_b))

    def turned(shape=(TILE, width)):
        return pl.BlockSpec((None,) + shape, lambda n, i: (n, tiles - 1 - i, 0))

    dproj, dbias = beside(early, dquery, lambda x: call(
        state_back_kernel,
        (count, tiles),
        [valid_spec]
        + [turned()] * 9
        + [
            pl.BlockSpec(
                (None, per_tile, PAIRS, LANES, LANES),
                lambda n, i: (n, tiles - 1 - i, 0, 0, 0),
            ),
        ]
        + [message_spec] * (size - 1),
        [
            (turned((TILE, 4 * width)), (count, length, 4 * width)),
            (whole((8, width)), (8, width)),
        ],
        [pltpu.VMEM((PAIRS, LANES, LANES), F32)],
        flops=dense * 2 * width,
        moved=each * 14,
        limit=60,
    )(
        valid,
        query,
        keys,
        values,
        cumul,
        slope,
        datt,
        x,
        dkeys,
        dvalues,
        full,
        *backward_parts,
    ))
    late_sent, late_kept = beside(early, dproj, lambda x: call(
        weight_kernel,
        (count, tiles),
        [
            tiled(),
            tiled((TILE, 4 * width)),
            whole((8, width)),
            whole(decay_up.shape),
            whole(decay_up.shape),
        ],
        [(whole((ROWS // 2, width)), (ROWS // 2, width))] * 2,
        [pltpu.VMEM((width, 4 * width), F32), pltpu.VMEM((ROWS, width), F32)],
        flops=dense * 4 * width,
        moved=each * 7,
    )(conv, x, dbias, decay_down.T, decay_up))
    late_pair = Paired(late_sent, late_kept, core)
    (dconv,) = beside([late_pair], late_kept, lambda x: call(
        hidden_kernel,
        (count, tiles),
        [tiled((TILE, 4 * width)), tiled(), whole((width, 4 * width))],
        [tile_row],
        [pltpu.VMEM((width, 3 * 4 * width), BF16)],
        flops=dense * 4 * width,
        moved=each * 7,
    )(lax.optimization_barrier((dproj, x))[0], conv, weights))
    d_above, d_below = borders(dconv)
    late = forked([late_pair], 384, (order_a, order_b))
    dmod_front, dtaps, tokens_grad = beside(early + late, dconv, lambda x: move_first(call(
        front_back_kernel,
        (count, tiles),
        [
            tiled(),
            per_image((length + 2 * GRID, width)),
            per_image(row),
            per_image((GRID, width)),
            per_image((GRID, width)),
            tiled(),
            tiled(),
            mod_spec,
            whole((9, width)),
        ],
        [
            tile_row,
            dmod_out,
            (whole((16, width)), (16, width)),
        ],
        [
            pltpu.VMEM((length + 2 * GRID, width), F32),
            pltpu.VMEM((9, 8, width), F32),
        ],
        flops=count * length * width * 100,
        moved=each * 6,
    )(tokens, normed, x, d_above, d_below, dnorm, dmid, modul, conv_taps)))

    dmod = (dmod_front + dmod_mlp + dmod_mix)[:, :6]
    own = jnp.where(mine == 0, info[:, :3], 0.0)
    ids = jnp.where(mine == 0, class_ids, 0).astype(F32)[:, None, None]
    ids = jnp.broadcast_to(ids, (count, 1, width))
    taps = jnp.concatenate([dtaps[None, :9], jnp.zeros((count - 1, 9, width), F32)])
    rows = jnp.concatenate([dmod, own, ids, taps, jnp.zeros((count, 5, width), F32)], axis=1)
    flow_r = Rows(rows, seq_bits, img_bits)
    none = jnp.zeros((), F32)
    while any(flow.busy() for flow in early + late):
        beside([flow_r] + early + late, none, lambda x: [x])
    spread_a, spread_b = (
        Spread(jnp.concatenate([one.keep, two.keep]), one.used) for one, two in zip(early, late)
    )
    while flow_r.busy():
        beside([flow_r, spread_a, spread_b], none, lambda x: [x])
    rows = flow_r.x
    images = rows.shape[0]
    ids = rows[:, 9, 0].astype(jnp.int32)
    g_first, g_second, g_class, g_ada, g_ada_bias, g_taps = beside([spread_a, spread_b], rows, lambda x: call(
        embed_kernel,
        (1,),
        [
            whole(rows.shape),
            whole(ada_weight.shape),
            whole(time_second.shape),
        ],
        [
            (whole(shape), shape)
            for shape in (
                time_first.shape,
                time_second.shape,
                class_table.shape,
                ada_weight.shape,
                (1, 6 * width),
                (9, width),
            )
        ],
        [],
        flops=images * 2 * 3 * width * width * 14,
        moved=4 * width * width * 20,
        prefetch=1,
    )(ids, x, ada_weight, time_second))
    while len(spread_a.used) > 1 or len(spread_b.used) > 1:
        beside([spread_a, spread_b], none, lambda x: [x])
    lasts = (spread_a.link(), spread_b.link())
    near = [spread_a.x, spread_b.x]
    far_ones = [swapped(x, *last) for x, last in zip(near, lasts)]
    near_core = [swapped(x, *core) for x in near]
    far_core = [swapped(x, *core) for x in far_ones]
    g_up, g_down, g_mix, g_proj = assembled(
        near, far_ones, near_core, far_core, lasts, core, early, units
    )

    rank = decay_up.shape[0]
    base = 3 * width
    return (
        block_out,
        tokens_grad,
        g_first,
        g_second,
        g_class,
        g_ada,
        g_ada_bias[0],
        g_taps,
        g_proj[:width],
        g_proj[width : 2 * width],
        g_proj[2 * width : base],
        g_proj[base : base + rank].T,
        g_proj[base + rank : base + 2 * rank],
        g_proj[base + 2 * rank],
        g_mix[width:],
        g_mix[:width],
        g_up,
        g_down,
    )


def solution(mesh):
    image, shared = P("img", "seq", None), P()
    return jax.shard_map(
        body,
        mesh=mesh,
        in_specs=(image, P("img", "seq"), P("img"), P("img")) + (shared,) * 16 + (image,),
        out_specs=(image, image) + (shared,) * 16,
        check_vma=False,
    )
```

```python
import functools
import math

import jax
import jax.numpy as jnp
from jax import lax
from jax.experimental import pallas as pl
from jax.experimental.pallas import tpu as pltpu
from jax.sharding import PartitionSpec as P

HEADS = 6
HEAD_DIM = 64
CLASSES = 1000
FREQ = 256
GRID = 64
WIDTH = 384
PAIRS = 3
LANES = 128
CHUNK = 128
TILE = 256
ROWS = 1280
EARLY = (768, 768, 384)
LATE = (256, 256, 128)
SPAN = 120.0
HIGH = lax.Precision.HIGHEST
F32 = jnp.float32
BF16 = jnp.bfloat16
GELU_C = math.sqrt(2.0 / math.pi)


def product(left, right):
    return jnp.dot(left, right, precision=HIGH, preferred_element_type=F32)


def dot(a, b, ca=1, cb=0):
    return lax.dot_general(a, b, (((ca,), (cb,)), ((), ())), preferred_element_type=F32)


def split(x):
    high = x.astype(BF16)
    return high, (x - high.astype(F32)).astype(BF16)


def mm3(a, b, ca=1, cb=0):
    return dot(a[0], b[0], ca, cb) + dot(a[1], b[0], ca, cb) + dot(a[0], b[1], ca, cb)


def split3(x):
    high = x.astype(BF16)
    rest = x - high.astype(F32)
    middle = rest.astype(BF16)
    return high, middle, (rest - middle.astype(F32)).astype(BF16)


def mm6(a, b, ca=1, cb=0):
    terms = ((0, 0), (0, 1), (1, 0), (1, 1), (0, 2), (2, 0))
    return sum(dot(a[i], b[j], ca, cb) for i, j in reversed(terms))


def wide6(x):
    h, m, l = split3(x)
    return jnp.concatenate([h, h, m, m, h, l], axis=1)


def tall6(w):
    h, m, l = split3(w)
    return jnp.concatenate([h, m, h, m, l, h], axis=0)


def wide3(x):
    high, low = split(x)
    return jnp.concatenate([high, high, low], axis=1)


def wide(x):
    high, low = split(x)
    return jnp.concatenate([high, low, high], axis=1)


def tall(w):
    high, low = split(w)
    return jnp.concatenate([high, high, low], axis=0)


def across(w):
    high, low = split(w)
    return jnp.concatenate([high, high, low], axis=1)


def lanes(x, p):
    return x[..., p * LANES : (p + 1) * LANES]


def first_half(shape):
    return lax.broadcasted_iota(jnp.int32, shape, len(shape) - 1) < HEAD_DIM


def block_diagonal(square):
    rows = lax.broadcasted_iota(jnp.int32, square.shape, 0) < HEAD_DIM
    return jnp.where(rows == first_half(square.shape), square, 0.0)


def head_mean(x):
    rows = lax.broadcasted_iota(jnp.int32, (LANES, LANES), 0) < HEAD_DIM
    ones = jnp.where(rows == first_half((LANES, LANES)), 1.0 / HEAD_DIM, 0.0).astype(BF16)
    high, low = split(x)
    return dot(
        jnp.concatenate([high, low], axis=1), jnp.concatenate([ones, ones], axis=0)
    )


def head_means(x):
    return jnp.concatenate([head_mean(lanes(x, p)) for p in range(PAIRS)], axis=1)


def stacked_heads(x):
    keep = first_half(x.shape)
    zero = jnp.zeros_like(x)
    return jnp.concatenate([jnp.where(keep, x, zero), jnp.where(keep, zero, x)], axis=0)


def merged_heads(x):
    rows = x.shape[0] // 2
    return jnp.where(first_half((rows, LANES)), x[:rows], x[rows:])


def sigmoid(x):
    return 1.0 / (1.0 + jnp.exp(-x))


def shifted(x, step):
    rows = x.shape[0]
    column = lax.broadcasted_iota(jnp.int32, x.shape, 0) % GRID
    if step == 1:
        return jnp.where(column == 0, 0.0, pltpu.roll(x, 1, 0))
    return jnp.where(column == GRID - 1, 0.0, pltpu.roll(x, rows - 1, 0))


def normalized(x):
    center = x - jnp.mean(x, axis=-1, keepdims=True)
    rate = lax.rsqrt(jnp.mean(center * center, axis=-1, keepdims=True) + 1e-06)
    return center * rate, rate


def normal_back(dhat, hat, rate):
    return rate * (
        dhat
        - jnp.mean(dhat, axis=-1, keepdims=True)
        - hat * jnp.mean(dhat * hat, axis=-1, keepdims=True)
    )


def triangle(size, upper):
    rows = lax.broadcasted_iota(jnp.int32, (size, size), 0)
    cols = lax.broadcasted_iota(jnp.int32, (size, size), 1)
    return jnp.where(cols >= rows if upper else cols <= rows, 1.0, 0.0).astype(BF16)


def running_sum(x, upper):
    tri = triangle(x.shape[0], upper)
    high = x.astype(BF16)
    rest = x - high.astype(F32)
    middle = rest.astype(BF16)
    low = (rest - middle.astype(F32)).astype(BF16)
    return dot(tri, high) + dot(tri, middle) + dot(tri, low)


def opening(tile):
    return (lax.axis_index("seq") == 0) & (tile == 0)


def spread(compact):
    keep = first_half(compact.shape)
    return jnp.concatenate(
        [jnp.where(keep, compact, 0.0), jnp.where(keep, 0.0, compact)], axis=0
    )


def linked(parts, p):
    total = jnp.zeros((HEAD_DIM, LANES), F32)
    for part in reversed(parts):
        total = part[p, 0:HEAD_DIM, :] + part[p, HEAD_DIM : HEAD_DIM + 1, :] * total
    return spread(total)


def as_column(row):
    return jnp.broadcast_to(row, (8, row.shape[1])).T[:, 0:1]


def applied(row, w_ref):
    return jnp.sum(as_column(row) * w_ref[...], axis=0, keepdims=True)


def condition_kernel(ids_ref, feat_ref, first_w_ref, second_w_ref, row_ref, ada_ref, bias_ref, mod_ref, info_ref):
    features = feat_ref[...]
    first = applied(features, first_w_ref)
    embed = applied(first * sigmoid(first), second_w_ref)
    at = lax.broadcasted_iota(jnp.int32, row_ref.shape, 0) == ids_ref[pl.program_id(0)] % 8
    embed = embed + jnp.sum(jnp.where(at, row_ref[...], 0.0), axis=0, keepdims=True)
    modul = applied(embed * sigmoid(embed), ada_ref)
    for j in range(6):
        at = slice(j * WIDTH, (j + 1) * WIDTH)
        mod_ref[j : j + 1, :] = modul[:, at] + bias_ref[at][None, :]
    info_ref[...] = jnp.zeros_like(info_ref)
    info_ref[0:1, 0:FREQ] = features
    info_ref[1:2, :] = first
    info_ref[2:3, :] = embed
    info_ref[3:4, :] = jnp.full((1, WIDTH), ids_ref[pl.program_id(0)], jnp.int32).astype(F32)


def embed_kernel(
    ids_ref, rows_ref, ada_ref, second_ref, gf_ref, gs_ref, gc_ref, ga_ref, gb_ref, gt_ref
):
    images = rows_ref.shape[0]
    features, first, embed = rows_ref[:, 6, 0:FREQ], rows_ref[:, 7, :], rows_ref[:, 8, :]
    gt_ref[...] = jnp.sum(rows_ref[:, 10:19, :], axis=0)

    def silu_back(x, grad):
        sig = sigmoid(x)
        return grad * (sig * (1.0 + x * (1.0 - sig)))

    act = split((embed * sigmoid(embed)).T)
    dembed = jnp.zeros((images, WIDTH), F32)
    for j in range(6):
        at = slice(j * WIDTH, (j + 1) * WIDTH)
        grad = rows_ref[:, j, :]
        dmod = split(grad)
        ga_ref[:, at] = mm3(act, dmod)
        gb_ref[at] = jnp.sum(grad, axis=0)
        dembed = dembed + mm3(dmod, split(ada_ref[:, at]), 1, 1)
    dembed = silu_back(embed, dembed)
    gc_ref[...] = jnp.zeros_like(gc_ref)

    def put(n, carry):
        mine = lax.broadcasted_iota(jnp.int32, (images, WIDTH), 0) == n
        row = jnp.sum(jnp.where(mine, dembed, 0.0), axis=0, keepdims=True)
        gc_ref[pl.ds(ids_ref[n], 1), :] += row
        return carry

    lax.fori_loop(0, images, put, 0)
    de = split(dembed)
    gs_ref[...] = mm3(split((first * sigmoid(first)).T), de)
    dfirst = silu_back(first, mm3(de, split(second_ref[...]), 1, 1))
    gf_ref[...] = mm3(split(features.T), split(dfirst))


def front_kernel(
    tok_ref,
    top_ref,
    bot_ref,
    valid_ref,
    mod_ref,
    taps_ref,
    wq_ref,
    wk_ref,
    wv_ref,
    down_ref,
    up_ref,
    bias_ref,
    w_ref,
    normed_ref,
    conv_ref,
    q_ref,
    k_ref,
    v_ref,
    cum_ref,
    slope_ref,
    far_ref,
    state_ref,
    fade_ref,
    out_ref,
    w3_ref,
    proj_ref,
    st_ref,
    dev_ref,
):
    image, i = pl.program_id(0), pl.program_id(1)
    length = tok_ref.shape[0]

    @pl.when((image == 0) & (i == 0))
    def _():
        w_ref[:, 0:WIDTH] = wq_ref[...] * HEAD_DIM ** (-0.5)
        w_ref[:, WIDTH : 2 * WIDTH] = wk_ref[...]
        w_ref[:, 2 * WIDTH : 3 * WIDTH] = wv_ref[...]
        w_ref[:, 3 * WIDTH :] = mm6(split3(down_ref[...]), split3(up_ref[...]), 0, 0)
        w3_ref[...] = tall6(w_ref[...])

    real = jnp.sum(valid_ref[...], axis=1, keepdims=True)
    shift = mod_ref[0:1, :]
    scale = 1.0 + mod_ref[1:2, :]

    def modulated(x):
        return normalized(x)[0] * scale + shift

    @pl.when(i == 0)
    def _():
        normed_ref[0:GRID, :] = jnp.where(
            lax.axis_index("seq") == 0, 0.0, modulated(top_ref[...])
        )
        normed_ref[pl.ds(length + GRID, GRID), :] = jnp.where(
            lax.axis_index("seq") == lax.axis_size("seq") - 1, 0.0, modulated(bot_ref[...])
        )
        for at in range(0, length, TILE):
            normed_ref[GRID + at : GRID + at + TILE, :] = modulated(tok_ref[at : at + TILE, :])
        st_ref[...] = jnp.zeros_like(st_ref)
        dev_ref[...] = jnp.zeros_like(dev_ref)

    start = pl.multiple_of(i * TILE, TILE)
    rows = [normed_ref[pl.ds(start + a * GRID, TILE), :] for a in range(3)]
    parts = [
        sum(taps_ref[3 * a + b : 3 * a + b + 1, :] * rows[a] for a in range(3))
        for b in range(3)
    ]
    conv = shifted(parts[0], 1) + parts[1] + shifted(parts[2], -1)
    conv_ref[...] = conv
    hidden = conv * sigmoid(conv)
    first = opening(i)

    @pl.when(first)
    def _():
        proj_ref[...] = dot(wide6(hidden), w3_ref[...])

    @pl.when(jnp.logical_not(first))
    def _():
        proj_ref[...] = dot(wide3(hidden), w3_ref[0 : 3 * WIDTH, :])

    proj = proj_ref[...]
    keep = (
        lax.broadcasted_iota(jnp.int32, (TILE, WIDTH), 0) + start < real
    )
    q = proj[:, :WIDTH]
    k = jnp.where(keep, proj[:, WIDTH : 2 * WIDTH], 0.0)
    v = jnp.where(keep, proj[:, 2 * WIDTH : 3 * WIDTH], 0.0)
    x = proj[:, 3 * WIDTH :] + bias_ref[...][None, :]
    small = jnp.exp(-jnp.abs(x))
    gates = jnp.where(keep, (jnp.minimum(x, 0.0) - jnp.log1p(small)) * (1.0 / 16.0), 0.0)
    slope = jnp.where(x >= 0, small, 1.0) / (1.0 + small)
    slope_ref[...] = jnp.where(keep, slope * (1.0 / 16.0), 0.0)
    q_ref[...] = q
    k_ref[...] = k
    v_ref[...] = v
    for c in range(TILE // CHUNK):
        at = slice(c * CHUNK, (c + 1) * CHUNK)
        cum = running_sum(gates[at], False)
        cum_ref[at, :] = cum
        final = cum[CHUNK - 1 : CHUNK, :]
        dev = dev_ref[0:1, :]
        far_ref[at, :] = q[at] * jnp.exp(cum + dev)
        fade_ref[c] = jnp.broadcast_to(jnp.exp(dev), (8, WIDTH))
        kd = k[at] * jnp.exp(final - cum)
        factor = jnp.exp(final)
        for p in range(PAIRS):
            state_ref[c, p] = st_ref[p]
            update = mm3(split(lanes(v[at], p)), split(lanes(kd, p)), 0, 0)
            st_ref[p] = lanes(factor, p) * st_ref[p] + block_diagonal(update)
        dev_ref[...] = dev_ref[...] + final

    @pl.when(i == pl.num_programs(1) - 1)
    def _():
        for p in range(PAIRS):
            out_ref[p, 0:HEAD_DIM, :] = st_ref[p, 0:HEAD_DIM, :] + st_ref[p, HEAD_DIM:, :]
            out_ref[p, HEAD_DIM:, :] = jnp.exp(lanes(dev_ref[...], p))


def exact_scores(q_ref, k_ref, cum_ref, base, s_ref):
    q = q_ref[pl.ds(base, CHUNK), :]
    cum = cum_ref[pl.ds(base, CHUNK), :]
    s_ref[...] = jnp.zeros_like(s_ref)

    def step(j, carry):
        key = k_ref[pl.ds(base + j, 1), :]
        weight = jnp.exp(jnp.minimum(cum - cum_ref[pl.ds(base + j, 1), :], 0.0))
        terms = q * key * weight
        for p in range(PAIRS):
            column = jnp.sum(stacked_heads(lanes(terms, p)), axis=1, keepdims=True)
            at = lax.broadcasted_iota(jnp.int32, (2 * CHUNK, CHUNK), 1) == j
            s_ref[p] = jnp.where(at, column, s_ref[p])
        return carry

    lax.fori_loop(0, CHUNK, step, 0)


def causal_two():
    rows = lax.broadcasted_iota(jnp.int32, (2 * CHUNK, CHUNK), 0) % CHUNK
    return rows >= lax.broadcasted_iota(jnp.int32, (2 * CHUNK, CHUNK), 1)


def inner_kernel(
    q_ref, k_ref, v_ref, cum_ref, state_ref, normed_ref, gate_ref, o_ref, s_ref, gp_ref, w3_ref, tmp_ref
):
    @pl.when((pl.program_id(0) == 0) & (pl.program_id(1) == 0))
    def _():
        w3_ref[...] = tall(gate_ref[...])

    start = pl.multiple_of(pl.program_id(1) * TILE + GRID, GRID)
    gp_ref[...] = dot(wide(normed_ref[pl.ds(start, TILE), :]), w3_ref[...])
    mask = causal_two()
    for c in range(TILE // CHUNK):
        base = c * CHUNK
        at = slice(base, base + CHUNK)
        q = q_ref[at, :]
        k = k_ref[at, :]
        cum = cum_ref[at, :]
        final = cum[CHUNK - 1 : CHUNK, :]
        wild = jnp.max(-final) > SPAN
        middle = 0.5 * final
        qf = split3(q * jnp.exp(cum - middle))
        kf = split3(k * jnp.exp(middle - cum))
        for p in range(PAIRS):
            qp = tuple(stacked_heads(lanes(part, p)) for part in qf[:2])
            kp = tuple(lanes(part, p) for part in kf[:2])
            tmp_ref[p] = mm3(qp, kp, 1, 1)

        @pl.when(opening(pl.program_id(1)) & (c == 0))
        def _():
            for p in range(PAIRS):
                qp = tuple(stacked_heads(lanes(part, p)) for part in qf)
                kp = tuple(lanes(part, p) for part in kf)
                tmp_ref[p] = mm6(qp, kp, 1, 1)

        @pl.when(wild)
        def _():
            exact_scores(q_ref, k_ref, cum_ref, base, tmp_ref)

        qd = q * jnp.exp(cum)
        for p in range(PAIRS):
            s = jnp.where(mask, tmp_ref[p], 0.0)
            s_ref[c, p] = s
            inner = merged_heads(mm3(split(s), split(lanes(v_ref[at, :], p))))
            outer = mm3(split(lanes(qd, p)), split(state_ref[c, p]), 1, 1)
            o_ref[at, p * LANES : (p + 1) * LANES] = inner + outer


def mix_kernel(o_ref, far_ref, tok_ref, gp_ref, mod_ref, out_w_ref, *rest):
    parts, (mid_ref, branch_ref, att_ref, st_ref, o3_ref) = rest[:-5], rest[-5:]
    image, tile = pl.program_id(0), pl.program_id(1)

    @pl.when((image == 0) & (tile == 0))
    def _():
        o3_ref[...] = tall(out_w_ref[...])

    @pl.when(tile == 0)
    def _():
        for p in range(PAIRS):
            st_ref[p] = linked(parts, p)

    far = split(far_ref[...])
    att = o_ref[...] + jnp.concatenate(
        [
            mm3(tuple(lanes(part, p) for part in far), split(st_ref[p]), 1, 1)
            for p in range(PAIRS)
        ],
        axis=1,
    )
    att_ref[...] = att
    rate = lax.rsqrt(head_means(att * att) + 1e-05)
    gp = gp_ref[...]
    branch = dot(wide(att * rate * (gp * sigmoid(gp))), o3_ref[...])
    branch_ref[...] = branch
    mid_ref[...] = tok_ref[...] + mod_ref[2:3, :] * branch


def mlp_kernel(
    mid_ref, cot_ref, mod_ref, up_ref, down_ref, block_ref, dmid_ref, dmod_ref, send_ref, keep_ref, u3_ref, ut_ref, d_ref, dt3_ref, gu_ref, gd_ref
):
    image, tile = pl.program_id(0), pl.program_id(1)
    units = up_ref.shape[1]

    @pl.when((image == 0) & (tile == 0))
    def _():
        u3_ref[...] = tall(up_ref[...])
        ut_ref[...] = across(up_ref[...])
        d_ref[...] = tall(down_ref[...])
        dt3_ref[...] = across(down_ref[...])
        gu_ref[...] = jnp.zeros_like(gu_ref)
        gd_ref[...] = jnp.zeros_like(gd_ref)

    @pl.when(tile == 0)
    def _():
        dmod_ref[...] = jnp.zeros_like(dmod_ref)

    shift_b = mod_ref[3:4, :]
    scale_b = 1.0 + mod_ref[4:5, :]
    gate_b = mod_ref[5:6, :]
    middle = mid_ref[...]
    hat, rate_b = normalized(middle)
    second = hat * scale_b + shift_b
    cot = cot_ref[...]
    dmlp = cot * gate_b
    u = dot(wide(second), u3_ref[...])
    square = u * u
    th = jnp.tanh(GELU_C * (u + 0.044715 * u * square))
    slope = 0.5 * (1.0 + th) + 0.5 * u * (1.0 - th * th) * (
        GELU_C * (1.0 + 3.0 * 0.044715 * square)
    )
    act = split(0.5 * u * (1.0 + th))
    mlp = dot(jnp.concatenate([act[0], act[1], act[0]], axis=1), d_ref[...])
    du = split(dot(wide(dmlp), dt3_ref[...], 1, 1) * slope)
    dsec = dot(jnp.concatenate([du[0], du[1], du[0]], axis=1), ut_ref[...], 1, 1)
    gu_ref[...] += dot(wide(second.T), jnp.concatenate([du[0], du[0], du[1]], axis=0))
    gd_ref[...] += dot(wide(dmlp.T), jnp.concatenate([act[0], act[0], act[1]], axis=0))
    block_ref[...] = middle + gate_b * mlp
    dmid_ref[...] = cot + normal_back(dsec * scale_b, hat, rate_b)
    dmod_ref[3:4, :] += jnp.sum(dsec, axis=0, keepdims=True)
    dmod_ref[4:5, :] += jnp.sum(dsec * hat, axis=0, keepdims=True)
    dmod_ref[5:6, :] += jnp.sum(cot * mlp, axis=0, keepdims=True)

    @pl.when((image == pl.num_programs(0) - 1) & (tile == pl.num_programs(1) - 1))
    def _():
        def lower(ref):
            for j in range(units // WIDTH):
                at = slice(j * WIDTH, (j + 1) * WIDTH)
                ref[at, :] = gu_ref[:, at]

        def upper(ref):
            ref[...] = gd_ref[...].T

        halves_out(lower, upper, send_ref, keep_ref)


def mix_back_kernel(
    dmid_ref,
    branch_ref,
    att_ref,
    gp_ref,
    far_ref,
    normed_ref,
    mod_ref,
    message_ref,
    out_w_ref,
    gate_w_ref,
    datt_ref,
    dnorm_ref,
    send_ref,
    keep_ref,
    dmod_ref,
    dmessage_ref,
    g_ref,
    ot3_ref,
    gt3_ref,
    dst_ref,
):
    image, tile = pl.program_id(0), pl.program_id(1)

    @pl.when((image == 0) & (tile == 0))
    def _():
        ot3_ref[...] = across(out_w_ref[...])
        gt3_ref[...] = across(gate_w_ref[...])
        g_ref[...] = jnp.zeros_like(g_ref)

    @pl.when(tile == 0)
    def _():
        dmod_ref[...] = jnp.zeros_like(dmod_ref)
        dst_ref[...] = jnp.zeros_like(dst_ref)

    dmid = dmid_ref[...]
    dmod_ref[2:3, :] += jnp.sum(dmid * branch_ref[...], axis=0, keepdims=True)
    dbr = split(dmid * mod_ref[2:3, :])
    dy = dot(jnp.concatenate([dbr[0], dbr[1], dbr[0]], axis=1), ot3_ref[...], 1, 1)
    att = att_ref[...]
    rate = lax.rsqrt(head_means(att * att) + 1e-05)
    unit = att * rate
    gp = gp_ref[...]
    sig = sigmoid(gp)
    gate = gp * sig
    g_ref[0:WIDTH, :] += dot(
        wide((unit * gate).T), jnp.concatenate([dbr[0], dbr[0], dbr[1]], axis=0)
    )
    dunit = dy * gate
    datt = rate * (dunit - unit * head_means(dunit * unit))
    datt_ref[...] = datt
    dg = split((dy * unit) * (sig * (1.0 + gp * (1.0 - sig))))
    dnorm_ref[...] = dot(jnp.concatenate([dg[0], dg[1], dg[0]], axis=1), gt3_ref[...], 1, 1)
    start = pl.multiple_of(tile * TILE + GRID, GRID)
    g_ref[WIDTH:, :] += dot(
        wide(normed_ref[pl.ds(start, TILE), :].T), jnp.concatenate([dg[0], dg[0], dg[1]], axis=0)
    )
    da = split(datt)
    far = split(far_ref[...])
    for p in range(PAIRS):
        dst_ref[p] += block_diagonal(
            mm3(tuple(lanes(part, p) for part in da), tuple(lanes(part, p) for part in far), 0, 0)
        )

    @pl.when(tile == pl.num_programs(1) - 1)
    def _():
        for p in range(PAIRS):
            dmessage_ref[p, 0:HEAD_DIM, :] = dst_ref[p, 0:HEAD_DIM, :] + dst_ref[p, HEAD_DIM:, :]
            dmessage_ref[p, HEAD_DIM:, :] = message_ref[p, HEAD_DIM:, :]

    @pl.when((image == pl.num_programs(0) - 1) & (tile == pl.num_programs(1) - 1))
    def _():
        def lower(ref):
            ref[...] = g_ref[0:WIDTH, :]

        def upper(ref):
            ref[...] = g_ref[WIDTH:, :]

        halves_out(lower, upper, send_ref, keep_ref)


def exact_back(q_ref, k_ref, cum_ref, ds_ref, base, dq_ref, dk_ref):
    q = q_ref[pl.ds(base, CHUNK), :]
    cum = cum_ref[pl.ds(base, CHUNK), :]
    dq_ref[...] = jnp.zeros_like(dq_ref)

    def step(j, carry):
        key = k_ref[pl.ds(base + j, 1), :]
        weight = jnp.exp(jnp.minimum(cum - cum_ref[pl.ds(base + j, 1), :], 0.0))
        at = lax.broadcasted_iota(jnp.int32, (2 * CHUNK, CHUNK), 1) == j
        columns = []
        for p in range(PAIRS):
            column = jnp.sum(jnp.where(at, ds_ref[p], 0.0), axis=1, keepdims=True)
            columns.append(merged_heads(jnp.broadcast_to(column, (2 * CHUNK, LANES))))
        ds = jnp.concatenate(columns, axis=1) * weight
        dq_ref[...] += ds * key
        dk_ref[pl.ds(j, 1), :] = jnp.sum(ds * q, axis=0, keepdims=True)
        return carry

    lax.fori_loop(0, CHUNK, step, 0)


def inner_back_kernel(
    q_ref,
    k_ref,
    v_ref,
    cum_ref,
    datt_ref,
    s_ref,
    state_ref,
    fade_ref,
    st_ref,
    dq_ref,
    dk_ref,
    dv_ref,
    full_ref,
    ds_ref,
    dqi_ref,
    dki_ref,
):
    mask = causal_two()
    for c in range(TILE // CHUNK):
        base = c * CHUNK
        at = slice(base, base + CHUNK)
        q = q_ref[at, :]
        k = k_ref[at, :]
        cum = cum_ref[at, :]
        final = cum[CHUNK - 1 : CHUNK, :]
        wild = jnp.max(-final) > SPAN
        middle = 0.5 * final
        eq = jnp.exp(cum - middle)
        ek = jnp.exp(middle - cum)
        qf = split(q * eq)
        kf = split(k * ek)
        da = split3(datt_ref[at, :])
        vs = split3(v_ref[at, :])
        for p in range(PAIRS):
            da2 = tuple(stacked_heads(lanes(part, p)) for part in da[:2])
            vp = tuple(lanes(part, p) for part in vs[:2])
            ds_ref[p] = jnp.where(mask, mm3(da2, vp, 1, 1), 0.0)

        @pl.when(opening(pl.program_id(1)) & (c == 0))
        def _():
            for p in range(PAIRS):
                da2 = tuple(stacked_heads(lanes(part, p)) for part in da)
                vp = tuple(lanes(part, p) for part in vs)
                ds_ref[p] = jnp.where(mask, mm6(da2, vp, 1, 1), 0.0)

        for p in range(PAIRS):
            da2 = tuple(stacked_heads(lanes(part, p)) for part in da[:2])
            ds2 = split(ds_ref[p])
            kp = tuple(lanes(part, p) for part in kf)
            qp = tuple(lanes(part, p) for part in qf)
            dqi_ref[:, p * LANES : (p + 1) * LANES] = merged_heads(mm3(ds2, kp)) * lanes(eq, p)
            q2 = tuple(stacked_heads(part) for part in qp)
            dki_ref[:, p * LANES : (p + 1) * LANES] = mm3(ds2, q2, 0, 0) * lanes(ek, p)
            s2 = split(s_ref[c, p])
            dv_ref[at, p * LANES : (p + 1) * LANES] = mm3(s2, da2, 0, 0)

        @pl.when(wild)
        def _():
            exact_back(q_ref, k_ref, cum_ref, ds_ref, base, dqi_ref, dki_ref)

        grow = jnp.exp(cum)
        for p in range(PAIRS):
            full = state_ref[c, p] + lanes(fade_ref[c, 0:1, :], p) * st_ref[p]
            full_ref[c, p] = full
            outer = mm3(tuple(lanes(part, p) for part in da[:2]), split(full))
            dq_ref[at, p * LANES : (p + 1) * LANES] = (
                dqi_ref[:, p * LANES : (p + 1) * LANES] + outer * lanes(grow, p)
            )
        dk_ref[at, :] = dki_ref[...]


def state_back_kernel(
    valid_ref,
    q_ref,
    k_ref,
    v_ref,
    cum_ref,
    slope_ref,
    datt_ref,
    dq_ref,
    dk_ref,
    dv_ref,
    full_ref,
    conv_ref,
    down_ref,
    up_ref,
    *rest,
):
    parts, (proj_ref, send_ref, keep_ref, dst_ref, dbias_ref, acc_ref, g_ref) = rest[:-7], rest[-7:]
    image, turn = pl.program_id(0), pl.program_id(1)
    tile = pl.num_programs(1) - 1 - turn

    @pl.when((image == 0) & (turn == 0))
    def _():
        dbias_ref[...] = jnp.zeros_like(dbias_ref)
        acc_ref[...] = jnp.zeros_like(acc_ref)

    @pl.when(turn == 0)
    def _():
        for p in range(PAIRS):
            dst_ref[p] = linked(parts, p)

    count = jnp.sum(valid_ref[...], axis=1, keepdims=True)
    keep = (
        lax.broadcasted_iota(jnp.int32, (CHUNK, WIDTH), 0) + tile * TILE
    )
    for c in reversed(range(TILE // CHUNK)):
        at = slice(c * CHUNK, (c + 1) * CHUNK)
        q = q_ref[at, :]
        k = k_ref[at, :]
        cum = cum_ref[at, :]
        final = cum[CHUNK - 1 : CHUNK, :]
        late = jnp.exp(final - cum)
        kd = k * late
        v = v_ref[at, :]
        qd = split(q * jnp.exp(cum))
        da = split(datt_ref[at, :])
        factor = jnp.exp(final)
        dk_parts, dv_parts, cross = [], [], []
        for p in range(PAIRS):
            old = dst_ref[p]
            pair = split(old)
            dk_parts.append(mm3(split(lanes(v, p)), pair))
            dv_parts.append(mm3(split(lanes(kd, p)), pair, 1, 1))
            leaving = lanes(factor, p) * full_ref[c, p] + block_diagonal(
                mm3(split(lanes(v, p)), split(lanes(kd, p)), 0, 0)
            )
            cross.append(jnp.sum(leaving * old, axis=0, keepdims=True))
            update = mm3(
                tuple(lanes(part, p) for part in da), tuple(lanes(part, p) for part in qd), 0, 0
            )
            dst_ref[p] = lanes(factor, p) * old + block_diagonal(update)
        dq = dq_ref[at, :]
        dk = dk_ref[at, :] + jnp.concatenate(dk_parts, axis=1) * late
        dv = dv_ref[at, :] + jnp.concatenate(dv_parts, axis=1)
        dgates = running_sum(q * dq - k * dk, True) + jnp.concatenate(cross, axis=1)
        dx = dgates * slope_ref[at, :]
        real = keep + c * CHUNK < count
        dk = jnp.where(real, dk, 0.0)
        dv = jnp.where(real, dv, 0.0)
        dbias_ref[...] += jnp.sum(dx.reshape(CHUNK // 8, 8, WIDTH), axis=0)
        proj_ref[at, 0:WIDTH] = dq
        proj_ref[at, WIDTH : 2 * WIDTH] = dk
        proj_ref[at, 2 * WIDTH : 3 * WIDTH] = dv
        proj_ref[at, 3 * WIDTH :] = dx
    conv = conv_ref[...]
    proj = split(proj_ref[...])
    acc_ref[...] += dot(
        wide((conv * sigmoid(conv)).T), jnp.concatenate([proj[0], proj[0], proj[1]], axis=0)
    )

    @pl.when((image == pl.num_programs(0) - 1) & (tile == 0))
    def _():
        for j in range(3):
            grad = acc_ref[:, j * WIDTH : (j + 1) * WIDTH]
            g_ref[j * WIDTH : (j + 1) * WIDTH, :] = (
                grad * HEAD_DIM ** (-0.5) if j == 0 else grad
            )
        grad = acc_ref[:, 3 * WIDTH :]
        base = 3 * WIDTH
        rank = up_ref.shape[0]
        g_ref[base:, :] = jnp.zeros_like(g_ref[base:, :])
        g_ref[base : base + rank, :] = mm6(split3(up_ref[...]), split3(grad), 1, 1)
        g_ref[base + rank : base + 2 * rank, :] = mm6(split3(down_ref[...]), split3(grad))
        g_ref[base + 2 * rank : base + 2 * rank + 1, :] = jnp.sum(
            dbias_ref[...], axis=0, keepdims=True
        )

        def lower(ref):
            ref[...] = g_ref[0 : ROWS // 2, :]

        def upper(ref):
            ref[...] = g_ref[ROWS // 2 :, :]

        halves_out(lower, upper, send_ref, keep_ref)


def hidden_kernel(proj_ref, conv_ref, w_ref, dconv_ref, wt3_ref):
    @pl.when((pl.program_id(0) == 0) & (pl.program_id(1) == 0))
    def _():
        wt3_ref[...] = across(w_ref[...])

    dhidden = dot(wide(proj_ref[...]), wt3_ref[...], 1, 1)
    conv = conv_ref[...]
    sig = sigmoid(conv)
    dconv_ref[...] = dhidden * (sig * (1.0 + conv * (1.0 - sig)))


def front_back_kernel(
    tok_ref,
    normed_ref,
    dconv_ref,
    top_ref,
    bot_ref,
    dnorm_ref,
    dmid_ref,
    mod_ref,
    taps_ref,
    mlp_ref,
    mix_ref,
    info_ref,
    grad_ref,
    rows_ref,
    dmod_ref,
    pad_ref,
    taps_acc_ref,
):
    length = dconv_ref.shape[0]
    image, i = pl.program_id(0), pl.program_id(1)

    @pl.when(i == 0)
    def _():
        taps_acc_ref[...] = jnp.zeros_like(taps_acc_ref)

    @pl.when(i == 0)
    def _():
        dmod_ref[...] = jnp.zeros_like(dmod_ref)
        pad_ref[0:GRID, :] = top_ref[...]
        pad_ref[pl.ds(length + GRID, GRID), :] = bot_ref[...]
        pad_ref[pl.ds(GRID, length), :] = dconv_ref[...]

    scale = 1.0 + mod_ref[1:2, :]

    def eights(x):
        return jnp.sum(x.reshape(x.shape[0] // 8, 8, WIDTH), axis=0)

    start = pl.multiple_of(i * TILE, TILE)
    rows = [pad_ref[pl.ds(start + (2 - a) * GRID, TILE), :] for a in range(3)]
    parts = [
        sum(taps_ref[3 * a + b : 3 * a + b + 1, :] * rows[a] for a in range(3))
        for b in range(3)
    ]
    dn = (
        shifted(parts[0], -1)
        + parts[1]
        + shifted(parts[2], 1)
        + dnorm_ref[...]
    )
    hat, rate = normalized(tok_ref[...])
    grad_ref[...] = dmid_ref[...] + normal_back(
        dn * scale, hat, rate
    )
    dmod_ref[0:1, :] += jnp.sum(dn, axis=0, keepdims=True)
    dmod_ref[1:2, :] += jnp.sum(dn * hat, axis=0, keepdims=True)
    own = rows[1]
    moved = [shifted(own, -1), own, shifted(own, 1)]
    for a in range(3):
        near = normed_ref[pl.ds(start + a * GRID, TILE), :]
        for b in range(3):
            taps_acc_ref[3 * a + b] += eights(moved[b] * near)

    @pl.when(i == pl.num_programs(1) - 1)
    def _():
        own = lax.axis_index("seq") == 0
        rows_ref[...] = jnp.zeros_like(rows_ref)
        rows_ref[0:6, :] = (dmod_ref[...] + mlp_ref[...] + mix_ref[...])[0:6, :]
        rows_ref[6:10, :] = jnp.where(own, info_ref[0:4, :], 0.0)
        for t in range(9):
            rows_ref[10 + t : 11 + t, :] = jnp.sum(taps_acc_ref[t], axis=0, keepdims=True)


def call(kernel, grid, ins, outs, scratch, flops=0, moved=0, prefetch=0, limit=24):
    return pl.pallas_call(
        kernel,
        grid_spec=pltpu.PrefetchScalarGridSpec(
            num_scalar_prefetch=prefetch,
            grid=grid,
            in_specs=ins,
            out_specs=[spec for spec, _ in outs],
            scratch_shapes=scratch,
        ),
        out_shape=[jax.ShapeDtypeStruct(shape, F32) for _, shape in outs],
        compiler_params=pltpu.CompilerParams(vmem_limit_bytes=limit * 1024 * 1024),
        cost_estimate=pl.CostEstimate(flops=4 * flops, bytes_accessed=4 * moved, transcendentals=0),
    )


def whole(shape):
    zeros = (0,) * len(shape)
    return pl.BlockSpec(shape, lambda *_: zeros, pipeline_mode=pl.Buffered(1))


def per_image(shape):
    zeros = (0,) * len(shape)
    return pl.BlockSpec((None,) + shape, lambda n, *_: (n,) + zeros)


def time_features(timesteps):
    half = FREQ // 2
    freqs = jnp.exp(-math.log(10000.0) * jnp.arange(half, dtype=F32) / half)
    angles = timesteps.astype(F32)[:, None] * freqs[None, :]
    return jnp.concatenate([jnp.cos(angles), jnp.sin(angles)], axis=1)


def halves(axis):
    return [1 << b for b in range(lax.axis_size(axis).bit_length() - 1)]


def swapped(x, axis, bit):
    return lax.ppermute(x, axis, [(i, i ^ bit) for i in range(lax.axis_size(axis))])


def is_high(axis, bit):
    return (lax.axis_index(axis) // bit) % 2


def step_kernel(items, *refs):
    ins, outs = refs[: 2 * len(items)], list(refs[2 * len(items) :])
    for n, (kind, link) in enumerate(items):
        own, got = ins[2 * n], ins[2 * n + 1]
        if kind == "sum":
            outs.pop(0)[...] = own[...] + got[...]
        elif kind == "join":
            out, size, high = outs.pop(0), own.shape[0], is_high(*link) == 1
            out[0:size] = jnp.where(high, got[...], own[...])
            out[size:] = jnp.where(high, own[...], got[...])
        else:
            half = own.shape[0] // 2
            high = is_high(*link)
            for side in (1 - high, high):
                start = side * half
                at = pl.ds(pl.multiple_of(start, 8) if half % 8 == 0 else start, half)
                outs.pop(0)[...] = own[at, :] + got[at, :]


def stepped(flows, got):
    items, arrays, shapes = [], [], []
    for flow, x in zip(flows, got):
        kind, link, own = flow.item()
        if kind == "split" and own.shape[0] % 16:
            flow.took_whole(own + x)
            continue
        items.append((flow, kind, link))
        arrays += [own, x]
        if kind == "split":
            shapes += [(own.shape[0] // 2, WIDTH)] * 2
        else:
            shapes.append((own.shape[0] * (2 if kind == "join" else 1),) + own.shape[1:])
    if not items:
        return
    outs = call(
        functools.partial(step_kernel, [item[1:] for item in items]),
        (1,),
        [whole(x.shape) for x in arrays],
        [(whole(shape), shape) for shape in shapes],
        [],
        flops=sum(x.size for x in arrays),
        moved=8 * sum(x.size for x in arrays),
        limit=24,
    )(*arrays)
    outs = list(outs)
    for flow, kind, _ in items:
        flow.took(*(outs.pop(0) for _ in range(2 if kind == "split" else 1)))


class Flow:
    def __init__(self, sent, keep, order):
        self.sent, self.keep = sent, keep
        self.order, self.used = list(order), []

    def busy(self):
        return bool(self.order)

    def send(self):
        return self.sent

    def link(self):
        return self.order[0]

    def item(self):
        self.used.append(self.order.pop(0))
        if self.order:
            return "split", self.order[0], self.keep
        return "sum", None, self.keep

    def took(self, *new):
        if len(new) == 2:
            self.sent, self.keep = new
        else:
            (self.keep,) = new

    def now(self):
        return self.sent if self.order else self.keep

    def took_whole(self, total):
        half = total.shape[0] // 2
        high = is_high(*self.order[0])
        self.sent = lax.dynamic_slice_in_dim(total, (1 - high) * half, half)
        self.keep = lax.dynamic_slice_in_dim(total, high * half, half)


class Spread:
    def __init__(self, x, used):
        self.x, self.used = x[None], list(used)

    def busy(self):
        return len(self.used) > 1

    def send(self):
        return self.x

    def link(self):
        return self.used[-1]

    def item(self):
        return "join", self.used.pop(), self.x

    def took(self, new):
        self.x = new

    def now(self):
        return self.x


class Rows:
    def __init__(self, x, sums, joins):
        self.x, self.sums, self.joins = x, list(sums), list(joins)

    def busy(self):
        return bool(self.sums or self.joins)

    def send(self):
        return self.x

    def link(self):
        return self.sums[0] if self.sums else self.joins[0]

    def item(self):
        if self.sums:
            self.sums.pop(0)
            return "sum", None, self.x
        return "join", self.joins.pop(0), self.x

    def took(self, new):
        self.x = new

    def now(self):
        return self.x


class Paired:
    def __init__(self, sent, keep, link):
        self.sent, self.keep, self.at, self.got = sent, keep, link, None

    def busy(self):
        return self.got is None

    def send(self):
        return self.sent

    def link(self):
        return self.at


def fork_kernel(parts, *refs):
    count = (len(refs) - 1 - 2 * len(parts)) // 2
    ins, outs, total = refs[: 2 * count], list(refs[2 * count : -1]), refs[-1]
    at = 0
    for n in range(count):
        rows = ins[2 * n].shape[0]
        total[at : at + rows, :] = ins[2 * n][...] + ins[2 * n + 1][...]
        at += rows
    for first, rows, link in parts:
        high = is_high(*link)
        for side in (1 - high, high):
            start = side * (rows // 2) + first
            outs.pop(0)[...] = total[pl.ds(pl.multiple_of(start, 8), rows // 2), :]


def forked(pairs, cuts, orders):
    rows = sum(cuts)
    starts = [sum(cuts[:n]) for n in range(len(cuts))]
    parts = [(start, cut, order[0]) for start, cut, order in zip(starts, cuts, orders)]
    arrays = [x for pair in pairs for x in (pair.keep, pair.got)]
    shapes = [(part[1] // 2, WIDTH) for part in parts for _ in range(2)]
    outs = call(
        functools.partial(fork_kernel, parts),
        (1,),
        [whole(x.shape) for x in arrays],
        [(whole(shape), shape) for shape in shapes],
        [pltpu.VMEM((rows, WIDTH), F32)],
        flops=rows * WIDTH,
        moved=12 * rows * WIDTH,
        limit=24,
    )(*arrays)
    return [Flow(outs[2 * n], outs[2 * n + 1], order) for n, order in enumerate(orders)]


def beside(flows, first, kernel):
    flows = [flow for flow in flows if flow.busy()]
    first, *sends = lax.optimization_barrier((first, *(flow.send() for flow in flows)))
    got = [swapped(x, *flow.link()) for flow, x in zip(flows, sends)]
    outs = kernel(first)
    head, *got = lax.optimization_barrier((outs[0], *got))
    for flow, x in zip(flows, got):
        if isinstance(flow, Paired):
            flow.got = x
    rest = [(flow, x) for flow, x in zip(flows, got) if not isinstance(flow, Paired)]
    stepped([flow for flow, _ in rest], [x for _, x in rest])
    return [head] + list(outs[1:])


def halves_out(lower, upper, send_ref, keep_ref):
    core = lax.axis_index("seq") % 2

    @pl.when(core == 0)
    def _():
        lower(keep_ref)
        upper(send_ref)

    @pl.when(core == 1)
    def _():
        lower(send_ref)
        upper(keep_ref)


def move_first(outs):
    return list(outs[1:]) + [outs[0]]


def messages(message, backward):
    size = lax.axis_size("seq")
    got = []
    for far in range(1, size):
        pairs = [(i, i + far) for i in range(size - far)]
        if backward:
            pairs = [(j, i) for i, j in pairs]
        got.append(lax.ppermute(message, "seq", pairs))
    return got


def plan(early_rows, pieces, units):
    late_rows = tuple(total // pieces for total in LATE)
    moves = []

    def place(kind, half, at):
        if kind == 0:
            if at >= units:
                return 2 + half, at - units, 0, units + WIDTH - at
            if half == 0:
                return 0, at % WIDTH, at // WIDTH, WIDTH - at % WIDTH
            return 1, at, 0, units - at
        row = half * (ROWS // 2) + at
        block = min(row // WIDTH, 3)
        room = ROWS // 2 - at
        return 4 + block, row - block * WIDTH, 0, min(room, WIDTH - row % WIDTH) if block < 3 else room

    for half in range(2):
        for kind in range(2):
            at = 0
            for flow in range(len(early_rows)):
                rows = early_rows[flow] if kind == 0 else late_rows[flow]
                base = 0 if kind == 0 else early_rows[flow]
                for piece in range(pieces):
                    done = 0
                    while done < rows:
                        out, row, block, room = place(kind, half, at)
                        span = min(rows - done, room)
                        moves.append((half, flow, piece, base + done, out, row, block, span))
                        done, at = done + span, at + span
    return moves


def assemble_kernel(moves, pieces, lasts, core, *refs):
    count = len(lasts)
    near, other, near_core, other_core = (refs[n * count : (n + 1) * count] for n in range(4))
    outs = refs[4 * count :]
    mine = is_high(*core)
    for half, flow, piece, row, out, start, block, span in moves:
        side, index = piece // (pieces // 2), piece % (pieces // 2)
        at = (index, slice(row, row + span), slice(None))
        own = is_high(*lasts[flow]) == side
        here = jnp.where(own, near[flow][at], other[flow][at])
        there = jnp.where(own, near_core[flow][at], other_core[flow][at])
        outs[out][start : start + span, block * WIDTH : (block + 1) * WIDTH] = jnp.where(
            mine == half, here, there
        )


def assembled(near, other, near_core, other_core, lasts, core, early, units):
    early_rows = tuple(flow.keep.shape[0] for flow in early)
    pieces = 2 * near[0].shape[0]
    moves = plan(early_rows, pieces, units)
    square = (WIDTH, WIDTH)
    shapes = [(WIDTH, units), (units, WIDTH)] + [square] * 5 + [(ROWS - 3 * WIDTH, WIDTH)]
    arrays = near + other + near_core + other_core
    return call(
        functools.partial(assemble_kernel, moves, pieces, lasts, core),
        (1,),
        [whole(x.shape) for x in arrays],
        [(whole(shape), shape) for shape in shapes],
        [],
        moved=4 * 4 * sum(x.size for x in near),
        limit=40,
    )(*arrays)


def body(
    tokens,
    valid_mask,
    timesteps,
    class_ids,
    time_first,
    time_second,
    class_table,
    ada_weight,
    ada_bias,
    conv_taps,
    query_proj,
    key_proj,
    value_proj,
    decay_down,
    decay_up,
    decay_bias,
    gate_proj,
    out_proj,
    mlp_up,
    mlp_down,
    cotangent,
):
    count, length, width = tokens.shape
    size, mine = lax.axis_size("seq"), lax.axis_index("seq")
    tiles, chunks = length // TILE, length // CHUNK
    per_tile = TILE // CHUNK
    up_pairs = [(i, i + 1) for i in range(size - 1)]
    down_pairs = [(j, i) for i, j in up_pairs]
    seq_bits = [("seq", bit) for bit in halves("seq")]
    img_bits = [("img", bit) for bit in halves("img")]
    core, order_a = seq_bits[0], seq_bits[1:] + img_bits
    order_b = img_bits[:2] + seq_bits[1:] + img_bits[2:]
    order_c = img_bits[2:] + seq_bits[1:] + img_bits[:2]
    orders = (order_a, order_b, order_c)

    def borders(x):
        return (
            lax.ppermute(x[:, length - GRID :], "seq", up_pairs),
            lax.ppermute(x[:, :GRID], "seq", down_pairs),
        )

    above, below = borders(tokens)

    square = (width, width)
    row = (length, width)
    dense = 2 * 3 * count * length * width
    each = 4 * count * length * width
    features = time_features(timesteps)
    mod_spec = per_image((6, width))
    modul, info = call(
        condition_kernel,
        (count,),
        [
            per_image((1, FREQ)),
            whole(time_first.shape),
            whole(time_second.shape),
            pl.BlockSpec((8, width), lambda n, ids: (ids[n] // 8, 0)),
            whole(ada_weight.shape),
            whole((6 * width,)),
        ],
        [
            (mod_spec, (count, 6, width)),
            (per_image((8, width)), (count, 8, width)),
        ],
        [],
        flops=1000000,
        moved=4 * 6 * width * width,
        prefetch=1,
        limit=60,
    )(class_ids, features[:, None], time_first, time_second, class_table, ada_weight, ada_bias)

    valid = valid_mask[:, None]
    valid_spec = per_image((1, length))
    message_shape = (PAIRS, HEAD_DIM + 8, LANES)
    def tiled(shape=(TILE, width)):
        return pl.BlockSpec((None,) + shape, lambda n, i: (n, i, 0))

    tile_row = (tiled(), (count,) + row)
    pair_spec = pl.BlockSpec(
        (None, per_tile, PAIRS, LANES, LANES), lambda n, i: (n, i, 0, 0, 0)
    )
    state_spec = pl.BlockSpec((None, PAIRS, LANES, LANES), lambda n, i: (n, 0, 0, 0))
    state_shape = (count, PAIRS, LANES, LANES)
    score_shape = (count, chunks, PAIRS, 2 * CHUNK, CHUNK)
    score_spec = pl.BlockSpec(
        (None, per_tile, PAIRS, 2 * CHUNK, CHUNK), lambda n, i: (n, i, 0, 0, 0)
    )
    normed_spec = per_image((length + 2 * GRID, width))
    message_spec = per_image(message_shape)
    fade_spec = pl.BlockSpec((None, per_tile, 8, width), lambda n, i: (n, i, 0, 0))
    (
        weights,
        normed,
        conv,
        query,
        keys,
        values,
        cumul,
        slope,
        far,
        states,
        fades,
        message,
    ) = call(
        front_kernel,
        (count, tiles),
        [
            per_image(row),
            per_image((GRID, width)),
            per_image((GRID, width)),
            valid_spec,
            mod_spec,
            whole((9, width)),
            whole(square),
            whole(square),
            whole(square),
            whole(decay_up.shape),
            whole(decay_up.shape),
            whole((width,)),
        ],
        [
            (whole((width, 4 * width)), (width, 4 * width)),
            (per_image((length + 2 * GRID, width)), (count, length + 2 * GRID, width)),
        ]
        + [tile_row] * 7
        + [
            (pair_spec, (count, chunks, PAIRS, LANES, LANES)),
            (fade_spec, (count, chunks, 8, width)),
            (message_spec, (count,) + message_shape),
        ],
        [
            pltpu.VMEM((6 * width, 4 * width), BF16),
            pltpu.VMEM((TILE, 4 * width), F32),
            pltpu.VMEM((PAIRS, LANES, LANES), F32),
            pltpu.VMEM((8, width), F32),
        ],
        flops=dense * 4 * width,
        moved=each * 10,
    )(
        tokens,
        above,
        below,
        valid,
        modul,
        conv_taps,
        query_proj,
        key_proj,
        value_proj,
        decay_down.T,
        decay_up,
        decay_bias,
    )

    forward_parts = messages(message, False)
    inner, scores, gate_in = call(
        inner_kernel,
        (count, tiles),
        [tiled()] * 4 + [pair_spec, normed_spec, whole(square)],
        [tile_row, (score_spec, score_shape), tile_row],
        [pltpu.VMEM((3 * width, width), BF16), pltpu.VMEM((PAIRS, 2 * CHUNK, CHUNK), F32)],
        flops=dense * 2 * width,
        moved=each * 9,
    )(query, keys, values, cumul, states, normed, gate_proj)

    middle, branch, attended, state_in = call(
        mix_kernel,
        (count, tiles),
        [tiled()] * 4 + [mod_spec, whole(square)] + [message_spec] * (size - 1),
        [tile_row] * 3 + [(state_spec, state_shape)],
        [pltpu.VMEM((3 * width, width), BF16)],
        flops=dense * 2 * width,
        moved=each * 7,
    )(inner, far, tokens, gate_in, modul, out_proj, *forward_parts)

    dmod_spec = per_image((8, width))
    dmod_out = (dmod_spec, (count, 8, width))

    units = mlp_up.shape[1]
    block_out, dmid, dmod_mlp, mlp_sent, mlp_kept = call(
        mlp_kernel,
        (count, tiles),
        [tiled(), tiled(), mod_spec, whole(mlp_up.shape), whole(mlp_down.shape)],
        [tile_row] * 2 + [dmod_out] + [(whole((units, width)), (units, width))] * 2,
        [
            pltpu.VMEM((3 * width, units), BF16),
            pltpu.VMEM((width, 3 * units), BF16),
            pltpu.VMEM((3 * units, width), BF16),
            pltpu.VMEM((units, 3 * width), BF16),
            pltpu.VMEM((width, units), F32),
            pltpu.VMEM((width, units), F32),
        ],        flops=dense * 6 * units,
        moved=each * 8,
        limit=40,
    )(middle, cotangent, modul, mlp_up, mlp_down)

    mlp_pair = Paired(mlp_sent, mlp_kept, core)
    datt, dnorm, mix_sent, mix_kept, dmod_mix, d_message = beside([mlp_pair], dmid, lambda x: call(
        mix_back_kernel,
        (count, tiles),
        [tiled()] * 5
        + [normed_spec, mod_spec, message_spec, whole(square), whole(square)],
        [tile_row] * 2
        + [(whole(square), square)] * 2
        + [dmod_out]
        + [(message_spec, (count,) + message_shape)],
        [
            pltpu.VMEM((2 * width, width), F32),
            pltpu.VMEM((width, 3 * width), BF16),
            pltpu.VMEM((width, 3 * width), BF16),
            pltpu.VMEM((PAIRS, LANES, LANES), F32),
        ],
        flops=dense * 5 * width,
        moved=each * 8,
        limit=60,
    )(x, branch, attended, gate_in, far, normed, modul, message, out_proj, gate_proj))
    mix_pair = Paired(mix_sent, mix_kept, core)
    d_message, datt = lax.optimization_barrier((d_message, datt))
    backward_parts = messages(d_message, True)

    dquery, dkeys, dvalues, full = beside([mix_pair], datt, lambda x: call(
        inner_back_kernel,
        (count, tiles),
        [tiled()] * 5 + [score_spec, pair_spec, fade_spec, state_spec],
        [tile_row] * 3 + [(pair_spec, (count, chunks, PAIRS, LANES, LANES))],
        [
            pltpu.VMEM((PAIRS, 2 * CHUNK, CHUNK), F32),
            pltpu.VMEM((CHUNK, width), F32),
            pltpu.VMEM((CHUNK, width), F32),
        ],
        flops=dense * 2 * width,
        moved=each * 12,
        limit=60,
    )(query, keys, values, cumul, x, scores, states, fades, state_in))

    early = forked([mlp_pair, mix_pair], EARLY, orders)

    def turned(shape=(TILE, width)):
        return pl.BlockSpec((None,) + shape, lambda n, i: (n, tiles - 1 - i, 0))

    dproj, late_sent, late_kept = beside(early, dquery, lambda x: call(
        state_back_kernel,
        (count, tiles),
        [valid_spec]
        + [turned()] * 9
        + [
            pl.BlockSpec(
                (None, per_tile, PAIRS, LANES, LANES),
                lambda n, i: (n, tiles - 1 - i, 0, 0, 0),
            ),
            turned(),
            whole(decay_up.shape),
            whole(decay_up.shape),
        ]
        + [message_spec] * (size - 1),
        [
            (turned((TILE, 4 * width)), (count, length, 4 * width)),
            (whole((ROWS // 2, width)), (ROWS // 2, width)),
            (whole((ROWS // 2, width)), (ROWS // 2, width)),
        ],
        [
            pltpu.VMEM((PAIRS, LANES, LANES), F32),
            pltpu.VMEM((8, width), F32),
            pltpu.VMEM((width, 4 * width), F32),
            pltpu.VMEM((ROWS, width), F32),
        ],
        flops=dense * 2 * width,
        moved=each * 14,
        limit=60,
    )(
        valid,
        query,
        keys,
        values,
        cumul,
        slope,
        datt,
        x,
        dkeys,
        dvalues,
        full,
        conv,
        decay_down.T,
        decay_up,
        *backward_parts,
    ))
    late_pair = Paired(late_sent, late_kept, core)
    (dconv,) = beside(early + [late_pair], late_kept, lambda x: call(
        hidden_kernel,
        (count, tiles),
        [tiled((TILE, 4 * width)), tiled(), whole((width, 4 * width))],
        [tile_row],
        [pltpu.VMEM((width, 3 * 4 * width), BF16)],
        flops=dense * 4 * width,
        moved=each * 7,
    )(lax.optimization_barrier((dproj, x))[0], conv, weights))
    d_above, d_below = borders(dconv)
    late = forked([late_pair], LATE, orders)
    rows, tokens_grad = beside(early + late, dconv, lambda x: move_first(call(
        front_back_kernel,
        (count, tiles),
        [
            tiled(),
            per_image((length + 2 * GRID, width)),
            per_image(row),
            per_image((GRID, width)),
            per_image((GRID, width)),
            tiled(),
            tiled(),
            mod_spec,
            whole((9, width)),
            dmod_spec,
            dmod_spec,
            dmod_spec,
        ],
        [
            tile_row,
            (per_image((24, width)), (count, 24, width)),
        ],
        [
            pltpu.VMEM((8, width), F32),
            pltpu.VMEM((length + 2 * GRID, width), F32),
            pltpu.VMEM((9, 8, width), F32),
        ],
        flops=count * length * width * 100,
        moved=each * 6,
    )(
        tokens, normed, x, d_above, d_below, dnorm, dmid, modul, conv_taps, dmod_mlp, dmod_mix, info
    )))

    flow_r = Rows(rows, seq_bits, img_bits)
    last = jnp.zeros((), F32)
    spreads = [None] * len(orders)
    while True:
        round_of = [flow for flow in late + early + [flow_r] + spreads if flow and flow.busy()]
        if not round_of:
            break
        for flow in round_of:
            got, last = lax.optimization_barrier((swapped(flow.send(), *flow.link()), last))
            stepped([flow], [got])
            last = flow.now()
        for n, (one, two) in enumerate(zip(early, late)):
            if spreads[n] is None and not one.busy() and not two.busy():
                spreads[n] = Spread(jnp.concatenate([one.keep, two.keep]), one.used)
    rows = flow_r.x
    images = rows.shape[0]
    ids = rows[:, 9, 0].astype(jnp.int32)
    lasts = tuple(flow.link() for flow in spreads)
    rows, *near = lax.optimization_barrier((rows, *(flow.x for flow in spreads)))
    g_first, g_second, g_class, g_ada, g_ada_bias, g_taps = call(
        embed_kernel,
        (1,),
        [
            whole(rows.shape),
            whole(ada_weight.shape),
            whole(time_second.shape),
        ],
        [
            (whole(shape), shape)
            for shape in (
                time_first.shape,
                time_second.shape,
                class_table.shape,
                ada_weight.shape,
                (6 * width,),
                (9, width),
            )
        ],
        [],
        flops=images * 2 * 3 * width * width * 14,
        moved=4 * width * width * 20,
        prefetch=1,
    )(ids, rows, ada_weight, time_second)
    far_ones = [swapped(x, *last) for x, last in zip(near, lasts)]
    near_core = [swapped(x, *core) for x in near]
    g_ada, *far_ones = lax.optimization_barrier((g_ada, *far_ones))
    far_core = [swapped(x, *core) for x in far_ones]
    g_up, g_down, g_out, g_gate, g_query, g_key, g_value, g_small = assembled(
        near, far_ones, near_core, far_core, lasts, core, early, units
    )

    rank = decay_up.shape[0]
    return (
        block_out,
        tokens_grad,
        g_first,
        g_second,
        g_class,
        g_ada,
        g_ada_bias,
        g_taps,
        g_query,
        g_key,
        g_value,
        g_small[:rank].T,
        g_small[rank : 2 * rank],
        g_small[2 * rank],
        g_gate,
        g_out,
        g_up,
        g_down,
    )


def solution(mesh):
    image, shared = P("img", "seq", None), P()
    return jax.shard_map(
        body,
        mesh=mesh,
        in_specs=(image, P("img", "seq"), P("img"), P("img")) + (shared,) * 16 + (image,),
        out_specs=(image, image) + (shared,) * 16,
        check_vma=False,
    )
```

```python
import functools
import math

import jax
import jax.numpy as jnp
from jax import lax
from jax.experimental import pallas as pl
from jax.experimental.pallas import tpu as pltpu
from jax.sharding import PartitionSpec as P

HEADS = 6
HEAD_DIM = 64
CLASSES = 1000
FREQ = 256
GRID = 64
WIDTH = 384
PAIRS = 3
LANES = 128
CHUNK = 128
TILE = 256
ROWS = 1280
EARLY = (768, 768, 384)
LATE = (384, 256, 0)
SPAN = 120.0
HIGH = lax.Precision.HIGHEST
F32 = jnp.float32
BF16 = jnp.bfloat16
GELU_C = math.sqrt(2.0 / math.pi)


def product(left, right):
    return jnp.dot(left, right, precision=HIGH, preferred_element_type=F32)


def dot(a, b, ca=1, cb=0):
    return lax.dot_general(a, b, (((ca,), (cb,)), ((), ())), preferred_element_type=F32)


def split(x):
    high = x.astype(BF16)
    return high, (x - high.astype(F32)).astype(BF16)


def mm3(a, b, ca=1, cb=0):
    return dot(a[0], b[0], ca, cb) + dot(a[1], b[0], ca, cb) + dot(a[0], b[1], ca, cb)


def split3(x):
    high = x.astype(BF16)
    rest = x - high.astype(F32)
    middle = rest.astype(BF16)
    return high, middle, (rest - middle.astype(F32)).astype(BF16)


def mm6(a, b, ca=1, cb=0):
    terms = ((0, 0), (0, 1), (1, 0), (1, 1), (0, 2), (2, 0))
    return sum(dot(a[i], b[j], ca, cb) for i, j in reversed(terms))


def wide6(x):
    h, m, l = split3(x)
    return jnp.concatenate([h, h, m, m, h, l], axis=1)


def tall6(w):
    h, m, l = split3(w)
    return jnp.concatenate([h, m, h, m, l, h], axis=0)


def wide3(x):
    high, low = split(x)
    return jnp.concatenate([high, high, low], axis=1)


def wide(x):
    high, low = split(x)
    return jnp.concatenate([high, low, high], axis=1)


def tall(w):
    high, low = split(w)
    return jnp.concatenate([high, high, low], axis=0)


def across(w):
    high, low = split(w)
    return jnp.concatenate([high, high, low], axis=1)


def lanes(x, p):
    return x[..., p * LANES : (p + 1) * LANES]


def first_half(shape):
    return lax.broadcasted_iota(jnp.int32, shape, len(shape) - 1) < HEAD_DIM


def block_diagonal(square):
    rows = lax.broadcasted_iota(jnp.int32, square.shape, 0) < HEAD_DIM
    return jnp.where(rows == first_half(square.shape), square, 0.0)


def head_mean(x):
    rows = lax.broadcasted_iota(jnp.int32, (LANES, LANES), 0) < HEAD_DIM
    ones = jnp.where(rows == first_half((LANES, LANES)), 1.0 / HEAD_DIM, 0.0).astype(BF16)
    high, low = split(x)
    return dot(
        jnp.concatenate([high, low], axis=1), jnp.concatenate([ones, ones], axis=0)
    )


def head_means(x):
    return jnp.concatenate([head_mean(lanes(x, p)) for p in range(PAIRS)], axis=1)


def stacked_heads(x):
    keep = first_half(x.shape)
    zero = jnp.zeros_like(x)
    return jnp.concatenate([jnp.where(keep, x, zero), jnp.where(keep, zero, x)], axis=0)


def merged_heads(x):
    rows = x.shape[0] // 2
    return jnp.where(first_half((rows, LANES)), x[:rows], x[rows:])


def sigmoid(x):
    return 1.0 / (1.0 + jnp.exp(-x))


def shifted(x, step):
    rows = x.shape[0]
    column = lax.broadcasted_iota(jnp.int32, x.shape, 0) % GRID
    if step == 1:
        return jnp.where(column == 0, 0.0, pltpu.roll(x, 1, 0))
    return jnp.where(column == GRID - 1, 0.0, pltpu.roll(x, rows - 1, 0))


def normalized(x):
    center = x - jnp.mean(x, axis=-1, keepdims=True)
    rate = lax.rsqrt(jnp.mean(center * center, axis=-1, keepdims=True) + 1e-06)
    return center * rate, rate


def normal_back(dhat, hat, rate):
    return rate * (
        dhat
        - jnp.mean(dhat, axis=-1, keepdims=True)
        - hat * jnp.mean(dhat * hat, axis=-1, keepdims=True)
    )


def triangle(size, upper):
    rows = lax.broadcasted_iota(jnp.int32, (size, size), 0)
    cols = lax.broadcasted_iota(jnp.int32, (size, size), 1)
    return jnp.where(cols >= rows if upper else cols <= rows, 1.0, 0.0).astype(BF16)


def running_sum(x, upper):
    tri = triangle(x.shape[0], upper)
    high = x.astype(BF16)
    rest = x - high.astype(F32)
    middle = rest.astype(BF16)
    low = (rest - middle.astype(F32)).astype(BF16)
    return dot(tri, high) + dot(tri, middle) + dot(tri, low)


def opening(tile):
    return (lax.axis_index("seq") == 0) & (tile == 0)


def spread(compact):
    keep = first_half(compact.shape)
    return jnp.concatenate(
        [jnp.where(keep, compact, 0.0), jnp.where(keep, 0.0, compact)], axis=0
    )


def linked(parts, p):
    total = jnp.zeros((HEAD_DIM, LANES), F32)
    for part in reversed(parts):
        total = part[p, 0:HEAD_DIM, :] + part[p, HEAD_DIM : HEAD_DIM + 1, :] * total
    return spread(total)


def as_column(row):
    return jnp.broadcast_to(row, (8, row.shape[1])).T[:, 0:1]


def applied(row, w_ref):
    return jnp.sum(as_column(row) * w_ref[...], axis=0, keepdims=True)


def condition_kernel(ids_ref, feat_ref, first_w_ref, second_w_ref, row_ref, ada_ref, bias_ref, mod_ref, info_ref):
    features = feat_ref[...]
    first = applied(features, first_w_ref)
    embed = applied(first * sigmoid(first), second_w_ref)
    at = lax.broadcasted_iota(jnp.int32, row_ref.shape, 0) == ids_ref[pl.program_id(0)] % 8
    embed = embed + jnp.sum(jnp.where(at, row_ref[...], 0.0), axis=0, keepdims=True)
    modul = applied(embed * sigmoid(embed), ada_ref)
    for j in range(6):
        at = slice(j * WIDTH, (j + 1) * WIDTH)
        mod_ref[j : j + 1, :] = modul[:, at] + bias_ref[at][None, :]
    info_ref[...] = jnp.zeros_like(info_ref)
    info_ref[0:1, 0:FREQ] = features
    info_ref[1:2, :] = first
    info_ref[2:3, :] = embed
    info_ref[3:4, :] = jnp.full((1, WIDTH), ids_ref[pl.program_id(0)], jnp.int32).astype(F32)


def embed_kernel(
    ids_ref, rows_ref, ada_ref, second_ref, gf_ref, gs_ref, gc_ref, ga_ref, gb_ref, gt_ref
):
    images = rows_ref.shape[0]
    features, first, embed = rows_ref[:, 6, 0:FREQ], rows_ref[:, 7, :], rows_ref[:, 8, :]
    gt_ref[...] = jnp.sum(rows_ref[:, 10:19, :], axis=0)

    def silu_back(x, grad):
        sig = sigmoid(x)
        return grad * (sig * (1.0 + x * (1.0 - sig)))

    act = split((embed * sigmoid(embed)).T)
    dembed = jnp.zeros((images, WIDTH), F32)
    for j in range(6):
        at = slice(j * WIDTH, (j + 1) * WIDTH)
        grad = rows_ref[:, j, :]
        dmod = split(grad)
        ga_ref[:, at] = mm3(act, dmod)
        gb_ref[at] = jnp.sum(grad, axis=0)
        dembed = dembed + mm3(dmod, split(ada_ref[:, at]), 1, 1)
    dembed = silu_back(embed, dembed)
    gc_ref[...] = jnp.zeros_like(gc_ref)

    def put(n, carry):
        mine = lax.broadcasted_iota(jnp.int32, (images, WIDTH), 0) == n
        row = jnp.sum(jnp.where(mine, dembed, 0.0), axis=0, keepdims=True)
        gc_ref[pl.ds(ids_ref[n], 1), :] += row
        return carry

    lax.fori_loop(0, images, put, 0)
    de = split(dembed)
    gs_ref[...] = mm3(split((first * sigmoid(first)).T), de)
    dfirst = silu_back(first, mm3(de, split(second_ref[...]), 1, 1))
    gf_ref[...] = mm3(split(features.T), split(dfirst))


def front_kernel(
    tok_ref,
    top_ref,
    bot_ref,
    valid_ref,
    mod_ref,
    taps_ref,
    wq_ref,
    wk_ref,
    wv_ref,
    down_ref,
    up_ref,
    bias_ref,
    w_ref,
    normed_ref,
    conv_ref,
    q_ref,
    k_ref,
    v_ref,
    cum_ref,
    slope_ref,
    far_ref,
    state_ref,
    fade_ref,
    out_ref,
    w3_ref,
    proj_ref,
    st_ref,
    dev_ref,
):
    image, i = pl.program_id(0), pl.program_id(1)
    length = tok_ref.shape[0]

    @pl.when((image == 0) & (i == 0))
    def _():
        w_ref[:, 0:WIDTH] = wq_ref[...] * HEAD_DIM ** (-0.5)
        w_ref[:, WIDTH : 2 * WIDTH] = wk_ref[...]
        w_ref[:, 2 * WIDTH : 3 * WIDTH] = wv_ref[...]
        w_ref[:, 3 * WIDTH :] = mm6(split3(down_ref[...]), split3(up_ref[...]), 0, 0)
        w3_ref[...] = tall6(w_ref[...])

    real = jnp.sum(valid_ref[...], axis=1, keepdims=True)
    shift = mod_ref[0:1, :]
    scale = 1.0 + mod_ref[1:2, :]

    def modulated(x):
        return normalized(x)[0] * scale + shift

    @pl.when(i == 0)
    def _():
        normed_ref[0:GRID, :] = jnp.where(
            lax.axis_index("seq") == 0, 0.0, modulated(top_ref[...])
        )
        normed_ref[pl.ds(length + GRID, GRID), :] = jnp.where(
            lax.axis_index("seq") == lax.axis_size("seq") - 1, 0.0, modulated(bot_ref[...])
        )
        for at in range(0, length, TILE):
            normed_ref[GRID + at : GRID + at + TILE, :] = modulated(tok_ref[at : at + TILE, :])
        st_ref[...] = jnp.zeros_like(st_ref)
        dev_ref[...] = jnp.zeros_like(dev_ref)

    start = pl.multiple_of(i * TILE, TILE)
    rows = [normed_ref[pl.ds(start + a * GRID, TILE), :] for a in range(3)]
    parts = [
        sum(taps_ref[3 * a + b : 3 * a + b + 1, :] * rows[a] for a in range(3))
        for b in range(3)
    ]
    conv = shifted(parts[0], 1) + parts[1] + shifted(parts[2], -1)
    conv_ref[...] = conv
    hidden = conv * sigmoid(conv)
    first = opening(i)

    @pl.when(first)
    def _():
        proj_ref[...] = dot(wide6(hidden), w3_ref[...])

    @pl.when(jnp.logical_not(first))
    def _():
        proj_ref[...] = dot(wide3(hidden), w3_ref[0 : 3 * WIDTH, :])

    proj = proj_ref[...]
    keep = (
        lax.broadcasted_iota(jnp.int32, (TILE, WIDTH), 0) + start < real
    )
    q = proj[:, :WIDTH]
    k = jnp.where(keep, proj[:, WIDTH : 2 * WIDTH], 0.0)
    v = jnp.where(keep, proj[:, 2 * WIDTH : 3 * WIDTH], 0.0)
    x = proj[:, 3 * WIDTH :] + bias_ref[...][None, :]
    small = jnp.exp(-jnp.abs(x))
    gates = jnp.where(keep, (jnp.minimum(x, 0.0) - jnp.log1p(small)) * (1.0 / 16.0), 0.0)
    slope = jnp.where(x >= 0, small, 1.0) / (1.0 + small)
    slope_ref[...] = jnp.where(keep, slope * (1.0 / 16.0), 0.0)
    q_ref[...] = q
    k_ref[...] = k
    v_ref[...] = v
    for c in range(TILE // CHUNK):
        at = slice(c * CHUNK, (c + 1) * CHUNK)
        cum = running_sum(gates[at], False)
        cum_ref[at, :] = cum
        final = cum[CHUNK - 1 : CHUNK, :]
        dev = dev_ref[0:1, :]
        far_ref[at, :] = q[at] * jnp.exp(cum + dev)
        fade_ref[c] = jnp.broadcast_to(jnp.exp(dev), (8, WIDTH))
        kd = k[at] * jnp.exp(final - cum)
        factor = jnp.exp(final)
        for p in range(PAIRS):
            state_ref[c, p] = st_ref[p]
            update = mm3(split(lanes(v[at], p)), split(lanes(kd, p)), 0, 0)
            st_ref[p] = lanes(factor, p) * st_ref[p] + block_diagonal(update)
        dev_ref[...] = dev_ref[...] + final

    @pl.when(i == pl.num_programs(1) - 1)
    def _():
        for p in range(PAIRS):
            out_ref[p, 0:HEAD_DIM, :] = st_ref[p, 0:HEAD_DIM, :] + st_ref[p, HEAD_DIM:, :]
            out_ref[p, HEAD_DIM:, :] = jnp.exp(lanes(dev_ref[...], p))


def exact_scores(q_ref, k_ref, cum_ref, base, s_ref):
    q = q_ref[pl.ds(base, CHUNK), :]
    cum = cum_ref[pl.ds(base, CHUNK), :]
    s_ref[...] = jnp.zeros_like(s_ref)

    def step(j, carry):
        key = k_ref[pl.ds(base + j, 1), :]
        weight = jnp.exp(jnp.minimum(cum - cum_ref[pl.ds(base + j, 1), :], 0.0))
        terms = q * key * weight
        for p in range(PAIRS):
            column = jnp.sum(stacked_heads(lanes(terms, p)), axis=1, keepdims=True)
            at = lax.broadcasted_iota(jnp.int32, (2 * CHUNK, CHUNK), 1) == j
            s_ref[p] = jnp.where(at, column, s_ref[p])
        return carry

    lax.fori_loop(0, CHUNK, step, 0)


def causal_two():
    rows = lax.broadcasted_iota(jnp.int32, (2 * CHUNK, CHUNK), 0) % CHUNK
    return rows >= lax.broadcasted_iota(jnp.int32, (2 * CHUNK, CHUNK), 1)


def inner_kernel(
    q_ref, k_ref, v_ref, cum_ref, state_ref, normed_ref, gate_ref, o_ref, s_ref, gp_ref, w3_ref, tmp_ref
):
    @pl.when((pl.program_id(0) == 0) & (pl.program_id(1) == 0))
    def _():
        w3_ref[...] = tall(gate_ref[...])

    start = pl.multiple_of(pl.program_id(1) * TILE + GRID, GRID)
    gp_ref[...] = dot(wide(normed_ref[pl.ds(start, TILE), :]), w3_ref[...])
    mask = causal_two()
    for c in range(TILE // CHUNK):
        base = c * CHUNK
        at = slice(base, base + CHUNK)
        q = q_ref[at, :]
        k = k_ref[at, :]
        cum = cum_ref[at, :]
        final = cum[CHUNK - 1 : CHUNK, :]
        wild = jnp.max(-final) > SPAN
        middle = 0.5 * final
        qf = split3(q * jnp.exp(cum - middle))
        kf = split3(k * jnp.exp(middle - cum))
        for p in range(PAIRS):
            qp = tuple(stacked_heads(lanes(part, p)) for part in qf[:2])
            kp = tuple(lanes(part, p) for part in kf[:2])
            tmp_ref[p] = mm3(qp, kp, 1, 1)

        @pl.when(opening(pl.program_id(1)) if c == 0 else False)
        def _():
            for p in range(PAIRS):
                qp = tuple(stacked_heads(lanes(part, p)) for part in qf)
                kp = tuple(lanes(part, p) for part in kf)
                tmp_ref[p] = mm6(qp, kp, 1, 1)

        @pl.when(wild)
        def _():
            exact_scores(q_ref, k_ref, cum_ref, base, tmp_ref)

        qd = q * jnp.exp(cum)
        for p in range(PAIRS):
            s = jnp.where(mask, tmp_ref[p], 0.0)
            s_ref[c, p] = s
            inner = merged_heads(mm3(split(s), split(lanes(v_ref[at, :], p))))
            outer = mm3(split(lanes(qd, p)), split(state_ref[c, p]), 1, 1)
            o_ref[at, p * LANES : (p + 1) * LANES] = inner + outer


def mix_kernel(o_ref, far_ref, tok_ref, gp_ref, mod_ref, out_w_ref, *rest):
    parts, (mid_ref, branch_ref, att_ref, st_ref, o3_ref) = rest[:-5], rest[-5:]
    image, tile = pl.program_id(0), pl.program_id(1)

    @pl.when((image == 0) & (tile == 0))
    def _():
        o3_ref[...] = tall(out_w_ref[...])

    @pl.when(tile == 0)
    def _():
        for p in range(PAIRS):
            st_ref[p] = linked(parts, p)

    far = split(far_ref[...])
    att = o_ref[...] + jnp.concatenate(
        [
            mm3(tuple(lanes(part, p) for part in far), split(st_ref[p]), 1, 1)
            for p in range(PAIRS)
        ],
        axis=1,
    )
    att_ref[...] = att
    rate = lax.rsqrt(head_means(att * att) + 1e-05)
    gp = gp_ref[...]
    branch = dot(wide(att * rate * (gp * sigmoid(gp))), o3_ref[...])
    branch_ref[...] = branch
    mid_ref[...] = tok_ref[...] + mod_ref[2:3, :] * branch


def mlp_kernel(
    mid_ref, cot_ref, mod_ref, up_ref, down_ref, block_ref, dmid_ref, dmod_ref, send_ref, keep_ref, u3_ref, ut_ref, d_ref, dt3_ref, gu_ref, gd_ref
):
    image, tile = pl.program_id(0), pl.program_id(1)
    units = up_ref.shape[1]

    @pl.when((image == 0) & (tile == 0))
    def _():
        u3_ref[...] = tall(up_ref[...])
        ut_ref[...] = across(up_ref[...])
        d_ref[...] = tall(down_ref[...])
        dt3_ref[...] = across(down_ref[...])
        gu_ref[...] = jnp.zeros_like(gu_ref)
        gd_ref[...] = jnp.zeros_like(gd_ref)

    @pl.when(tile == 0)
    def _():
        dmod_ref[...] = jnp.zeros_like(dmod_ref)

    shift_b = mod_ref[3:4, :]
    scale_b = 1.0 + mod_ref[4:5, :]
    gate_b = mod_ref[5:6, :]
    middle = mid_ref[...]
    hat, rate_b = normalized(middle)
    second = hat * scale_b + shift_b
    cot = cot_ref[...]
    dmlp = cot * gate_b
    u = dot(wide(second), u3_ref[...])
    square = u * u
    th = jnp.tanh(GELU_C * (u + 0.044715 * u * square))
    slope = 0.5 * (1.0 + th) + 0.5 * u * (1.0 - th * th) * (
        GELU_C * (1.0 + 3.0 * 0.044715 * square)
    )
    act = split(0.5 * u * (1.0 + th))
    mlp = dot(jnp.concatenate([act[0], act[1], act[0]], axis=1), d_ref[...])
    du = split(dot(wide(dmlp), dt3_ref[...], 1, 1) * slope)
    dsec = dot(jnp.concatenate([du[0], du[1], du[0]], axis=1), ut_ref[...], 1, 1)
    gu_ref[...] += dot(wide(second.T), jnp.concatenate([du[0], du[0], du[1]], axis=0))
    gd_ref[...] += dot(wide(dmlp.T), jnp.concatenate([act[0], act[0], act[1]], axis=0))
    block_ref[...] = middle + gate_b * mlp
    dmid_ref[...] = cot + normal_back(dsec * scale_b, hat, rate_b)
    dmod_ref[3:4, :] += jnp.sum(dsec, axis=0, keepdims=True)
    dmod_ref[4:5, :] += jnp.sum(dsec * hat, axis=0, keepdims=True)
    dmod_ref[5:6, :] += jnp.sum(cot * mlp, axis=0, keepdims=True)

    @pl.when((image == pl.num_programs(0) - 1) & (tile == pl.num_programs(1) - 1))
    def _():
        def lower(ref):
            for j in range(units // WIDTH):
                at = slice(j * WIDTH, (j + 1) * WIDTH)
                ref[at, :] = gu_ref[:, at]

        def upper(ref):
            ref[...] = gd_ref[...].T

        halves_out(lower, upper, send_ref, keep_ref)


def mix_back_kernel(
    dmid_ref,
    branch_ref,
    att_ref,
    gp_ref,
    far_ref,
    normed_ref,
    mod_ref,
    message_ref,
    out_w_ref,
    gate_w_ref,
    datt_ref,
    dnorm_ref,
    send_ref,
    keep_ref,
    dmod_ref,
    dmessage_ref,
    g_ref,
    ot3_ref,
    gt3_ref,
    dst_ref,
):
    image, tile = pl.program_id(0), pl.program_id(1)

    @pl.when((image == 0) & (tile == 0))
    def _():
        ot3_ref[...] = across(out_w_ref[...])
        gt3_ref[...] = across(gate_w_ref[...])
        g_ref[...] = jnp.zeros_like(g_ref)

    @pl.when(tile == 0)
    def _():
        dmod_ref[...] = jnp.zeros_like(dmod_ref)
        dst_ref[...] = jnp.zeros_like(dst_ref)

    dmid = dmid_ref[...]
    dmod_ref[2:3, :] += jnp.sum(dmid * branch_ref[...], axis=0, keepdims=True)
    dbr = split(dmid * mod_ref[2:3, :])
    dy = dot(jnp.concatenate([dbr[0], dbr[1], dbr[0]], axis=1), ot3_ref[...], 1, 1)
    att = att_ref[...]
    rate = lax.rsqrt(head_means(att * att) + 1e-05)
    unit = att * rate
    gp = gp_ref[...]
    sig = sigmoid(gp)
    gate = gp * sig
    g_ref[0:WIDTH, :] += dot(
        wide((unit * gate).T), jnp.concatenate([dbr[0], dbr[0], dbr[1]], axis=0)
    )
    dunit = dy * gate
    datt = rate * (dunit - unit * head_means(dunit * unit))
    datt_ref[...] = datt
    dg = split((dy * unit) * (sig * (1.0 + gp * (1.0 - sig))))
    dnorm_ref[...] = dot(jnp.concatenate([dg[0], dg[1], dg[0]], axis=1), gt3_ref[...], 1, 1)
    start = pl.multiple_of(tile * TILE + GRID, GRID)
    g_ref[WIDTH:, :] += dot(
        wide(normed_ref[pl.ds(start, TILE), :].T), jnp.concatenate([dg[0], dg[0], dg[1]], axis=0)
    )
    da = split(datt)
    far = split(far_ref[...])
    for p in range(PAIRS):
        dst_ref[p] += block_diagonal(
            mm3(tuple(lanes(part, p) for part in da), tuple(lanes(part, p) for part in far), 0, 0)
        )

    @pl.when(tile == pl.num_programs(1) - 1)
    def _():
        for p in range(PAIRS):
            dmessage_ref[p, 0:HEAD_DIM, :] = dst_ref[p, 0:HEAD_DIM, :] + dst_ref[p, HEAD_DIM:, :]
            dmessage_ref[p, HEAD_DIM:, :] = message_ref[p, HEAD_DIM:, :]

    @pl.when((image == pl.num_programs(0) - 1) & (tile == pl.num_programs(1) - 1))
    def _():
        def lower(ref):
            ref[...] = g_ref[0:WIDTH, :]

        def upper(ref):
            ref[...] = g_ref[WIDTH:, :]

        halves_out(lower, upper, send_ref, keep_ref)


def exact_back(q_ref, k_ref, cum_ref, ds_ref, base, dq_ref, dk_ref):
    q = q_ref[pl.ds(base, CHUNK), :]
    cum = cum_ref[pl.ds(base, CHUNK), :]
    dq_ref[...] = jnp.zeros_like(dq_ref)

    def step(j, carry):
        key = k_ref[pl.ds(base + j, 1), :]
        weight = jnp.exp(jnp.minimum(cum - cum_ref[pl.ds(base + j, 1), :], 0.0))
        at = lax.broadcasted_iota(jnp.int32, (2 * CHUNK, CHUNK), 1) == j
        columns = []
        for p in range(PAIRS):
            column = jnp.sum(jnp.where(at, ds_ref[p], 0.0), axis=1, keepdims=True)
            columns.append(merged_heads(jnp.broadcast_to(column, (2 * CHUNK, LANES))))
        ds = jnp.concatenate(columns, axis=1) * weight
        dq_ref[...] += ds * key
        dk_ref[pl.ds(j, 1), :] = jnp.sum(ds * q, axis=0, keepdims=True)
        return carry

    lax.fori_loop(0, CHUNK, step, 0)


def inner_back_kernel(
    q_ref,
    k_ref,
    v_ref,
    cum_ref,
    datt_ref,
    s_ref,
    state_ref,
    fade_ref,
    st_ref,
    dq_ref,
    dk_ref,
    dv_ref,
    full_ref,
    ds_ref,
    dqi_ref,
    dki_ref,
):
    mask = causal_two()
    for c in range(TILE // CHUNK):
        base = c * CHUNK
        at = slice(base, base + CHUNK)
        q = q_ref[at, :]
        k = k_ref[at, :]
        cum = cum_ref[at, :]
        final = cum[CHUNK - 1 : CHUNK, :]
        wild = jnp.max(-final) > SPAN
        middle = 0.5 * final
        eq = jnp.exp(cum - middle)
        ek = jnp.exp(middle - cum)
        qf = split(q * eq)
        kf = split(k * ek)
        da = split3(datt_ref[at, :])
        vs = split3(v_ref[at, :])
        for p in range(PAIRS):
            da2 = tuple(stacked_heads(lanes(part, p)) for part in da[:2])
            vp = tuple(lanes(part, p) for part in vs[:2])
            ds_ref[p] = jnp.where(mask, mm3(da2, vp, 1, 1), 0.0)

        @pl.when(opening(pl.program_id(1)) if c == 0 else False)
        def _():
            for p in range(PAIRS):
                da2 = tuple(stacked_heads(lanes(part, p)) for part in da)
                vp = tuple(lanes(part, p) for part in vs)
                ds_ref[p] = jnp.where(mask, mm6(da2, vp, 1, 1), 0.0)

        for p in range(PAIRS):
            da2 = tuple(stacked_heads(lanes(part, p)) for part in da[:2])
            ds2 = split(ds_ref[p])
            kp = tuple(lanes(part, p) for part in kf)
            qp = tuple(lanes(part, p) for part in qf)
            dqi_ref[:, p * LANES : (p + 1) * LANES] = merged_heads(mm3(ds2, kp)) * lanes(eq, p)
            q2 = tuple(stacked_heads(part) for part in qp)
            dki_ref[:, p * LANES : (p + 1) * LANES] = mm3(ds2, q2, 0, 0) * lanes(ek, p)
            s2 = split(s_ref[c, p])
            dv_ref[at, p * LANES : (p + 1) * LANES] = mm3(s2, da2, 0, 0)

        @pl.when(wild)
        def _():
            exact_back(q_ref, k_ref, cum_ref, ds_ref, base, dqi_ref, dki_ref)

        grow = jnp.exp(cum)
        for p in range(PAIRS):
            full = state_ref[c, p] + lanes(fade_ref[c, 0:1, :], p) * st_ref[p]
            full_ref[c, p] = full
            outer = mm3(tuple(lanes(part, p) for part in da[:2]), split(full))
            dq_ref[at, p * LANES : (p + 1) * LANES] = (
                dqi_ref[:, p * LANES : (p + 1) * LANES] + outer * lanes(grow, p)
            )
        dk_ref[at, :] = dki_ref[...]


def state_back_kernel(
    valid_ref,
    q_ref,
    k_ref,
    v_ref,
    cum_ref,
    slope_ref,
    datt_ref,
    dq_ref,
    dk_ref,
    dv_ref,
    full_ref,
    conv_ref,
    down_ref,
    up_ref,
    *rest,
):
    parts, (proj_ref, send_ref, keep_ref, dst_ref, dbias_ref, acc_ref, g_ref) = rest[:-7], rest[-7:]
    image, turn = pl.program_id(0), pl.program_id(1)
    tile = pl.num_programs(1) - 1 - turn

    @pl.when((image == 0) & (turn == 0))
    def _():
        dbias_ref[...] = jnp.zeros_like(dbias_ref)
        acc_ref[...] = jnp.zeros_like(acc_ref)

    @pl.when(turn == 0)
    def _():
        for p in range(PAIRS):
            dst_ref[p] = linked(parts, p)

    count = jnp.sum(valid_ref[...], axis=1, keepdims=True)
    keep = (
        lax.broadcasted_iota(jnp.int32, (CHUNK, WIDTH), 0) + tile * TILE
    )
    for c in reversed(range(TILE // CHUNK)):
        at = slice(c * CHUNK, (c + 1) * CHUNK)
        q = q_ref[at, :]
        k = k_ref[at, :]
        cum = cum_ref[at, :]
        final = cum[CHUNK - 1 : CHUNK, :]
        late = jnp.exp(final - cum)
        kd = k * late
        v = v_ref[at, :]
        qd = split(q * jnp.exp(cum))
        da = split(datt_ref[at, :])
        factor = jnp.exp(final)
        dk_parts, dv_parts, cross = [], [], []
        for p in range(PAIRS):
            old = dst_ref[p]
            pair = split(old)
            dk_parts.append(mm3(split(lanes(v, p)), pair))
            dv_parts.append(mm3(split(lanes(kd, p)), pair, 1, 1))
            leaving = lanes(factor, p) * full_ref[c, p] + block_diagonal(
                mm3(split(lanes(v, p)), split(lanes(kd, p)), 0, 0)
            )
            cross.append(jnp.sum(leaving * old, axis=0, keepdims=True))
            update = mm3(
                tuple(lanes(part, p) for part in da), tuple(lanes(part, p) for part in qd), 0, 0
            )
            dst_ref[p] = lanes(factor, p) * old + block_diagonal(update)
        dq = dq_ref[at, :]
        dk = dk_ref[at, :] + jnp.concatenate(dk_parts, axis=1) * late
        dv = dv_ref[at, :] + jnp.concatenate(dv_parts, axis=1)
        dgates = running_sum(q * dq - k * dk, True) + jnp.concatenate(cross, axis=1)
        dx = dgates * slope_ref[at, :]
        real = keep + c * CHUNK < count
        dk = jnp.where(real, dk, 0.0)
        dv = jnp.where(real, dv, 0.0)
        dbias_ref[...] += jnp.sum(dx.reshape(CHUNK // 8, 8, WIDTH), axis=0)
        proj_ref[at, 0:WIDTH] = dq
        proj_ref[at, WIDTH : 2 * WIDTH] = dk
        proj_ref[at, 2 * WIDTH : 3 * WIDTH] = dv
        proj_ref[at, 3 * WIDTH :] = dx
    conv = conv_ref[...]
    proj = split(proj_ref[...])
    acc_ref[...] += dot(
        wide((conv * sigmoid(conv)).T), jnp.concatenate([proj[0], proj[0], proj[1]], axis=0)
    )

    @pl.when((image == pl.num_programs(0) - 1) & (tile == 0))
    def _():
        for j in range(3):
            grad = acc_ref[:, j * WIDTH : (j + 1) * WIDTH]
            g_ref[j * WIDTH : (j + 1) * WIDTH, :] = (
                grad * HEAD_DIM ** (-0.5) if j == 0 else grad
            )
        grad = acc_ref[:, 3 * WIDTH :]
        base = 3 * WIDTH
        rank = up_ref.shape[0]
        g_ref[base:, :] = jnp.zeros_like(g_ref[base:, :])
        g_ref[base : base + rank, :] = mm6(split3(up_ref[...]), split3(grad), 1, 1)
        g_ref[base + rank : base + 2 * rank, :] = mm6(split3(down_ref[...]), split3(grad))
        g_ref[base + 2 * rank : base + 2 * rank + 1, :] = jnp.sum(
            dbias_ref[...], axis=0, keepdims=True
        )

        def lower(ref):
            ref[...] = g_ref[0 : ROWS // 2, :]

        def upper(ref):
            ref[...] = g_ref[ROWS // 2 :, :]

        halves_out(lower, upper, send_ref, keep_ref)


def hidden_kernel(proj_ref, conv_ref, w_ref, dconv_ref, wt3_ref):
    @pl.when((pl.program_id(0) == 0) & (pl.program_id(1) == 0))
    def _():
        wt3_ref[...] = across(w_ref[...])

    dhidden = dot(wide(proj_ref[...]), wt3_ref[...], 1, 1)
    conv = conv_ref[...]
    sig = sigmoid(conv)
    dconv_ref[...] = dhidden * (sig * (1.0 + conv * (1.0 - sig)))


def front_back_kernel(
    tok_ref,
    normed_ref,
    dconv_ref,
    top_ref,
    bot_ref,
    dnorm_ref,
    dmid_ref,
    mod_ref,
    taps_ref,
    mlp_ref,
    mix_ref,
    info_ref,
    grad_ref,
    rows_ref,
    dmod_ref,
    pad_ref,
    taps_acc_ref,
):
    length = dconv_ref.shape[0]
    image, i = pl.program_id(0), pl.program_id(1)

    @pl.when(i == 0)
    def _():
        taps_acc_ref[...] = jnp.zeros_like(taps_acc_ref)

    @pl.when(i == 0)
    def _():
        dmod_ref[...] = jnp.zeros_like(dmod_ref)
        pad_ref[0:GRID, :] = top_ref[...]
        pad_ref[pl.ds(length + GRID, GRID), :] = bot_ref[...]
        pad_ref[pl.ds(GRID, length), :] = dconv_ref[...]

    scale = 1.0 + mod_ref[1:2, :]

    def eights(x):
        return jnp.sum(x.reshape(x.shape[0] // 8, 8, WIDTH), axis=0)

    start = pl.multiple_of(i * TILE, TILE)
    rows = [pad_ref[pl.ds(start + (2 - a) * GRID, TILE), :] for a in range(3)]
    parts = [
        sum(taps_ref[3 * a + b : 3 * a + b + 1, :] * rows[a] for a in range(3))
        for b in range(3)
    ]
    dn = (
        shifted(parts[0], -1)
        + parts[1]
        + shifted(parts[2], 1)
        + dnorm_ref[...]
    )
    hat, rate = normalized(tok_ref[...])
    grad_ref[...] = dmid_ref[...] + normal_back(
        dn * scale, hat, rate
    )
    dmod_ref[0:1, :] += jnp.sum(dn, axis=0, keepdims=True)
    dmod_ref[1:2, :] += jnp.sum(dn * hat, axis=0, keepdims=True)
    own = rows[1]
    moved = [shifted(own, -1), own, shifted(own, 1)]
    for a in range(3):
        near = normed_ref[pl.ds(start + a * GRID, TILE), :]
        for b in range(3):
            taps_acc_ref[3 * a + b] += eights(moved[b] * near)

    @pl.when(i == pl.num_programs(1) - 1)
    def _():
        own = lax.axis_index("seq") == 0
        rows_ref[...] = jnp.zeros_like(rows_ref)
        rows_ref[0:6, :] = (dmod_ref[...] + mlp_ref[...] + mix_ref[...])[0:6, :]
        rows_ref[6:10, :] = jnp.where(own, info_ref[0:4, :], 0.0)
        for t in range(9):
            rows_ref[10 + t : 11 + t, :] = jnp.sum(taps_acc_ref[t], axis=0, keepdims=True)


def call(kernel, grid, ins, outs, scratch, flops=0, moved=0, prefetch=0, limit=24):
    return pl.pallas_call(
        kernel,
        grid_spec=pltpu.PrefetchScalarGridSpec(
            num_scalar_prefetch=prefetch,
            grid=grid,
            in_specs=ins,
            out_specs=[spec for spec, _ in outs],
            scratch_shapes=scratch,
        ),
        out_shape=[jax.ShapeDtypeStruct(shape, F32) for _, shape in outs],
        compiler_params=pltpu.CompilerParams(vmem_limit_bytes=limit * 1024 * 1024),
        cost_estimate=pl.CostEstimate(flops=4 * flops, bytes_accessed=4 * moved, transcendentals=0),
    )


def whole(shape):
    zeros = (0,) * len(shape)
    return pl.BlockSpec(shape, lambda *_: zeros, pipeline_mode=pl.Buffered(1))


def per_image(shape):
    zeros = (0,) * len(shape)
    return pl.BlockSpec((None,) + shape, lambda n, *_: (n,) + zeros)


def time_features(timesteps):
    half = FREQ // 2
    freqs = jnp.exp(-math.log(10000.0) * jnp.arange(half, dtype=F32) / half)
    angles = timesteps.astype(F32)[:, None] * freqs[None, :]
    return jnp.concatenate([jnp.cos(angles), jnp.sin(angles)], axis=1)


def halves(axis):
    return [1 << b for b in range(lax.axis_size(axis).bit_length() - 1)]


def swapped(x, axis, bit):
    return lax.ppermute(x, axis, [(i, i ^ bit) for i in range(lax.axis_size(axis))])


def is_high(axis, bit):
    return (lax.axis_index(axis) // bit) % 2


def step_kernel(items, *refs):
    ins, outs = refs[: 2 * len(items)], list(refs[2 * len(items) :])
    for n, (kind, link) in enumerate(items):
        own, got = ins[2 * n], ins[2 * n + 1]
        if kind == "sum":
            outs.pop(0)[...] = own[...] + got[...]
        elif kind == "join":
            out, size, high = outs.pop(0), own.shape[0], is_high(*link) == 1
            out[0:size] = jnp.where(high, got[...], own[...])
            out[size:] = jnp.where(high, own[...], got[...])
        else:
            half = own.shape[0] // 2
            high = is_high(*link)
            for side in (1 - high, high):
                start = side * half
                at = pl.ds(pl.multiple_of(start, 8) if half % 8 == 0 else start, half)
                outs.pop(0)[...] = own[at, :] + got[at, :]


def stepped(flows, got):
    items, arrays, shapes = [], [], []
    for flow, x in zip(flows, got):
        kind, link, own = flow.item()
        if kind == "split" and own.shape[0] % 16:
            flow.took_whole(own + x)
            continue
        items.append((flow, kind, link))
        arrays += [own, x]
        if kind == "split":
            shapes += [(own.shape[0] // 2, WIDTH)] * 2
        else:
            shapes.append((own.shape[0] * (2 if kind == "join" else 1),) + own.shape[1:])
    if not items:
        return
    outs = call(
        functools.partial(step_kernel, [item[1:] for item in items]),
        (1,),
        [whole(x.shape) for x in arrays],
        [(whole(shape), shape) for shape in shapes],
        [],
        flops=sum(x.size for x in arrays),
        moved=8 * sum(x.size for x in arrays),
        limit=24,
    )(*arrays)
    outs = list(outs)
    for flow, kind, _ in items:
        flow.took(*(outs.pop(0) for _ in range(2 if kind == "split" else 1)))


class Flow:
    def __init__(self, sent, keep, order):
        self.sent, self.keep = sent, keep
        self.order, self.used = list(order), []

    def busy(self):
        return bool(self.order)

    def send(self):
        return self.sent

    def link(self):
        return self.order[0]

    def item(self):
        self.used.append(self.order.pop(0))
        if self.order:
            return "split", self.order[0], self.keep
        return "sum", None, self.keep

    def took(self, *new):
        if len(new) == 2:
            self.sent, self.keep = new
        else:
            (self.keep,) = new

    def now(self):
        return self.sent if self.order else self.keep

    def took_whole(self, total):
        half = total.shape[0] // 2
        high = is_high(*self.order[0])
        self.sent = lax.dynamic_slice_in_dim(total, (1 - high) * half, half)
        self.keep = lax.dynamic_slice_in_dim(total, high * half, half)


class Spread:
    def __init__(self, x, used):
        self.x, self.used = x[None], list(used)

    def busy(self):
        return len(self.used) > 1

    def send(self):
        return self.x

    def link(self):
        return self.used[-1]

    def item(self):
        return "join", self.used.pop(), self.x

    def took(self, new):
        self.x = new

    def now(self):
        return self.x


class Rows:
    def __init__(self, x, sums, joins):
        self.x, self.sums, self.joins = x, list(sums), list(joins)

    def busy(self):
        return bool(self.sums or self.joins)

    def send(self):
        return self.x

    def link(self):
        return self.sums[0] if self.sums else self.joins[0]

    def item(self):
        if self.sums:
            self.sums.pop(0)
            return "sum", None, self.x
        return "join", self.joins.pop(0), self.x

    def took(self, new):
        self.x = new

    def now(self):
        return self.x


class Paired:
    def __init__(self, sent, keep, link):
        self.sent, self.keep, self.at, self.got = sent, keep, link, None

    def busy(self):
        return self.got is None

    def send(self):
        return self.sent

    def link(self):
        return self.at


def fork_kernel(parts, *refs):
    count = (len(refs) - 1 - 2 * len(parts)) // 2
    ins, outs, total = refs[: 2 * count], list(refs[2 * count : -1]), refs[-1]
    at = 0
    for n in range(count):
        rows = ins[2 * n].shape[0]
        total[at : at + rows, :] = ins[2 * n][...] + ins[2 * n + 1][...]
        at += rows
    for first, rows, link in parts:
        high = is_high(*link)
        for side in (1 - high, high):
            start = side * (rows // 2) + first
            outs.pop(0)[...] = total[pl.ds(pl.multiple_of(start, 8), rows // 2), :]


def forked(pairs, cuts, orders):
    rows = sum(cuts)
    starts = [sum(cuts[:n]) for n in range(len(cuts))]
    parts = [(start, cut, order[0]) for start, cut, order in zip(starts, cuts, orders)]
    arrays = [x for pair in pairs for x in (pair.keep, pair.got)]
    shapes = [(part[1] // 2, WIDTH) for part in parts for _ in range(2)]
    outs = call(
        functools.partial(fork_kernel, parts),
        (1,),
        [whole(x.shape) for x in arrays],
        [(whole(shape), shape) for shape in shapes],
        [pltpu.VMEM((rows, WIDTH), F32)],
        flops=rows * WIDTH,
        moved=12 * rows * WIDTH,
        limit=24,
    )(*arrays)
    return [Flow(outs[2 * n], outs[2 * n + 1], order) for n, order in enumerate(orders)]


def beside(flows, first, kernel):
    flows = [flow for flow in flows if flow.busy()]
    first, *sends = lax.optimization_barrier((first, *(flow.send() for flow in flows)))
    got = [swapped(x, *flow.link()) for flow, x in zip(flows, sends)]
    outs = kernel(first)
    head, *got = lax.optimization_barrier((outs[0], *got))
    for flow, x in zip(flows, got):
        if isinstance(flow, Paired):
            flow.got = x
    rest = [(flow, x) for flow, x in zip(flows, got) if not isinstance(flow, Paired)]
    stepped([flow for flow, _ in rest], [x for _, x in rest])
    return [head] + list(outs[1:])


def halves_out(lower, upper, send_ref, keep_ref):
    core = lax.axis_index("seq") % 2

    @pl.when(core == 0)
    def _():
        lower(keep_ref)
        upper(send_ref)

    @pl.when(core == 1)
    def _():
        lower(send_ref)
        upper(keep_ref)


def move_first(outs):
    return list(outs[1:]) + [outs[0]]


def messages(message, backward):
    size = lax.axis_size("seq")
    got = []
    for far in range(1, size):
        pairs = [(i, i + far) for i in range(size - far)]
        if backward:
            pairs = [(j, i) for i, j in pairs]
        got.append(lax.ppermute(message, "seq", pairs))
    return got


def plan(early_rows, pieces, units):
    late_rows = tuple(total // pieces for total in LATE)
    moves = []

    def place(kind, half, at):
        if kind == 0:
            if at >= units:
                return 2 + half, at - units, 0, units + WIDTH - at
            if half == 0:
                return 0, at % WIDTH, at // WIDTH, WIDTH - at % WIDTH
            return 1, at, 0, units - at
        row = half * (ROWS // 2) + at
        block = min(row // WIDTH, 3)
        room = ROWS // 2 - at
        return 4 + block, row - block * WIDTH, 0, min(room, WIDTH - row % WIDTH) if block < 3 else room

    for half in range(2):
        for kind in range(2):
            at = 0
            for flow in range(len(early_rows)):
                rows = early_rows[flow] if kind == 0 else late_rows[flow]
                base = 0 if kind == 0 else early_rows[flow]
                for piece in range(pieces):
                    done = 0
                    while done < rows:
                        out, row, block, room = place(kind, half, at)
                        span = min(rows - done, room)
                        moves.append((half, flow, piece, base + done, out, row, block, span))
                        done, at = done + span, at + span
    return moves


def assemble_kernel(moves, pieces, lasts, core, *refs):
    count = len(lasts)
    near, other, near_core, other_core = (refs[n * count : (n + 1) * count] for n in range(4))
    outs = refs[4 * count :]
    mine = is_high(*core)
    for half, flow, piece, row, out, start, block, span in moves:
        side, index = piece // (pieces // 2), piece % (pieces // 2)
        at = (index, slice(row, row + span), slice(None))
        own = is_high(*lasts[flow]) == side
        here = jnp.where(own, near[flow][at], other[flow][at])
        there = jnp.where(own, near_core[flow][at], other_core[flow][at])
        outs[out][start : start + span, block * WIDTH : (block + 1) * WIDTH] = jnp.where(
            mine == half, here, there
        )


def assembled(near, other, near_core, other_core, lasts, core, early, units):
    early_rows = tuple(flow.keep.shape[0] for flow in early)
    pieces = 2 * near[0].shape[0]
    moves = plan(early_rows, pieces, units)
    square = (WIDTH, WIDTH)
    shapes = [(WIDTH, units), (units, WIDTH)] + [square] * 5 + [(ROWS - 3 * WIDTH, WIDTH)]
    arrays = near + other + near_core + other_core
    return call(
        functools.partial(assemble_kernel, moves, pieces, lasts, core),
        (1,),
        [whole(x.shape) for x in arrays],
        [(whole(shape), shape) for shape in shapes],
        [],
        moved=4 * 4 * sum(x.size for x in near),
        limit=40,
    )(*arrays)


def body(
    tokens,
    valid_mask,
    timesteps,
    class_ids,
    time_first,
    time_second,
    class_table,
    ada_weight,
    ada_bias,
    conv_taps,
    query_proj,
    key_proj,
    value_proj,
    decay_down,
    decay_up,
    decay_bias,
    gate_proj,
    out_proj,
    mlp_up,
    mlp_down,
    cotangent,
):
    count, length, width = tokens.shape
    size, mine = lax.axis_size("seq"), lax.axis_index("seq")
    tiles, chunks = length // TILE, length // CHUNK
    per_tile = TILE // CHUNK
    up_pairs = [(i, i + 1) for i in range(size - 1)]
    down_pairs = [(j, i) for i, j in up_pairs]
    seq_bits = [("seq", bit) for bit in halves("seq")]
    img_bits = [("img", bit) for bit in halves("img")]
    core, order_a = seq_bits[0], seq_bits[1:] + img_bits
    order_b = img_bits[:2] + seq_bits[1:] + img_bits[2:]
    order_c = img_bits[2:] + seq_bits[1:] + img_bits[:2]
    orders = (order_a, order_b, order_c)

    def borders(x):
        return (
            lax.ppermute(x[:, length - GRID :], "seq", up_pairs),
            lax.ppermute(x[:, :GRID], "seq", down_pairs),
        )

    above, below = borders(tokens)

    square = (width, width)
    row = (length, width)
    dense = 2 * 3 * count * length * width
    each = 4 * count * length * width
    features = time_features(timesteps)
    mod_spec = per_image((6, width))
    modul, info = call(
        condition_kernel,
        (count,),
        [
            per_image((1, FREQ)),
            whole(time_first.shape),
            whole(time_second.shape),
            pl.BlockSpec((8, width), lambda n, ids: (ids[n] // 8, 0)),
            whole(ada_weight.shape),
            whole((6 * width,)),
        ],
        [
            (mod_spec, (count, 6, width)),
            (per_image((8, width)), (count, 8, width)),
        ],
        [],
        flops=1000000,
        moved=4 * 6 * width * width,
        prefetch=1,
        limit=60,
    )(class_ids, features[:, None], time_first, time_second, class_table, ada_weight, ada_bias)

    valid = valid_mask[:, None]
    valid_spec = per_image((1, length))
    message_shape = (PAIRS, HEAD_DIM + 8, LANES)
    def tiled(shape=(TILE, width)):
        return pl.BlockSpec((None,) + shape, lambda n, i: (n, i, 0))

    tile_row = (tiled(), (count,) + row)
    pair_spec = pl.BlockSpec(
        (None, per_tile, PAIRS, LANES, LANES), lambda n, i: (n, i, 0, 0, 0)
    )
    state_spec = pl.BlockSpec((None, PAIRS, LANES, LANES), lambda n, i: (n, 0, 0, 0))
    state_shape = (count, PAIRS, LANES, LANES)
    score_shape = (count, chunks, PAIRS, 2 * CHUNK, CHUNK)
    score_spec = pl.BlockSpec(
        (None, per_tile, PAIRS, 2 * CHUNK, CHUNK), lambda n, i: (n, i, 0, 0, 0)
    )
    normed_spec = per_image((length + 2 * GRID, width))
    message_spec = per_image(message_shape)
    fade_spec = pl.BlockSpec((None, per_tile, 8, width), lambda n, i: (n, i, 0, 0))
    (
        weights,
        normed,
        conv,
        query,
        keys,
        values,
        cumul,
        slope,
        far,
        states,
        fades,
        message,
    ) = call(
        front_kernel,
        (count, tiles),
        [
            per_image(row),
            per_image((GRID, width)),
            per_image((GRID, width)),
            valid_spec,
            mod_spec,
            whole((9, width)),
            whole(square),
            whole(square),
            whole(square),
            whole(decay_up.shape),
            whole(decay_up.shape),
            whole((width,)),
        ],
        [
            (whole((width, 4 * width)), (width, 4 * width)),
            (per_image((length + 2 * GRID, width)), (count, length + 2 * GRID, width)),
        ]
        + [tile_row] * 7
        + [
            (pair_spec, (count, chunks, PAIRS, LANES, LANES)),
            (fade_spec, (count, chunks, 8, width)),
            (message_spec, (count,) + message_shape),
        ],
        [
            pltpu.VMEM((6 * width, 4 * width), BF16),
            pltpu.VMEM((TILE, 4 * width), F32),
            pltpu.VMEM((PAIRS, LANES, LANES), F32),
            pltpu.VMEM((8, width), F32),
        ],
        flops=dense * 4 * width,
        moved=each * 10,
    )(
        tokens,
        above,
        below,
        valid,
        modul,
        conv_taps,
        query_proj,
        key_proj,
        value_proj,
        decay_down.T,
        decay_up,
        decay_bias,
    )

    forward_parts = messages(message, False)
    inner, scores, gate_in = call(
        inner_kernel,
        (count, tiles),
        [tiled()] * 4 + [pair_spec, normed_spec, whole(square)],
        [tile_row, (score_spec, score_shape), tile_row],
        [pltpu.VMEM((3 * width, width), BF16), pltpu.VMEM((PAIRS, 2 * CHUNK, CHUNK), F32)],
        flops=dense * 2 * width,
        moved=each * 9,
    )(query, keys, values, cumul, states, normed, gate_proj)

    middle, branch, attended, state_in = call(
        mix_kernel,
        (count, tiles),
        [tiled()] * 4 + [mod_spec, whole(square)] + [message_spec] * (size - 1),
        [tile_row] * 3 + [(state_spec, state_shape)],
        [pltpu.VMEM((3 * width, width), BF16)],
        flops=dense * 2 * width,
        moved=each * 7,
    )(inner, far, tokens, gate_in, modul, out_proj, *forward_parts)

    dmod_spec = per_image((8, width))
    dmod_out = (dmod_spec, (count, 8, width))

    units = mlp_up.shape[1]
    block_out, dmid, dmod_mlp, mlp_sent, mlp_kept = call(
        mlp_kernel,
        (count, tiles),
        [tiled(), tiled(), mod_spec, whole(mlp_up.shape), whole(mlp_down.shape)],
        [tile_row] * 2 + [dmod_out] + [(whole((units, width)), (units, width))] * 2,
        [
            pltpu.VMEM((3 * width, units), BF16),
            pltpu.VMEM((width, 3 * units), BF16),
            pltpu.VMEM((3 * units, width), BF16),
            pltpu.VMEM((units, 3 * width), BF16),
            pltpu.VMEM((width, units), F32),
            pltpu.VMEM((width, units), F32),
        ],        flops=dense * 6 * units,
        moved=each * 8,
        limit=40,
    )(middle, cotangent, modul, mlp_up, mlp_down)

    mlp_pair = Paired(mlp_sent, mlp_kept, core)
    datt, dnorm, mix_sent, mix_kept, dmod_mix, d_message = beside([mlp_pair], dmid, lambda x: call(
        mix_back_kernel,
        (count, tiles),
        [tiled()] * 5
        + [normed_spec, mod_spec, message_spec, whole(square), whole(square)],
        [tile_row] * 2
        + [(whole(square), square)] * 2
        + [dmod_out]
        + [(message_spec, (count,) + message_shape)],
        [
            pltpu.VMEM((2 * width, width), F32),
            pltpu.VMEM((width, 3 * width), BF16),
            pltpu.VMEM((width, 3 * width), BF16),
            pltpu.VMEM((PAIRS, LANES, LANES), F32),
        ],
        flops=dense * 5 * width,
        moved=each * 8,
        limit=60,
    )(x, branch, attended, gate_in, far, normed, modul, message, out_proj, gate_proj))
    mix_pair = Paired(mix_sent, mix_kept, core)
    d_message, datt = lax.optimization_barrier((d_message, datt))
    backward_parts = messages(d_message, True)

    dquery, dkeys, dvalues, full = beside([mix_pair], datt, lambda x: call(
        inner_back_kernel,
        (count, tiles),
        [tiled()] * 5 + [score_spec, pair_spec, fade_spec, state_spec],
        [tile_row] * 3 + [(pair_spec, (count, chunks, PAIRS, LANES, LANES))],
        [
            pltpu.VMEM((PAIRS, 2 * CHUNK, CHUNK), F32),
            pltpu.VMEM((CHUNK, width), F32),
            pltpu.VMEM((CHUNK, width), F32),
        ],
        flops=dense * 2 * width,
        moved=each * 12,
        limit=60,
    )(query, keys, values, cumul, x, scores, states, fades, state_in))

    early = forked([mlp_pair, mix_pair], EARLY, orders)

    def turned(shape=(TILE, width)):
        return pl.BlockSpec((None,) + shape, lambda n, i: (n, tiles - 1 - i, 0))

    dproj, late_sent, late_kept = beside(early, dquery, lambda x: call(
        state_back_kernel,
        (count, tiles),
        [valid_spec]
        + [turned()] * 9
        + [
            pl.BlockSpec(
                (None, per_tile, PAIRS, LANES, LANES),
                lambda n, i: (n, tiles - 1 - i, 0, 0, 0),
            ),
            turned(),
            whole(decay_up.shape),
            whole(decay_up.shape),
        ]
        + [message_spec] * (size - 1),
        [
            (turned((TILE, 4 * width)), (count, length, 4 * width)),
            (whole((ROWS // 2, width)), (ROWS // 2, width)),
            (whole((ROWS // 2, width)), (ROWS // 2, width)),
        ],
        [
            pltpu.VMEM((PAIRS, LANES, LANES), F32),
            pltpu.VMEM((8, width), F32),
            pltpu.VMEM((width, 4 * width), F32),
            pltpu.VMEM((ROWS, width), F32),
        ],
        flops=dense * 2 * width,
        moved=each * 14,
        limit=60,
    )(
        valid,
        query,
        keys,
        values,
        cumul,
        slope,
        datt,
        x,
        dkeys,
        dvalues,
        full,
        conv,
        decay_down.T,
        decay_up,
        *backward_parts,
    ))
    late_pair = Paired(late_sent, late_kept, core)
    (dconv,) = beside(early + [late_pair], late_kept, lambda x: call(
        hidden_kernel,
        (count, tiles),
        [tiled((TILE, 4 * width)), tiled(), whole((width, 4 * width))],
        [tile_row],
        [pltpu.VMEM((width, 3 * 4 * width), BF16)],
        flops=dense * 4 * width,
        moved=each * 7,
    )(lax.optimization_barrier((dproj, x))[0], conv, weights))
    d_above, d_below = borders(dconv)
    late = forked([late_pair], LATE[:2], orders[:2])
    rows, tokens_grad = beside(early + late, dconv, lambda x: move_first(call(
        front_back_kernel,
        (count, tiles),
        [
            tiled(),
            per_image((length + 2 * GRID, width)),
            per_image(row),
            per_image((GRID, width)),
            per_image((GRID, width)),
            tiled(),
            tiled(),
            mod_spec,
            whole((9, width)),
            dmod_spec,
            dmod_spec,
            dmod_spec,
        ],
        [
            tile_row,
            (per_image((24, width)), (count, 24, width)),
        ],
        [
            pltpu.VMEM((8, width), F32),
            pltpu.VMEM((length + 2 * GRID, width), F32),
            pltpu.VMEM((9, 8, width), F32),
        ],
        flops=count * length * width * 100,
        moved=each * 6,
    )(
        tokens, normed, x, d_above, d_below, dnorm, dmid, modul, conv_taps, dmod_mlp, dmod_mix, info
    )))

    flow_r = Rows(rows, seq_bits, img_bits)
    last = jnp.zeros((), F32)
    spreads = [None] * len(orders)
    while True:
        round_of = [flow for flow in late + early + [flow_r] + spreads if flow and flow.busy()]
        if not round_of:
            break
        for flow in round_of:
            got, last = lax.optimization_barrier((swapped(flow.send(), *flow.link()), last))
            stepped([flow], [got])
            last = flow.now()
        for n, one in enumerate(early):
            parts = [one] + late[n : n + 1]
            if spreads[n] is None and not any(part.busy() for part in parts):
                spreads[n] = Spread(jnp.concatenate([part.keep for part in parts]), one.used)
    rows = flow_r.x
    images = rows.shape[0]
    ids = rows[:, 9, 0].astype(jnp.int32)
    lasts = tuple(flow.link() for flow in spreads)
    rows, *near = lax.optimization_barrier((rows, *(flow.x for flow in spreads)))
    g_first, g_second, g_class, g_ada, g_ada_bias, g_taps = call(
        embed_kernel,
        (1,),
        [
            whole(rows.shape),
            whole(ada_weight.shape),
            whole(time_second.shape),
        ],
        [
            (whole(shape), shape)
            for shape in (
                time_first.shape,
                time_second.shape,
                class_table.shape,
                ada_weight.shape,
                (6 * width,),
                (9, width),
            )
        ],
        [],
        flops=images * 2 * 3 * width * width * 14,
        moved=4 * width * width * 20,
        prefetch=1,
    )(ids, rows, ada_weight, time_second)
    far_ones = [swapped(x, *last) for x, last in zip(near, lasts)]
    near_core = [swapped(x, *core) for x in near]
    g_ada, *far_ones = lax.optimization_barrier((g_ada, *far_ones))
    far_core = [swapped(x, *core) for x in far_ones]
    g_up, g_down, g_out, g_gate, g_query, g_key, g_value, g_small = assembled(
        near, far_ones, near_core, far_core, lasts, core, early, units
    )

    rank = decay_up.shape[0]
    return (
        block_out,
        tokens_grad,
        g_first,
        g_second,
        g_class,
        g_ada,
        g_ada_bias,
        g_taps,
        g_query,
        g_key,
        g_value,
        g_small[:rank].T,
        g_small[rank : 2 * rank],
        g_small[2 * rank],
        g_gate,
        g_out,
        g_up,
        g_down,
    )


def solution(mesh):
    image, shared = P("img", "seq", None), P()
    return jax.shard_map(
        body,
        mesh=mesh,
        in_specs=(image, P("img", "seq"), P("img"), P("img")) + (shared,) * 16 + (image,),
        out_specs=(image, image) + (shared,) * 16,
        check_vma=False,
    )
```

```python
import functools
import math

import jax
import jax.numpy as jnp
from jax import lax
from jax.experimental import pallas as pl
from jax.experimental.pallas import tpu as pltpu
from jax.sharding import PartitionSpec as P

HEADS = 6
HEAD_DIM = 64
CLASSES = 1000
FREQ = 256
GRID = 64
WIDTH = 384
PAIRS = 3
LANES = 128
CHUNK = 128
TILE = 256
ROWS = 1280
EARLY = (768, 768, 384)
LATE = (384, 256, 0)
SPAN = 120.0
HIGH = lax.Precision.HIGHEST
F32 = jnp.float32
BF16 = jnp.bfloat16
GELU_C = math.sqrt(2.0 / math.pi)


def product(left, right):
    return jnp.dot(left, right, precision=HIGH, preferred_element_type=F32)


def dot(a, b, ca=1, cb=0):
    return lax.dot_general(a, b, (((ca,), (cb,)), ((), ())), preferred_element_type=F32)


def split(x):
    high = x.astype(BF16)
    return high, (x - high.astype(F32)).astype(BF16)


def mm3(a, b, ca=1, cb=0):
    return dot(a[0], b[0], ca, cb) + dot(a[1], b[0], ca, cb) + dot(a[0], b[1], ca, cb)


def split3(x):
    high = x.astype(BF16)
    rest = x - high.astype(F32)
    middle = rest.astype(BF16)
    return high, middle, (rest - middle.astype(F32)).astype(BF16)


def mm6(a, b, ca=1, cb=0):
    terms = ((0, 0), (0, 1), (1, 0), (1, 1), (0, 2), (2, 0))
    return sum(dot(a[i], b[j], ca, cb) for i, j in reversed(terms))


def wide6(x):
    h, m, l = split3(x)
    return jnp.concatenate([h, h, m, m, h, l], axis=1)


def tall6(w):
    h, m, l = split3(w)
    return jnp.concatenate([h, m, h, m, l, h], axis=0)


def wide3(x):
    high, low = split(x)
    return jnp.concatenate([high, high, low], axis=1)


def wide(x):
    high, low = split(x)
    return jnp.concatenate([high, low, high], axis=1)


def tall(w):
    high, low = split(w)
    return jnp.concatenate([high, high, low], axis=0)


def across(w):
    high, low = split(w)
    return jnp.concatenate([high, high, low], axis=1)


def lanes(x, p):
    return x[..., p * LANES : (p + 1) * LANES]


def first_half(shape):
    return lax.broadcasted_iota(jnp.int32, shape, len(shape) - 1) < HEAD_DIM


def block_diagonal(square):
    rows = lax.broadcasted_iota(jnp.int32, square.shape, 0) < HEAD_DIM
    return jnp.where(rows == first_half(square.shape), square, 0.0)


def head_mean(x):
    rows = lax.broadcasted_iota(jnp.int32, (LANES, LANES), 0) < HEAD_DIM
    ones = jnp.where(rows == first_half((LANES, LANES)), 1.0 / HEAD_DIM, 0.0).astype(BF16)
    high, low = split(x)
    return dot(
        jnp.concatenate([high, low], axis=1), jnp.concatenate([ones, ones], axis=0)
    )


def head_means(x):
    return jnp.concatenate([head_mean(lanes(x, p)) for p in range(PAIRS)], axis=1)


def stacked_heads(x):
    keep = first_half(x.shape)
    zero = jnp.zeros_like(x)
    return jnp.concatenate([jnp.where(keep, x, zero), jnp.where(keep, zero, x)], axis=0)


def merged_heads(x):
    rows = x.shape[0] // 2
    return jnp.where(first_half((rows, LANES)), x[:rows], x[rows:])


def sigmoid(x):
    return 1.0 / (1.0 + jnp.exp(-x))


def shifted(x, step):
    rows = x.shape[0]
    column = lax.broadcasted_iota(jnp.int32, x.shape, 0) % GRID
    if step == 1:
        return jnp.where(column == 0, 0.0, pltpu.roll(x, 1, 0))
    return jnp.where(column == GRID - 1, 0.0, pltpu.roll(x, rows - 1, 0))


def normalized(x):
    center = x - jnp.mean(x, axis=-1, keepdims=True)
    rate = lax.rsqrt(jnp.mean(center * center, axis=-1, keepdims=True) + 1e-06)
    return center * rate, rate


def normal_back(dhat, hat, rate):
    return rate * (
        dhat
        - jnp.mean(dhat, axis=-1, keepdims=True)
        - hat * jnp.mean(dhat * hat, axis=-1, keepdims=True)
    )


def triangle(size, upper):
    rows = lax.broadcasted_iota(jnp.int32, (size, size), 0)
    cols = lax.broadcasted_iota(jnp.int32, (size, size), 1)
    return jnp.where(cols >= rows if upper else cols <= rows, 1.0, 0.0).astype(BF16)


def running_sum(x, upper):
    tri = triangle(x.shape[0], upper)
    high = x.astype(BF16)
    rest = x - high.astype(F32)
    middle = rest.astype(BF16)
    low = (rest - middle.astype(F32)).astype(BF16)
    return dot(tri, high) + dot(tri, middle) + dot(tri, low)


def opening(tile):
    return (lax.axis_index("seq") == 0) & (tile == 0)


def spread(compact):
    keep = first_half(compact.shape)
    return jnp.concatenate(
        [jnp.where(keep, compact, 0.0), jnp.where(keep, 0.0, compact)], axis=0
    )


def linked(parts, p):
    total = jnp.zeros((HEAD_DIM, LANES), F32)
    for part in reversed(parts):
        total = part[p, 0:HEAD_DIM, :] + part[p, HEAD_DIM : HEAD_DIM + 1, :] * total
    return spread(total)


def as_column(row):
    return jnp.broadcast_to(row, (8, row.shape[1])).T[:, 0:1]


def applied(row, w_ref):
    return jnp.sum(as_column(row) * w_ref[...], axis=0, keepdims=True)


def condition_kernel(ids_ref, feat_ref, first_w_ref, second_w_ref, row_ref, ada_ref, bias_ref, mod_ref, info_ref):
    features = feat_ref[...]
    first = applied(features, first_w_ref)
    embed = applied(first * sigmoid(first), second_w_ref)
    at = lax.broadcasted_iota(jnp.int32, row_ref.shape, 0) == ids_ref[pl.program_id(0)] % 8
    embed = embed + jnp.sum(jnp.where(at, row_ref[...], 0.0), axis=0, keepdims=True)
    modul = applied(embed * sigmoid(embed), ada_ref)
    for j in range(6):
        at = slice(j * WIDTH, (j + 1) * WIDTH)
        mod_ref[j : j + 1, :] = modul[:, at] + bias_ref[at][None, :]
    info_ref[...] = jnp.zeros_like(info_ref)
    info_ref[0:1, 0:FREQ] = features
    info_ref[1:2, :] = first
    info_ref[2:3, :] = embed
    info_ref[3:4, :] = jnp.full((1, WIDTH), ids_ref[pl.program_id(0)], jnp.int32).astype(F32)


def embed_kernel(
    ids_ref, rows_ref, ada_ref, second_ref, gf_ref, gs_ref, gc_ref, ga_ref, gb_ref, gt_ref
):
    images = rows_ref.shape[0]
    features, first, embed = rows_ref[:, 6, 0:FREQ], rows_ref[:, 7, :], rows_ref[:, 8, :]
    gt_ref[...] = jnp.sum(rows_ref[:, 10:19, :], axis=0)

    def silu_back(x, grad):
        sig = sigmoid(x)
        return grad * (sig * (1.0 + x * (1.0 - sig)))

    act = split((embed * sigmoid(embed)).T)
    dembed = jnp.zeros((images, WIDTH), F32)
    for j in range(6):
        at = slice(j * WIDTH, (j + 1) * WIDTH)
        grad = rows_ref[:, j, :]
        dmod = split(grad)
        ga_ref[:, at] = mm3(act, dmod)
        gb_ref[at] = jnp.sum(grad, axis=0)
        dembed = dembed + mm3(dmod, split(ada_ref[:, at]), 1, 1)
    dembed = silu_back(embed, dembed)
    gc_ref[...] = jnp.zeros_like(gc_ref)

    def put(n, carry):
        mine = lax.broadcasted_iota(jnp.int32, (images, WIDTH), 0) == n
        row = jnp.sum(jnp.where(mine, dembed, 0.0), axis=0, keepdims=True)
        gc_ref[pl.ds(ids_ref[n], 1), :] += row
        return carry

    lax.fori_loop(0, images, put, 0)
    de = split(dembed)
    gs_ref[...] = mm3(split((first * sigmoid(first)).T), de)
    dfirst = silu_back(first, mm3(de, split(second_ref[...]), 1, 1))
    gf_ref[...] = mm3(split(features.T), split(dfirst))


def front_kernel(
    tok_ref,
    top_ref,
    bot_ref,
    valid_ref,
    mod_ref,
    taps_ref,
    wq_ref,
    wk_ref,
    wv_ref,
    down_ref,
    up_ref,
    bias_ref,
    w_ref,
    normed_ref,
    conv_ref,
    q_ref,
    k_ref,
    v_ref,
    cum_ref,
    slope_ref,
    far_ref,
    state_ref,
    fade_ref,
    out_ref,
    w3_ref,
    proj_ref,
    st_ref,
    dev_ref,
):
    image, i = pl.program_id(0), pl.program_id(1)
    length = tok_ref.shape[0]

    @pl.when((image == 0) & (i == 0))
    def _():
        w_ref[:, 0:WIDTH] = wq_ref[...] * HEAD_DIM ** (-0.5)
        w_ref[:, WIDTH : 2 * WIDTH] = wk_ref[...]
        w_ref[:, 2 * WIDTH : 3 * WIDTH] = wv_ref[...]
        w_ref[:, 3 * WIDTH :] = mm6(split3(down_ref[...]), split3(up_ref[...]), 0, 0)
        w3_ref[...] = tall6(w_ref[...])

    real = jnp.sum(valid_ref[...], axis=1, keepdims=True)
    shift = mod_ref[0:1, :]
    scale = 1.0 + mod_ref[1:2, :]

    def modulated(x):
        return normalized(x)[0] * scale + shift

    @pl.when(i == 0)
    def _():
        normed_ref[0:GRID, :] = jnp.where(
            lax.axis_index("seq") == 0, 0.0, modulated(top_ref[...])
        )
        normed_ref[pl.ds(length + GRID, GRID), :] = jnp.where(
            lax.axis_index("seq") == lax.axis_size("seq") - 1, 0.0, modulated(bot_ref[...])
        )
        for at in range(0, length, TILE):
            normed_ref[GRID + at : GRID + at + TILE, :] = modulated(tok_ref[at : at + TILE, :])
        st_ref[...] = jnp.zeros_like(st_ref)
        dev_ref[...] = jnp.zeros_like(dev_ref)

    start = pl.multiple_of(i * TILE, TILE)
    rows = [normed_ref[pl.ds(start + a * GRID, TILE), :] for a in range(3)]
    parts = [
        sum(taps_ref[3 * a + b : 3 * a + b + 1, :] * rows[a] for a in range(3))
        for b in range(3)
    ]
    conv = shifted(parts[0], 1) + parts[1] + shifted(parts[2], -1)
    conv_ref[...] = conv
    hidden = conv * sigmoid(conv)
    first = opening(i)

    @pl.when(first)
    def _():
        proj_ref[...] = dot(wide6(hidden), w3_ref[...])

    @pl.when(jnp.logical_not(first))
    def _():
        proj_ref[...] = dot(wide3(hidden), w3_ref[0 : 3 * WIDTH, :])

    proj = proj_ref[...]
    keep = (
        lax.broadcasted_iota(jnp.int32, (TILE, WIDTH), 0) + start < real
    )
    q = proj[:, :WIDTH]
    k = jnp.where(keep, proj[:, WIDTH : 2 * WIDTH], 0.0)
    v = jnp.where(keep, proj[:, 2 * WIDTH : 3 * WIDTH], 0.0)
    x = proj[:, 3 * WIDTH :] + bias_ref[...][None, :]
    small = jnp.exp(-jnp.abs(x))
    gates = jnp.where(keep, (jnp.minimum(x, 0.0) - jnp.log1p(small)) * (1.0 / 16.0), 0.0)
    slope = jnp.where(x >= 0, small, 1.0) / (1.0 + small)
    slope_ref[...] = jnp.where(keep, slope * (1.0 / 16.0), 0.0)
    q_ref[...] = q
    k_ref[...] = k
    v_ref[...] = v
    for c in range(TILE // CHUNK):
        at = slice(c * CHUNK, (c + 1) * CHUNK)
        cum = running_sum(gates[at], False)
        cum_ref[at, :] = cum
        final = cum[CHUNK - 1 : CHUNK, :]
        dev = dev_ref[0:1, :]
        far_ref[at, :] = q[at] * jnp.exp(cum + dev)
        fade_ref[c] = jnp.broadcast_to(jnp.exp(dev), (8, WIDTH))
        kd = k[at] * jnp.exp(final - cum)
        factor = jnp.exp(final)
        for p in range(PAIRS):
            state_ref[c, p] = st_ref[p]
            update = mm3(split(lanes(v[at], p)), split(lanes(kd, p)), 0, 0)
            st_ref[p] = lanes(factor, p) * st_ref[p] + block_diagonal(update)
        dev_ref[...] = dev_ref[...] + final

    @pl.when(i == pl.num_programs(1) - 1)
    def _():
        for p in range(PAIRS):
            out_ref[p, 0:HEAD_DIM, :] = st_ref[p, 0:HEAD_DIM, :] + st_ref[p, HEAD_DIM:, :]
            out_ref[p, HEAD_DIM:, :] = jnp.exp(lanes(dev_ref[...], p))


def exact_scores(q_ref, k_ref, cum_ref, base, s_ref):
    q = q_ref[pl.ds(base, CHUNK), :]
    cum = cum_ref[pl.ds(base, CHUNK), :]
    s_ref[...] = jnp.zeros_like(s_ref)

    def step(j, carry):
        key = k_ref[pl.ds(base + j, 1), :]
        weight = jnp.exp(jnp.minimum(cum - cum_ref[pl.ds(base + j, 1), :], 0.0))
        terms = q * key * weight
        for p in range(PAIRS):
            column = jnp.sum(stacked_heads(lanes(terms, p)), axis=1, keepdims=True)
            at = lax.broadcasted_iota(jnp.int32, (2 * CHUNK, CHUNK), 1) == j
            s_ref[p] = jnp.where(at, column, s_ref[p])
        return carry

    lax.fori_loop(0, CHUNK, step, 0)


def causal_two():
    rows = lax.broadcasted_iota(jnp.int32, (2 * CHUNK, CHUNK), 0) % CHUNK
    return rows >= lax.broadcasted_iota(jnp.int32, (2 * CHUNK, CHUNK), 1)


def inner_kernel(
    q_ref, k_ref, v_ref, cum_ref, state_ref, normed_ref, gate_ref, o_ref, s_ref, gp_ref, w3_ref, tmp_ref
):
    @pl.when((pl.program_id(0) == 0) & (pl.program_id(1) == 0))
    def _():
        w3_ref[...] = tall(gate_ref[...])

    start = pl.multiple_of(pl.program_id(1) * TILE + GRID, GRID)
    gp_ref[...] = dot(wide(normed_ref[pl.ds(start, TILE), :]), w3_ref[...])
    mask = causal_two()
    for c in range(TILE // CHUNK):
        base = c * CHUNK
        at = slice(base, base + CHUNK)
        q = q_ref[at, :]
        k = k_ref[at, :]
        cum = cum_ref[at, :]
        final = cum[CHUNK - 1 : CHUNK, :]
        wild = jnp.max(-final) > SPAN
        middle = 0.5 * final
        qf = split3(q * jnp.exp(cum - middle))
        kf = split3(k * jnp.exp(middle - cum))
        for p in range(PAIRS):
            qp = tuple(stacked_heads(lanes(part, p)) for part in qf[:2])
            kp = tuple(lanes(part, p) for part in kf[:2])
            tmp_ref[p] = mm3(qp, kp, 1, 1)

        @pl.when(opening(pl.program_id(1)) if c == 0 else False)
        def _():
            for p in range(PAIRS):
                qp = tuple(stacked_heads(lanes(part, p)) for part in qf)
                kp = tuple(lanes(part, p) for part in kf)
                tmp_ref[p] = mm6(qp, kp, 1, 1)

        @pl.when(wild)
        def _():
            exact_scores(q_ref, k_ref, cum_ref, base, tmp_ref)

        qd = q * jnp.exp(cum)
        for p in range(PAIRS):
            s = jnp.where(mask, tmp_ref[p], 0.0)
            s_ref[c, p] = s
            inner = merged_heads(mm3(split(s), split(lanes(v_ref[at, :], p))))
            outer = mm3(split(lanes(qd, p)), split(state_ref[c, p]), 1, 1)
            o_ref[at, p * LANES : (p + 1) * LANES] = inner + outer


def mix_kernel(o_ref, far_ref, tok_ref, gp_ref, mod_ref, out_w_ref, *rest):
    parts, (mid_ref, branch_ref, att_ref, st_ref, o3_ref) = rest[:-5], rest[-5:]
    image, tile = pl.program_id(0), pl.program_id(1)

    @pl.when((image == 0) & (tile == 0))
    def _():
        o3_ref[...] = tall(out_w_ref[...])

    @pl.when(tile == 0)
    def _():
        for p in range(PAIRS):
            st_ref[p] = linked(parts, p)

    far = split(far_ref[...])
    att = o_ref[...] + jnp.concatenate(
        [
            mm3(tuple(lanes(part, p) for part in far), split(st_ref[p]), 1, 1)
            for p in range(PAIRS)
        ],
        axis=1,
    )
    att_ref[...] = att
    rate = lax.rsqrt(head_means(att * att) + 1e-05)
    gp = gp_ref[...]
    branch = dot(wide(att * rate * (gp * sigmoid(gp))), o3_ref[...])
    branch_ref[...] = branch
    mid_ref[...] = tok_ref[...] + mod_ref[2:3, :] * branch


def mlp_kernel(
    mid_ref, cot_ref, mod_ref, up_ref, down_ref, block_ref, dmid_ref, dmod_ref, send_ref, keep_ref, u3_ref, ut_ref, d_ref, dt3_ref, gu_ref, gd_ref
):
    image, tile = pl.program_id(0), pl.program_id(1)
    units = up_ref.shape[1]

    @pl.when((image == 0) & (tile == 0))
    def _():
        u3_ref[...] = tall(up_ref[...])
        ut_ref[...] = across(up_ref[...])
        d_ref[...] = tall(down_ref[...])
        dt3_ref[...] = across(down_ref[...])
        gu_ref[...] = jnp.zeros_like(gu_ref)
        gd_ref[...] = jnp.zeros_like(gd_ref)

    @pl.when(tile == 0)
    def _():
        dmod_ref[...] = jnp.zeros_like(dmod_ref)

    shift_b = mod_ref[3:4, :]
    scale_b = 1.0 + mod_ref[4:5, :]
    gate_b = mod_ref[5:6, :]
    middle = mid_ref[...]
    hat, rate_b = normalized(middle)
    second = hat * scale_b + shift_b
    cot = cot_ref[...]
    dmlp = cot * gate_b
    u = dot(wide(second), u3_ref[...])
    square = u * u
    th = jnp.tanh(GELU_C * (u + 0.044715 * u * square))
    slope = 0.5 * (1.0 + th) + 0.5 * u * (1.0 - th * th) * (
        GELU_C * (1.0 + 3.0 * 0.044715 * square)
    )
    act = split(0.5 * u * (1.0 + th))
    mlp = dot(jnp.concatenate([act[0], act[1], act[0]], axis=1), d_ref[...])
    du = split(dot(wide(dmlp), dt3_ref[...], 1, 1) * slope)
    dsec = dot(jnp.concatenate([du[0], du[1], du[0]], axis=1), ut_ref[...], 1, 1)
    gu_ref[...] += dot(wide(second.T), jnp.concatenate([du[0], du[0], du[1]], axis=0))
    gd_ref[...] += dot(wide(dmlp.T), jnp.concatenate([act[0], act[0], act[1]], axis=0))
    block_ref[...] = middle + gate_b * mlp
    dmid_ref[...] = cot + normal_back(dsec * scale_b, hat, rate_b)
    dmod_ref[3:4, :] += jnp.sum(dsec, axis=0, keepdims=True)
    dmod_ref[4:5, :] += jnp.sum(dsec * hat, axis=0, keepdims=True)
    dmod_ref[5:6, :] += jnp.sum(cot * mlp, axis=0, keepdims=True)

    @pl.when((image == pl.num_programs(0) - 1) & (tile == pl.num_programs(1) - 1))
    def _():
        def lower(ref):
            for j in range(units // WIDTH):
                at = slice(j * WIDTH, (j + 1) * WIDTH)
                ref[at, :] = gu_ref[:, at]

        def upper(ref):
            ref[...] = gd_ref[...].T

        halves_out(lower, upper, send_ref, keep_ref)


def mix_back_kernel(
    dmid_ref,
    branch_ref,
    att_ref,
    gp_ref,
    far_ref,
    normed_ref,
    mod_ref,
    message_ref,
    out_w_ref,
    gate_w_ref,
    datt_ref,
    dnorm_ref,
    send_ref,
    keep_ref,
    dmod_ref,
    dmessage_ref,
    g_ref,
    ot3_ref,
    gt3_ref,
    dst_ref,
):
    image, tile = pl.program_id(0), pl.program_id(1)

    @pl.when((image == 0) & (tile == 0))
    def _():
        ot3_ref[...] = across(out_w_ref[...])
        gt3_ref[...] = across(gate_w_ref[...])
        g_ref[...] = jnp.zeros_like(g_ref)

    @pl.when(tile == 0)
    def _():
        dmod_ref[...] = jnp.zeros_like(dmod_ref)
        dst_ref[...] = jnp.zeros_like(dst_ref)

    dmid = dmid_ref[...]
    dmod_ref[2:3, :] += jnp.sum(dmid * branch_ref[...], axis=0, keepdims=True)
    dbr = split(dmid * mod_ref[2:3, :])
    dy = dot(jnp.concatenate([dbr[0], dbr[1], dbr[0]], axis=1), ot3_ref[...], 1, 1)
    att = att_ref[...]
    rate = lax.rsqrt(head_means(att * att) + 1e-05)
    unit = att * rate
    gp = gp_ref[...]
    sig = sigmoid(gp)
    gate = gp * sig
    g_ref[0:WIDTH, :] += dot(
        wide((unit * gate).T), jnp.concatenate([dbr[0], dbr[0], dbr[1]], axis=0)
    )
    dunit = dy * gate
    datt = rate * (dunit - unit * head_means(dunit * unit))
    datt_ref[...] = datt
    dg = split((dy * unit) * (sig * (1.0 + gp * (1.0 - sig))))
    dnorm_ref[...] = dot(jnp.concatenate([dg[0], dg[1], dg[0]], axis=1), gt3_ref[...], 1, 1)
    start = pl.multiple_of(tile * TILE + GRID, GRID)
    g_ref[WIDTH:, :] += dot(
        wide(normed_ref[pl.ds(start, TILE), :].T), jnp.concatenate([dg[0], dg[0], dg[1]], axis=0)
    )
    da = split(datt)
    far = split(far_ref[...])
    for p in range(PAIRS):
        dst_ref[p] += block_diagonal(
            mm3(tuple(lanes(part, p) for part in da), tuple(lanes(part, p) for part in far), 0, 0)
        )

    @pl.when(tile == pl.num_programs(1) - 1)
    def _():
        for p in range(PAIRS):
            dmessage_ref[p, 0:HEAD_DIM, :] = dst_ref[p, 0:HEAD_DIM, :] + dst_ref[p, HEAD_DIM:, :]
            dmessage_ref[p, HEAD_DIM:, :] = message_ref[p, HEAD_DIM:, :]

    @pl.when((image == pl.num_programs(0) - 1) & (tile == pl.num_programs(1) - 1))
    def _():
        def lower(ref):
            ref[...] = g_ref[0:WIDTH, :]

        def upper(ref):
            ref[...] = g_ref[WIDTH:, :]

        halves_out(lower, upper, send_ref, keep_ref)


def exact_back(q_ref, k_ref, cum_ref, ds_ref, base, dq_ref, dk_ref):
    q = q_ref[pl.ds(base, CHUNK), :]
    cum = cum_ref[pl.ds(base, CHUNK), :]
    dq_ref[...] = jnp.zeros_like(dq_ref)

    def step(j, carry):
        key = k_ref[pl.ds(base + j, 1), :]
        weight = jnp.exp(jnp.minimum(cum - cum_ref[pl.ds(base + j, 1), :], 0.0))
        at = lax.broadcasted_iota(jnp.int32, (2 * CHUNK, CHUNK), 1) == j
        columns = []
        for p in range(PAIRS):
            column = jnp.sum(jnp.where(at, ds_ref[p], 0.0), axis=1, keepdims=True)
            columns.append(merged_heads(jnp.broadcast_to(column, (2 * CHUNK, LANES))))
        ds = jnp.concatenate(columns, axis=1) * weight
        dq_ref[...] += ds * key
        dk_ref[pl.ds(j, 1), :] = jnp.sum(ds * q, axis=0, keepdims=True)
        return carry

    lax.fori_loop(0, CHUNK, step, 0)


def inner_back_kernel(
    q_ref,
    k_ref,
    v_ref,
    cum_ref,
    datt_ref,
    s_ref,
    state_ref,
    fade_ref,
    st_ref,
    dq_ref,
    dk_ref,
    dv_ref,
    full_ref,
    ds_ref,
    dqi_ref,
    dki_ref,
):
    mask = causal_two()
    for c in range(TILE // CHUNK):
        base = c * CHUNK
        at = slice(base, base + CHUNK)
        q = q_ref[at, :]
        k = k_ref[at, :]
        cum = cum_ref[at, :]
        final = cum[CHUNK - 1 : CHUNK, :]
        wild = jnp.max(-final) > SPAN
        middle = 0.5 * final
        eq = jnp.exp(cum - middle)
        ek = jnp.exp(middle - cum)
        qf = split(q * eq)
        kf = split(k * ek)
        da = split3(datt_ref[at, :])
        vs = split3(v_ref[at, :])
        for p in range(PAIRS):
            da2 = tuple(stacked_heads(lanes(part, p)) for part in da[:2])
            vp = tuple(lanes(part, p) for part in vs[:2])
            ds_ref[p] = jnp.where(mask, mm3(da2, vp, 1, 1), 0.0)

        @pl.when(opening(pl.program_id(1)) if c == 0 else False)
        def _():
            for p in range(PAIRS):
                da2 = tuple(stacked_heads(lanes(part, p)) for part in da)
                vp = tuple(lanes(part, p) for part in vs)
                ds_ref[p] = jnp.where(mask, mm6(da2, vp, 1, 1), 0.0)

        for p in range(PAIRS):
            da2 = tuple(stacked_heads(lanes(part, p)) for part in da[:2])
            ds2 = split(ds_ref[p])
            kp = tuple(lanes(part, p) for part in kf)
            qp = tuple(lanes(part, p) for part in qf)
            dqi_ref[:, p * LANES : (p + 1) * LANES] = merged_heads(mm3(ds2, kp)) * lanes(eq, p)
            q2 = tuple(stacked_heads(part) for part in qp)
            dki_ref[:, p * LANES : (p + 1) * LANES] = mm3(ds2, q2, 0, 0) * lanes(ek, p)
            s2 = split(s_ref[c, p])
            dv_ref[at, p * LANES : (p + 1) * LANES] = mm3(s2, da2, 0, 0)

        @pl.when(wild)
        def _():
            exact_back(q_ref, k_ref, cum_ref, ds_ref, base, dqi_ref, dki_ref)

        grow = jnp.exp(cum)
        for p in range(PAIRS):
            full = state_ref[c, p] + lanes(fade_ref[c, 0:1, :], p) * st_ref[p]
            full_ref[c, p] = full
            outer = mm3(tuple(lanes(part, p) for part in da[:2]), split(full))
            dq_ref[at, p * LANES : (p + 1) * LANES] = (
                dqi_ref[:, p * LANES : (p + 1) * LANES] + outer * lanes(grow, p)
            )
        dk_ref[at, :] = dki_ref[...]


def state_back_kernel(
    valid_ref,
    q_ref,
    k_ref,
    v_ref,
    cum_ref,
    slope_ref,
    datt_ref,
    dq_ref,
    dk_ref,
    dv_ref,
    full_ref,
    conv_ref,
    down_ref,
    up_ref,
    *rest,
):
    parts, (proj_ref, send_ref, keep_ref, dst_ref, dbias_ref, acc_ref, g_ref) = rest[:-7], rest[-7:]
    image, turn = pl.program_id(0), pl.program_id(1)
    tile = pl.num_programs(1) - 1 - turn

    @pl.when((image == 0) & (turn == 0))
    def _():
        dbias_ref[...] = jnp.zeros_like(dbias_ref)
        acc_ref[...] = jnp.zeros_like(acc_ref)

    @pl.when(turn == 0)
    def _():
        for p in range(PAIRS):
            dst_ref[p] = linked(parts, p)

    count = jnp.sum(valid_ref[...], axis=1, keepdims=True)
    keep = (
        lax.broadcasted_iota(jnp.int32, (CHUNK, WIDTH), 0) + tile * TILE
    )
    for c in reversed(range(TILE // CHUNK)):
        at = slice(c * CHUNK, (c + 1) * CHUNK)
        q = q_ref[at, :]
        k = k_ref[at, :]
        cum = cum_ref[at, :]
        final = cum[CHUNK - 1 : CHUNK, :]
        late = jnp.exp(final - cum)
        kd = k * late
        v = v_ref[at, :]
        qd = split(q * jnp.exp(cum))
        da = split(datt_ref[at, :])
        factor = jnp.exp(final)
        dk_parts, dv_parts, cross = [], [], []
        for p in range(PAIRS):
            old = dst_ref[p]
            pair = split(old)
            dk_parts.append(mm3(split(lanes(v, p)), pair))
            dv_parts.append(mm3(split(lanes(kd, p)), pair, 1, 1))
            leaving = lanes(factor, p) * full_ref[c, p] + block_diagonal(
                mm3(split(lanes(v, p)), split(lanes(kd, p)), 0, 0)
            )
            cross.append(jnp.sum(leaving * old, axis=0, keepdims=True))
            update = mm3(
                tuple(lanes(part, p) for part in da), tuple(lanes(part, p) for part in qd), 0, 0
            )
            dst_ref[p] = lanes(factor, p) * old + block_diagonal(update)
        dq = dq_ref[at, :]
        dk = dk_ref[at, :] + jnp.concatenate(dk_parts, axis=1) * late
        dv = dv_ref[at, :] + jnp.concatenate(dv_parts, axis=1)
        dgates = running_sum(q * dq - k * dk, True) + jnp.concatenate(cross, axis=1)
        dx = dgates * slope_ref[at, :]
        real = keep + c * CHUNK < count
        dk = jnp.where(real, dk, 0.0)
        dv = jnp.where(real, dv, 0.0)
        dbias_ref[...] += jnp.sum(dx.reshape(CHUNK // 8, 8, WIDTH), axis=0)
        proj_ref[at, 0:WIDTH] = dq
        proj_ref[at, WIDTH : 2 * WIDTH] = dk
        proj_ref[at, 2 * WIDTH : 3 * WIDTH] = dv
        proj_ref[at, 3 * WIDTH :] = dx
    conv = conv_ref[...]
    proj = split(proj_ref[...])
    acc_ref[...] += dot(
        wide((conv * sigmoid(conv)).T), jnp.concatenate([proj[0], proj[0], proj[1]], axis=0)
    )

    @pl.when((image == pl.num_programs(0) - 1) & (tile == 0))
    def _():
        for j in range(3):
            grad = acc_ref[:, j * WIDTH : (j + 1) * WIDTH]
            g_ref[j * WIDTH : (j + 1) * WIDTH, :] = (
                grad * HEAD_DIM ** (-0.5) if j == 0 else grad
            )
        grad = acc_ref[:, 3 * WIDTH :]
        base = 3 * WIDTH
        rank = up_ref.shape[0]
        g_ref[base:, :] = jnp.zeros_like(g_ref[base:, :])
        g_ref[base : base + rank, :] = mm6(split3(up_ref[...]), split3(grad), 1, 1)
        g_ref[base + rank : base + 2 * rank, :] = mm6(split3(down_ref[...]), split3(grad))
        g_ref[base + 2 * rank : base + 2 * rank + 1, :] = jnp.sum(
            dbias_ref[...], axis=0, keepdims=True
        )

        def lower(ref):
            ref[...] = g_ref[0 : ROWS // 2, :]

        def upper(ref):
            ref[...] = g_ref[ROWS // 2 :, :]

        halves_out(lower, upper, send_ref, keep_ref)


def hidden_kernel(proj_ref, conv_ref, w_ref, dconv_ref, wt3_ref):
    @pl.when((pl.program_id(0) == 0) & (pl.program_id(1) == 0))
    def _():
        wt3_ref[...] = across(w_ref[...])

    dhidden = dot(wide(proj_ref[...]), wt3_ref[...], 1, 1)
    conv = conv_ref[...]
    sig = sigmoid(conv)
    dconv_ref[...] = dhidden * (sig * (1.0 + conv * (1.0 - sig)))


def front_back_kernel(
    tok_ref,
    normed_ref,
    dconv_ref,
    top_ref,
    bot_ref,
    dnorm_ref,
    dmid_ref,
    mod_ref,
    taps_ref,
    mlp_ref,
    mix_ref,
    info_ref,
    grad_ref,
    rows_ref,
    dmod_ref,
    pad_ref,
    taps_acc_ref,
):
    length = dconv_ref.shape[0]
    image, i = pl.program_id(0), pl.program_id(1)

    @pl.when(i == 0)
    def _():
        taps_acc_ref[...] = jnp.zeros_like(taps_acc_ref)

    @pl.when(i == 0)
    def _():
        dmod_ref[...] = jnp.zeros_like(dmod_ref)
        pad_ref[0:GRID, :] = top_ref[...]
        pad_ref[pl.ds(length + GRID, GRID), :] = bot_ref[...]
        pad_ref[pl.ds(GRID, length), :] = dconv_ref[...]

    scale = 1.0 + mod_ref[1:2, :]

    def eights(x):
        return jnp.sum(x.reshape(x.shape[0] // 8, 8, WIDTH), axis=0)

    start = pl.multiple_of(i * TILE, TILE)
    rows = [pad_ref[pl.ds(start + (2 - a) * GRID, TILE), :] for a in range(3)]
    parts = [
        sum(taps_ref[3 * a + b : 3 * a + b + 1, :] * rows[a] for a in range(3))
        for b in range(3)
    ]
    dn = (
        shifted(parts[0], -1)
        + parts[1]
        + shifted(parts[2], 1)
        + dnorm_ref[...]
    )
    hat, rate = normalized(tok_ref[...])
    grad_ref[...] = dmid_ref[...] + normal_back(
        dn * scale, hat, rate
    )
    dmod_ref[0:1, :] += jnp.sum(dn, axis=0, keepdims=True)
    dmod_ref[1:2, :] += jnp.sum(dn * hat, axis=0, keepdims=True)
    own = rows[1]
    moved = [shifted(own, -1), own, shifted(own, 1)]
    for a in range(3):
        near = normed_ref[pl.ds(start + a * GRID, TILE), :]
        for b in range(3):
            taps_acc_ref[3 * a + b] += eights(moved[b] * near)

    @pl.when(i == pl.num_programs(1) - 1)
    def _():
        own = lax.axis_index("seq") == 0
        rows_ref[...] = jnp.zeros_like(rows_ref)
        rows_ref[0:6, :] = (dmod_ref[...] + mlp_ref[...] + mix_ref[...])[0:6, :]
        rows_ref[6:10, :] = jnp.where(own, info_ref[0:4, :], 0.0)
        for t in range(9):
            rows_ref[10 + t : 11 + t, :] = jnp.sum(taps_acc_ref[t], axis=0, keepdims=True)


def call(kernel, grid, ins, outs, scratch, flops=0, moved=0, prefetch=0, limit=24):
    return pl.pallas_call(
        kernel,
        grid_spec=pltpu.PrefetchScalarGridSpec(
            num_scalar_prefetch=prefetch,
            grid=grid,
            in_specs=ins,
            out_specs=[spec for spec, _ in outs],
            scratch_shapes=scratch,
        ),
        out_shape=[jax.ShapeDtypeStruct(shape, F32) for _, shape in outs],
        compiler_params=pltpu.CompilerParams(vmem_limit_bytes=limit * 1024 * 1024),
        cost_estimate=pl.CostEstimate(flops=4 * flops, bytes_accessed=4 * moved, transcendentals=0),
    )


def whole(shape):
    zeros = (0,) * len(shape)
    return pl.BlockSpec(shape, lambda *_: zeros, pipeline_mode=pl.Buffered(1))


def per_image(shape):
    zeros = (0,) * len(shape)
    return pl.BlockSpec((None,) + shape, lambda n, *_: (n,) + zeros)


def time_features(timesteps):
    half = FREQ // 2
    freqs = jnp.exp(-math.log(10000.0) * jnp.arange(half, dtype=F32) / half)
    angles = timesteps.astype(F32)[:, None] * freqs[None, :]
    return jnp.concatenate([jnp.cos(angles), jnp.sin(angles)], axis=1)


def halves(axis):
    return [1 << b for b in range(lax.axis_size(axis).bit_length() - 1)]


def swapped(x, axis, bit):
    return lax.ppermute(x, axis, [(i, i ^ bit) for i in range(lax.axis_size(axis))])


def is_high(axis, bit):
    return (lax.axis_index(axis) // bit) % 2


def step_kernel(items, *refs):
    ins, outs = refs[: 2 * len(items)], list(refs[2 * len(items) :])
    for n, (kind, link) in enumerate(items):
        own, got = ins[2 * n], ins[2 * n + 1]
        if kind == "sum":
            outs.pop(0)[...] = own[...] + got[...]
        elif kind == "join":
            out, size, high = outs.pop(0), own.shape[0], is_high(*link) == 1
            out[0:size] = jnp.where(high, got[...], own[...])
            out[size:] = jnp.where(high, own[...], got[...])
        else:
            half = own.shape[0] // 2
            high = is_high(*link)
            for side in (1 - high, high):
                start = side * half
                at = pl.ds(pl.multiple_of(start, 8) if half % 8 == 0 else start, half)
                outs.pop(0)[...] = own[at, :] + got[at, :]


def stepped(flows, got):
    items, arrays, shapes = [], [], []
    for flow, x in zip(flows, got):
        kind, link, own = flow.item()
        if kind == "split" and own.shape[0] % 16:
            flow.took_whole(own + x)
            continue
        items.append((flow, kind, link))
        arrays += [own, x]
        if kind == "split":
            shapes += [(own.shape[0] // 2, WIDTH)] * 2
        else:
            shapes.append((own.shape[0] * (2 if kind == "join" else 1),) + own.shape[1:])
    if not items:
        return
    outs = call(
        functools.partial(step_kernel, [item[1:] for item in items]),
        (1,),
        [whole(x.shape) for x in arrays],
        [(whole(shape), shape) for shape in shapes],
        [],
        flops=sum(x.size for x in arrays),
        moved=8 * sum(x.size for x in arrays),
        limit=24,
    )(*arrays)
    outs = list(outs)
    for flow, kind, _ in items:
        flow.took(*(outs.pop(0) for _ in range(2 if kind == "split" else 1)))


class Flow:
    def __init__(self, sent, keep, order):
        self.sent, self.keep = sent, keep
        self.order, self.used = list(order), []

    def busy(self):
        return bool(self.order)

    def send(self):
        return self.sent

    def link(self):
        return self.order[0]

    def item(self):
        self.used.append(self.order.pop(0))
        if self.order:
            return "split", self.order[0], self.keep
        return "sum", None, self.keep

    def took(self, *new):
        if len(new) == 2:
            self.sent, self.keep = new
        else:
            (self.keep,) = new

    def now(self):
        return self.sent if self.order else self.keep

    def took_whole(self, total):
        half = total.shape[0] // 2
        high = is_high(*self.order[0])
        self.sent = lax.dynamic_slice_in_dim(total, (1 - high) * half, half)
        self.keep = lax.dynamic_slice_in_dim(total, high * half, half)


class Spread:
    def __init__(self, x, used):
        self.x, self.used = x[None], list(used)

    def busy(self):
        return len(self.used) > 1

    def send(self):
        return self.x

    def link(self):
        return self.used[-1]

    def item(self):
        return "join", self.used.pop(), self.x

    def took(self, new):
        self.x = new

    def now(self):
        return self.x


class Rows:
    def __init__(self, x, sums, joins):
        self.x, self.sums, self.joins = x, list(sums), list(joins)

    def busy(self):
        return bool(self.sums or self.joins)

    def send(self):
        return self.x

    def link(self):
        return self.sums[0] if self.sums else self.joins[0]

    def item(self):
        if self.sums:
            self.sums.pop(0)
            return "sum", None, self.x
        return "join", self.joins.pop(0), self.x

    def took(self, new):
        self.x = new

    def now(self):
        return self.x


class Paired:
    def __init__(self, sent, keep, link):
        self.sent, self.keep, self.at, self.got = sent, keep, link, None

    def busy(self):
        return self.got is None

    def send(self):
        return self.sent

    def link(self):
        return self.at


def fork_kernel(parts, *refs):
    count = (len(refs) - 1 - 2 * len(parts)) // 2
    ins, outs, total = refs[: 2 * count], list(refs[2 * count : -1]), refs[-1]
    at = 0
    for n in range(count):
        rows = ins[2 * n].shape[0]
        total[at : at + rows, :] = ins[2 * n][...] + ins[2 * n + 1][...]
        at += rows
    for first, rows, link in parts:
        high = is_high(*link)
        for side in (1 - high, high):
            start = side * (rows // 2) + first
            outs.pop(0)[...] = total[pl.ds(pl.multiple_of(start, 8), rows // 2), :]


def forked(pairs, cuts, orders):
    rows = sum(cuts)
    starts = [sum(cuts[:n]) for n in range(len(cuts))]
    parts = [(start, cut, order[0]) for start, cut, order in zip(starts, cuts, orders)]
    arrays = [x for pair in pairs for x in (pair.keep, pair.got)]
    shapes = [(part[1] // 2, WIDTH) for part in parts for _ in range(2)]
    outs = call(
        functools.partial(fork_kernel, parts),
        (1,),
        [whole(x.shape) for x in arrays],
        [(whole(shape), shape) for shape in shapes],
        [pltpu.VMEM((rows, WIDTH), F32)],
        flops=rows * WIDTH,
        moved=12 * rows * WIDTH,
        limit=24,
    )(*arrays)
    return [Flow(outs[2 * n], outs[2 * n + 1], order) for n, order in enumerate(orders)]


def beside(flows, first, kernel):
    flows = [flow for flow in flows if flow.busy()]
    first, *sends = lax.optimization_barrier((first, *(flow.send() for flow in flows)))
    got = [swapped(x, *flow.link()) for flow, x in zip(flows, sends)]
    outs = kernel(first)
    head, *got = lax.optimization_barrier((outs[0], *got))
    for flow, x in zip(flows, got):
        if isinstance(flow, Paired):
            flow.got = x
    rest = [(flow, x) for flow, x in zip(flows, got) if not isinstance(flow, Paired)]
    stepped([flow for flow, _ in rest], [x for _, x in rest])
    return [head] + list(outs[1:])


def halves_out(lower, upper, send_ref, keep_ref):
    core = lax.axis_index("seq") % 2

    @pl.when(core == 0)
    def _():
        lower(keep_ref)
        upper(send_ref)

    @pl.when(core == 1)
    def _():
        lower(send_ref)
        upper(keep_ref)


def move_first(outs):
    return list(outs[1:]) + [outs[0]]


def messages(message, backward):
    size = lax.axis_size("seq")
    got = []
    for far in range(1, size):
        pairs = [(i, i + far) for i in range(size - far)]
        if backward:
            pairs = [(j, i) for i, j in pairs]
        got.append(lax.ppermute(message, "seq", pairs))
    return got


def plan(early_rows, pieces, units):
    late_rows = tuple(total // pieces for total in LATE)
    moves = []

    def place(kind, half, at):
        if kind == 0:
            if at >= units:
                return 2 + half, at - units, 0, units + WIDTH - at
            if half == 0:
                return 0, at % WIDTH, at // WIDTH, WIDTH - at % WIDTH
            return 1, at, 0, units - at
        row = half * (ROWS // 2) + at
        block = min(row // WIDTH, 3)
        room = ROWS // 2 - at
        return 4 + block, row - block * WIDTH, 0, min(room, WIDTH - row % WIDTH) if block < 3 else room

    for half in range(2):
        for kind in range(2):
            at = 0
            for flow in range(len(early_rows)):
                rows = early_rows[flow] if kind == 0 else late_rows[flow]
                base = 0 if kind == 0 else early_rows[flow]
                for piece in range(pieces):
                    done = 0
                    while done < rows:
                        out, row, block, room = place(kind, half, at)
                        span = min(rows - done, room)
                        moves.append((half, flow, piece, base + done, out, row, block, span))
                        done, at = done + span, at + span
    return moves


def assemble_kernel(moves, pieces, lasts, core, *refs):
    count = len(lasts)
    near, other, near_core, other_core = (refs[n * count : (n + 1) * count] for n in range(4))
    outs = refs[4 * count :]
    mine = is_high(*core)
    for half, flow, piece, row, out, start, block, span in moves:
        side, index = piece // (pieces // 2), piece % (pieces // 2)
        at = (index, slice(row, row + span), slice(None))
        own = is_high(*lasts[flow]) == side
        here = jnp.where(own, near[flow][at], other[flow][at])
        there = jnp.where(own, near_core[flow][at], other_core[flow][at])
        outs[out][start : start + span, block * WIDTH : (block + 1) * WIDTH] = jnp.where(
            mine == half, here, there
        )


def assembled(near, other, near_core, other_core, lasts, core, early, units):
    early_rows = tuple(flow.keep.shape[0] for flow in early)
    pieces = 2 * near[0].shape[0]
    moves = plan(early_rows, pieces, units)
    square = (WIDTH, WIDTH)
    shapes = [(WIDTH, units), (units, WIDTH)] + [square] * 5 + [(ROWS - 3 * WIDTH, WIDTH)]
    arrays = near + other + near_core + other_core
    return call(
        functools.partial(assemble_kernel, moves, pieces, lasts, core),
        (1,),
        [whole(x.shape) for x in arrays],
        [(whole(shape), shape) for shape in shapes],
        [],
        moved=4 * 4 * sum(x.size for x in near),
        limit=40,
    )(*arrays)


def body(
    tokens,
    valid_mask,
    timesteps,
    class_ids,
    time_first,
    time_second,
    class_table,
    ada_weight,
    ada_bias,
    conv_taps,
    query_proj,
    key_proj,
    value_proj,
    decay_down,
    decay_up,
    decay_bias,
    gate_proj,
    out_proj,
    mlp_up,
    mlp_down,
    cotangent,
):
    count, length, width = tokens.shape
    size, mine = lax.axis_size("seq"), lax.axis_index("seq")
    tiles, chunks = length // TILE, length // CHUNK
    per_tile = TILE // CHUNK
    up_pairs = [(i, i + 1) for i in range(size - 1)]
    down_pairs = [(j, i) for i, j in up_pairs]
    seq_bits = [("seq", bit) for bit in halves("seq")]
    img_bits = [("img", bit) for bit in halves("img")]
    core, order_a = seq_bits[0], seq_bits[1:] + img_bits
    order_b = img_bits[:2] + seq_bits[1:] + img_bits[2:]
    order_c = img_bits[2:] + seq_bits[1:] + img_bits[:2]
    orders = (order_a, order_b, order_c)

    def borders(x):
        return (
            lax.ppermute(x[:, length - GRID :], "seq", up_pairs),
            lax.ppermute(x[:, :GRID], "seq", down_pairs),
        )

    above, below = borders(tokens)

    square = (width, width)
    row = (length, width)
    dense = 2 * 3 * count * length * width
    each = 4 * count * length * width
    features = time_features(timesteps)
    mod_spec = per_image((6, width))
    modul, info = call(
        condition_kernel,
        (count,),
        [
            per_image((1, FREQ)),
            whole(time_first.shape),
            whole(time_second.shape),
            pl.BlockSpec((8, width), lambda n, ids: (ids[n] // 8, 0)),
            whole(ada_weight.shape),
            whole((6 * width,)),
        ],
        [
            (mod_spec, (count, 6, width)),
            (per_image((8, width)), (count, 8, width)),
        ],
        [],
        flops=1000000,
        moved=4 * 6 * width * width,
        prefetch=1,
        limit=60,
    )(class_ids, features[:, None], time_first, time_second, class_table, ada_weight, ada_bias)

    valid = valid_mask[:, None]
    valid_spec = per_image((1, length))
    message_shape = (PAIRS, HEAD_DIM + 8, LANES)
    def tiled(shape=(TILE, width)):
        return pl.BlockSpec((None,) + shape, lambda n, i: (n, i, 0))

    tile_row = (tiled(), (count,) + row)
    pair_spec = pl.BlockSpec(
        (None, per_tile, PAIRS, LANES, LANES), lambda n, i: (n, i, 0, 0, 0)
    )
    state_spec = pl.BlockSpec((None, PAIRS, LANES, LANES), lambda n, i: (n, 0, 0, 0))
    state_shape = (count, PAIRS, LANES, LANES)
    score_shape = (count, chunks, PAIRS, 2 * CHUNK, CHUNK)
    score_spec = pl.BlockSpec(
        (None, per_tile, PAIRS, 2 * CHUNK, CHUNK), lambda n, i: (n, i, 0, 0, 0)
    )
    normed_spec = per_image((length + 2 * GRID, width))
    message_spec = per_image(message_shape)
    fade_spec = pl.BlockSpec((None, per_tile, 8, width), lambda n, i: (n, i, 0, 0))
    (
        weights,
        normed,
        conv,
        query,
        keys,
        values,
        cumul,
        slope,
        far,
        states,
        fades,
        message,
    ) = call(
        front_kernel,
        (count, tiles),
        [
            per_image(row),
            per_image((GRID, width)),
            per_image((GRID, width)),
            valid_spec,
            mod_spec,
            whole((9, width)),
            whole(square),
            whole(square),
            whole(square),
            whole(decay_up.shape),
            whole(decay_up.shape),
            whole((width,)),
        ],
        [
            (whole((width, 4 * width)), (width, 4 * width)),
            (per_image((length + 2 * GRID, width)), (count, length + 2 * GRID, width)),
        ]
        + [tile_row] * 7
        + [
            (pair_spec, (count, chunks, PAIRS, LANES, LANES)),
            (fade_spec, (count, chunks, 8, width)),
            (message_spec, (count,) + message_shape),
        ],
        [
            pltpu.VMEM((6 * width, 4 * width), BF16),
            pltpu.VMEM((TILE, 4 * width), F32),
            pltpu.VMEM((PAIRS, LANES, LANES), F32),
            pltpu.VMEM((8, width), F32),
        ],
        flops=dense * 4 * width,
        moved=each * 10,
    )(
        tokens,
        above,
        below,
        valid,
        modul,
        conv_taps,
        query_proj,
        key_proj,
        value_proj,
        decay_down.T,
        decay_up,
        decay_bias,
    )

    forward_parts = messages(message, False)
    inner, scores, gate_in = call(
        inner_kernel,
        (count, tiles),
        [tiled()] * 4 + [pair_spec, normed_spec, whole(square)],
        [tile_row, (score_spec, score_shape), tile_row],
        [pltpu.VMEM((3 * width, width), BF16), pltpu.VMEM((PAIRS, 2 * CHUNK, CHUNK), F32)],
        flops=dense * 2 * width,
        moved=each * 9,
    )(query, keys, values, cumul, states, normed, gate_proj)

    middle, branch, attended, state_in = call(
        mix_kernel,
        (count, tiles),
        [tiled()] * 4 + [mod_spec, whole(square)] + [message_spec] * (size - 1),
        [tile_row] * 3 + [(state_spec, state_shape)],
        [pltpu.VMEM((3 * width, width), BF16)],
        flops=dense * 2 * width,
        moved=each * 7,
    )(inner, far, tokens, gate_in, modul, out_proj, *forward_parts)

    dmod_spec = per_image((8, width))
    dmod_out = (dmod_spec, (count, 8, width))

    units = mlp_up.shape[1]
    block_out, dmid, dmod_mlp, mlp_sent, mlp_kept = call(
        mlp_kernel,
        (count, tiles),
        [tiled(), tiled(), mod_spec, whole(mlp_up.shape), whole(mlp_down.shape)],
        [tile_row] * 2 + [dmod_out] + [(whole((units, width)), (units, width))] * 2,
        [
            pltpu.VMEM((3 * width, units), BF16),
            pltpu.VMEM((width, 3 * units), BF16),
            pltpu.VMEM((3 * units, width), BF16),
            pltpu.VMEM((units, 3 * width), BF16),
            pltpu.VMEM((width, units), F32),
            pltpu.VMEM((width, units), F32),
        ],        flops=dense * 6 * units,
        moved=each * 8,
        limit=40,
    )(middle, cotangent, modul, mlp_up, mlp_down)

    mlp_pair = Paired(mlp_sent, mlp_kept, core)
    datt, dnorm, mix_sent, mix_kept, dmod_mix, d_message = beside([mlp_pair], dmid, lambda x: call(
        mix_back_kernel,
        (count, tiles),
        [tiled()] * 5
        + [normed_spec, mod_spec, message_spec, whole(square), whole(square)],
        [tile_row] * 2
        + [(whole(square), square)] * 2
        + [dmod_out]
        + [(message_spec, (count,) + message_shape)],
        [
            pltpu.VMEM((2 * width, width), F32),
            pltpu.VMEM((width, 3 * width), BF16),
            pltpu.VMEM((width, 3 * width), BF16),
            pltpu.VMEM((PAIRS, LANES, LANES), F32),
        ],
        flops=dense * 5 * width,
        moved=each * 8,
        limit=60,
    )(x, branch, attended, gate_in, far, normed, modul, message, out_proj, gate_proj))
    mix_pair = Paired(mix_sent, mix_kept, core)
    d_message, datt = lax.optimization_barrier((d_message, datt))
    backward_parts = messages(d_message, True)

    dquery, dkeys, dvalues, full = beside([mix_pair], datt, lambda x: call(
        inner_back_kernel,
        (count, tiles),
        [tiled()] * 5 + [score_spec, pair_spec, fade_spec, state_spec],
        [tile_row] * 3 + [(pair_spec, (count, chunks, PAIRS, LANES, LANES))],
        [
            pltpu.VMEM((PAIRS, 2 * CHUNK, CHUNK), F32),
            pltpu.VMEM((CHUNK, width), F32),
            pltpu.VMEM((CHUNK, width), F32),
        ],
        flops=dense * 2 * width,
        moved=each * 12,
        limit=60,
    )(query, keys, values, cumul, x, scores, states, fades, state_in))

    early = forked([mlp_pair, mix_pair], EARLY, orders)

    def turned(shape=(TILE, width)):
        return pl.BlockSpec((None,) + shape, lambda n, i: (n, tiles - 1 - i, 0))

    dproj, late_sent, late_kept = beside(early, dquery, lambda x: call(
        state_back_kernel,
        (count, tiles),
        [valid_spec]
        + [turned()] * 9
        + [
            pl.BlockSpec(
                (None, per_tile, PAIRS, LANES, LANES),
                lambda n, i: (n, tiles - 1 - i, 0, 0, 0),
            ),
            turned(),
            whole(decay_up.shape),
            whole(decay_up.shape),
        ]
        + [message_spec] * (size - 1),
        [
            (turned((TILE, 4 * width)), (count, length, 4 * width)),
            (whole((ROWS // 2, width)), (ROWS // 2, width)),
            (whole((ROWS // 2, width)), (ROWS // 2, width)),
        ],
        [
            pltpu.VMEM((PAIRS, LANES, LANES), F32),
            pltpu.VMEM((8, width), F32),
            pltpu.VMEM((width, 4 * width), F32),
            pltpu.VMEM((ROWS, width), F32),
        ],
        flops=dense * 2 * width,
        moved=each * 14,
        limit=44,
    )(
        valid,
        query,
        keys,
        values,
        cumul,
        slope,
        datt,
        x,
        dkeys,
        dvalues,
        full,
        conv,
        decay_down.T,
        decay_up,
        *backward_parts,
    ))
    late_pair = Paired(late_sent, late_kept, core)
    (dconv,) = beside(early + [late_pair], late_kept, lambda x: call(
        hidden_kernel,
        (count, tiles),
        [tiled((TILE, 4 * width)), tiled(), whole((width, 4 * width))],
        [tile_row],
        [pltpu.VMEM((width, 3 * 4 * width), BF16)],
        flops=dense * 4 * width,
        moved=each * 7,
    )(lax.optimization_barrier((dproj, x))[0], conv, weights))
    d_above, d_below = borders(dconv)
    late = forked([late_pair], LATE[:2], orders[:2])
    rows, tokens_grad = beside(early + late, dconv, lambda x: move_first(call(
        front_back_kernel,
        (count, tiles),
        [
            tiled(),
            per_image((length + 2 * GRID, width)),
            per_image(row),
            per_image((GRID, width)),
            per_image((GRID, width)),
            tiled(),
            tiled(),
            mod_spec,
            whole((9, width)),
            dmod_spec,
            dmod_spec,
            dmod_spec,
        ],
        [
            tile_row,
            (per_image((24, width)), (count, 24, width)),
        ],
        [
            pltpu.VMEM((8, width), F32),
            pltpu.VMEM((length + 2 * GRID, width), F32),
            pltpu.VMEM((9, 8, width), F32),
        ],
        flops=count * length * width * 100,
        moved=each * 6,
    )(
        tokens, normed, x, d_above, d_below, dnorm, dmid, modul, conv_taps, dmod_mlp, dmod_mix, info
    )))

    flow_r = Rows(rows, seq_bits, img_bits)
    last = jnp.zeros((), F32)
    spreads = [None] * len(orders)
    while True:
        round_of = [flow for flow in late + early + [flow_r] + spreads if flow and flow.busy()]
        if not round_of:
            break
        for flow in round_of:
            got, last = lax.optimization_barrier((swapped(flow.send(), *flow.link()), last))
            stepped([flow], [got])
            last = flow.now()
        for n, one in enumerate(early):
            parts = [one] + late[n : n + 1]
            if spreads[n] is None and not any(part.busy() for part in parts):
                spreads[n] = Spread(jnp.concatenate([part.keep for part in parts]), one.used)
    rows = flow_r.x
    images = rows.shape[0]
    ids = rows[:, 9, 0].astype(jnp.int32)
    lasts = tuple(flow.link() for flow in spreads)
    rows, *near = lax.optimization_barrier((rows, *(flow.x for flow in spreads)))
    g_first, g_second, g_class, g_ada, g_ada_bias, g_taps = call(
        embed_kernel,
        (1,),
        [
            whole(rows.shape),
            whole(ada_weight.shape),
            whole(time_second.shape),
        ],
        [
            (whole(shape), shape)
            for shape in (
                time_first.shape,
                time_second.shape,
                class_table.shape,
                ada_weight.shape,
                (6 * width,),
                (9, width),
            )
        ],
        [],
        flops=images * 2 * 3 * width * width * 14,
        moved=4 * width * width * 20,
        prefetch=1,
    )(ids, rows, ada_weight, time_second)
    far_ones = [swapped(x, *last) for x, last in zip(near, lasts)]
    near_core = [swapped(x, *core) for x in near]
    g_ada, *far_ones = lax.optimization_barrier((g_ada, *far_ones))
    far_core = [swapped(x, *core) for x in far_ones]
    g_up, g_down, g_out, g_gate, g_query, g_key, g_value, g_small = assembled(
        near, far_ones, near_core, far_core, lasts, core, early, units
    )

    rank = decay_up.shape[0]
    return (
        block_out,
        tokens_grad,
        g_first,
        g_second,
        g_class,
        g_ada,
        g_ada_bias,
        g_taps,
        g_query,
        g_key,
        g_value,
        g_small[:rank].T,
        g_small[rank : 2 * rank],
        g_small[2 * rank],
        g_gate,
        g_out,
        g_up,
        g_down,
    )


def solution(mesh):
    image, shared = P("img", "seq", None), P()
    return jax.shard_map(
        body,
        mesh=mesh,
        in_specs=(image, P("img", "seq"), P("img"), P("img")) + (shared,) * 16 + (image,),
        out_specs=(image, image) + (shared,) * 16,
        check_vma=False,
    )
```
